128 devices in a mesh: gx: 4 (over z), gy: 4 (over x), gz: 8 (over y, core).
Axes of the slice: x: 4, y: 4, z: 4, core: 2. Of those that a mesh axis runs over, the one named last changes fastest.
Arguments:
- orbitals: float32 [32, 32, 32, 1024], P(None, 'gx', 'gy', 'gz'), may hold values from -6 to 6
- potential: float32 [32, 32, 1024], P('gx', 'gy', 'gz'), may hold values from -2 to 0
- projectors: float32 [1024, 4, 512], P(('gx', 'gy', 'gz')), may hold values from -0.5 to 0.5
- owner_rank: int32 [1024], replicated, may hold values from 0 to 127, as said below
- box_anchor: int32 [3, 1024], replicated, may hold values from 0 to 120, as said below
- box_extent: int32 [1024], replicated, may hold values from 4 to 8
- coupling: float32 [1024, 4], replicated, may hold values from 0.5 to 3
Outputs:
- filtered: float32 [32, 32, 32, 1024], P(None, 'gx', 'gy', 'gz')
- intersection: float32 [32, 32], replicated
The draws below stay inside these ranges and needn't reach their ends.
Inputs may be any that keep to these rules, and one draw needn't show every extreme that they name: owner_rank[a] is (ix * 4 + iy) * 8 + iz for the domain (ix, iy, iz) that holds all of atom a's box; every device holds at most 24 atoms, an eighth of the devices exactly 24. box_anchor[0, a] is at most 0, box_anchor[1, a] at most 0, box_anchor[2, a] at most 120, so each box lies inside its owner's domain.
All inputs are finite; a program needn't handle non-finite values.
Results may differ from the reference program's by a relative error of at most 0.00013.
Values sent between devices are 32-bit elements; how exact they have to be, the bound alone decides.
A program may use at most 128 MiB of HBM per device.

```python
import math
import jax
import jax.numpy as jnp
from jax import lax

S = 32
NPROJ = 4
B = 8
DEGREE = 4
CX = 8
CY = 8
CZ = 128
ATOM_DEV = 8
NX = 32
NY = 32
NZ = 1024
ATOMS = 1024
N_GY = 4
N_GZ = 8


def owner_table(key):
    devices_all = ATOMS // ATOM_DEV
    eighth = devices_all // 8
    base_loads = jnp.concatenate([jnp.full((eighth,), 3 * ATOM_DEV, jnp.int32), jnp.full((3 * eighth,), ATOM_DEV, jnp.int32), jnp.full((4 * eighth,), ATOM_DEV // 2, jnp.int32)])
    device_order = jax.random.permutation(jax.random.fold_in(key, 11), devices_all)
    device_loads = jnp.zeros((devices_all,), jnp.int32).at[device_order].set(base_loads)
    sorted_owner = jnp.repeat(jnp.arange(devices_all, dtype=jnp.int32), device_loads, total_repeat_length=ATOMS)
    shuffle = jax.random.permutation(jax.random.fold_in(key, 12), ATOMS)
    return sorted_owner[shuffle]


def draw_owner_rank(key, part):
    return owner_table(key)


def draw_box_anchor(key, part):
    upper_ends = jnp.array([[CX - B + 1], [CY - B + 1], [CZ - B + 1]], jnp.int32)
    jitter = jax.random.randint(jax.random.fold_in(key, 13), (3, ATOMS), 0, upper_ends, dtype=jnp.int32)
    jitter = jitter.at[2, 0].set(CZ - B)
    jitter = jitter.at[0, 1].set(0)
    return jitter.astype(jnp.int32)


def plant(entries, own_key, low, largest):
    index_at = [jax.random.randint(jax.random.fold_in(own_key, axis), (), 0, length) for axis, length in enumerate(entries.shape)]
    main_axis = entries.shape.index(max(entries.shape))
    neighbour = index_at[:main_axis] + [(index_at[main_axis] + 1) % entries.shape[main_axis]] + index_at[main_axis + 1:]
    return entries.at[tuple(index_at)].set(low).at[tuple(neighbour)].set(largest)


def levels(key, extent, cuts, least, high):
    factor_of, own = 1.0, jax.random.fold_in(key, 6)
    for axis_at, blocks in cuts:
        steps = jnp.exp(jax.random.uniform(jax.random.fold_in(own, axis_at), (blocks,), jnp.float32, least / len(cuts), high / len(cuts)))
        factor_of = factor_of * jnp.repeat(steps, extent[axis_at] // blocks).reshape([-1 if axis == axis_at else 1 for axis in range(len(extent))])
    return factor_of


def bell_draw(key, shape, width, most, cuts=(), kind=jnp.bfloat16):
    values = width * jax.random.normal(key, shape, jnp.float32)
    if cuts:
        values = values * levels(key, shape, cuts, -0.22, 0.18)
    return jnp.clip(values, -most, most).astype(kind)


def setup_inputs(seed: int = 0) -> dict:
    seeds = jax.random.split(jax.random.key(seed), 8)
    return {
        "orbitals": bell_draw(seeds[0], (S, NX, NY, NZ), 1.0, 6.0, ((1, 4), (2, 4), (3, 8)), jnp.float32),
        "potential": jnp.clip(-2.0 + 2.0 * jax.random.uniform(seeds[1], (NX, NY, NZ), jnp.float32) ** levels(seeds[1], (NX, NY, NZ), ((0, 4), (1, 4), (2, 8)), -0.2, 0.2), -2.0, 0.0),
        "projectors": bell_draw(seeds[2], (ATOMS, NPROJ, B * B * B), 0.08, 0.5, ((0, 128),), jnp.float32),
        "owner_rank": draw_owner_rank(jax.random.fold_in(seeds[7], 71), 0),
        "box_anchor": draw_box_anchor(jax.random.fold_in(seeds[7], 71), 0),
        "box_extent": plant(jax.random.randint(seeds[5], (ATOMS,), B // 2, B + 1), jax.random.fold_in(seeds[5], 1), B // 2, B).astype(jnp.int32),
        "coupling": jnp.clip(jnp.exp(jax.random.uniform(seeds[6], (ATOMS, NPROJ), jnp.float32, math.log(0.5), math.log(3.0))), 0.5, 3.0),
    }


STENCIL = (-5369.0 / 1800.0, 12.0 / 7.0, -15.0 / 56.0, 10.0 / 189.0, -1.0 / 112.0, 2.0 / 1925.0, -1.0 / 16632.0)
SPACING = 0.5
LOW_EDGE = -2.5
CUTOFF = 4.0
UPPER = 60.0


def laplace_wrap(field):
    padded = jnp.pad(field, 6, mode="wrap")
    span_x, span_y, span_z = field.shape
    summed = 3.0 * STENCIL[0] * field
    for offset in range(1, 7):
        weight = STENCIL[offset]
        summed = summed + weight * (padded[6 + offset:6 + offset + span_x, 6:6 + span_y, 6:6 + span_z] + padded[6 - offset:6 - offset + span_x, 6:6 + span_y, 6:6 + span_z])
        summed = summed + weight * (padded[6:6 + span_x, 6 + offset:6 + offset + span_y, 6:6 + span_z] + padded[6:6 + span_x, 6 - offset:6 - offset + span_y, 6:6 + span_z])
        summed = summed + weight * (padded[6:6 + span_x, 6:6 + span_y, 6 + offset:6 + offset + span_z] + padded[6:6 + span_x, 6:6 + span_y, 6 - offset:6 - offset + span_z])
    return summed / (SPACING * SPACING)


def box_masks(box_extent):
    cell_offsets = jnp.arange(B, dtype=jnp.int32)
    limit = box_extent[:, None, None, None]
    inside = (cell_offsets[None, :, None, None] < limit) & (cell_offsets[None, None, :, None] < limit) & (cell_offsets[None, None, None, :] < limit)
    return inside.reshape(box_extent.shape[0], B * B * B).astype(jnp.float32)


def nonlocal_one(field, masked, corners, coupling):
    def add_atom(atom_index, nonlocal_sum):
        corner = (corners[0, atom_index].astype(jnp.int32), corners[1, atom_index].astype(jnp.int32), corners[2, atom_index].astype(jnp.int32))
        box_cells = lax.dynamic_slice(field, corner, (B, B, B)).reshape(B * B * B)
        coeffs = jnp.dot(masked[atom_index], box_cells, precision=lax.Precision.HIGHEST) * coupling[atom_index]
        addition = jnp.dot(coeffs, masked[atom_index], precision=lax.Precision.HIGHEST).reshape(B, B, B)
        current = lax.dynamic_slice(nonlocal_sum, corner, (B, B, B))
        return lax.dynamic_update_slice(nonlocal_sum, current + addition, corner)
    return lax.fori_loop(0, ATOMS, add_atom, jnp.zeros_like(field))


def reference(orbitals, potential, projectors, owner_rank, box_anchor, box_extent, coupling):
    masked = projectors * box_masks(box_extent)[:, None, :]
    own_x = owner_rank // (N_GY * N_GZ)
    own_y = (owner_rank // N_GZ) % N_GY
    own_z = owner_rank % N_GZ
    corners = (jnp.stack([own_x * CX, own_y * CY, own_z * CZ]) + box_anchor).astype(jnp.int32)

    def apply_h(field):
        return -0.5 * laplace_wrap(field) + potential * field + nonlocal_one(field, masked, corners, coupling)

    def filter_one(field):
        half_width = (UPPER - CUTOFF) / 2.0
        middle = (UPPER + CUTOFF) / 2.0
        sigma_one = half_width / (LOW_EDGE - middle)
        sigma_now = sigma_one
        result = (apply_h(field) - middle * field) * (sigma_one / half_width)
        previous = field
        for degree_step in range(1, DEGREE):
            sigma_next = 1.0 / (2.0 / sigma_one - sigma_now)
            next_state = (apply_h(result) - middle * result) * (2.0 * sigma_next / half_width) - (sigma_now * sigma_next) * previous
            previous = result
            result = next_state
            sigma_now = sigma_next
        return result

    filtered = lax.map(filter_one, orbitals)
    flattened = filtered.reshape(filtered.shape[0], -1)
    intersection = jnp.dot(flattened, flattened.T, precision=lax.Precision.HIGHEST) / (NX * NY * NZ)
    return filtered, intersection
```

```python
import functools

import jax
import jax.numpy as jnp
import numpy as np
from jax import lax
from jax.experimental import pallas as pl
from jax.experimental.pallas import tpu as pltpu
from jax.sharding import PartitionSpec as P

B = 8
DEGREE = 4
STENCIL = (
    -5369.0 / 1800.0,
    12.0 / 7.0,
    -15.0 / 56.0,
    10.0 / 189.0,
    -1.0 / 112.0,
    2.0 / 1925.0,
    -1.0 / 16632.0,
)
SPACING = 0.5
LOW_EDGE = -2.5
CUTOFF = 4.0
UPPER = 60.0
HALF = (UPPER - CUTOFF) / 2.0
MIDDLE = (UPPER + CUTOFF) / 2.0

G = 16
PAD = 40
ROWS = 208
HALO = 32
MARGIN = 27
RANGES = ((16, 176), (24, 160), (32, 144), (40, 128))
WSCALE = 35.0 / 32.0
KIN = -0.5 / (SPACING * SPACING)
DIAG = KIN * 3.0 * STENCIL[0] - MIDDLE
SLOTS = 1040
F32 = jnp.float32
BF16 = jnp.bfloat16


def steps():
    sigma_one = HALF / (LOW_EDGE - MIDDLE)
    sigma = sigma_one
    out = [(sigma_one / HALF, 0.0)]
    for _ in range(1, DEGREE):
        nxt = 1.0 / (2.0 / sigma_one - sigma)
        out.append((2.0 * nxt / HALF, sigma * nxt))
        sigma = nxt
    return out


def weights():
    c = np.asarray(STENCIL, np.float64) * WSCALE

    def coef(m):
        m = abs(m)
        return c[m] if 1 <= m <= 6 else 0.0

    eye = np.eye(8)
    band = {s: np.array([[coef(8 * s + a - b) for b in range(8)] for a in range(8)]) for s in (-1, 0, 1)}
    two = np.eye(2)
    centre = np.kron(two, np.kron(band[0], eye) + np.kron(eye, band[0]))
    ym, yp = (np.kron(two, np.kron(eye, band[s])) for s in (-1, 1))
    xm, xp = (np.kron(two, np.kron(band[s], eye)) for s in (-1, 1))
    zero = np.zeros_like(centre)
    own = np.block([[centre, ym], [yp, centre]])
    other = np.block([[zero, yp], [ym, zero]])
    left = np.block([[xm, zero], [zero, xm]])
    right = np.block([[xp, zero], [zero, xp]])
    return np.concatenate([own, other, left, right], axis=0).astype(np.float32)


def filter_kernel(
    counts, slot_id, owner, anchor, extent, coupling,
    x_ref, v_ref, p_ref, w_ref, o_ref,
    bufa, bufb, hi, lo, pm, pg, rows_ref, coef_ref, slot_d, slot_r,
):
    lane = lax.broadcasted_iota(jnp.int32, (8, 128), 1)
    sub = lax.broadcasted_iota(jnp.int32, (8, 128), 0)
    first_half = lane < 64
    upper = sub < 4
    reach = jnp.maximum(jnp.maximum((lane % 64) // 8, lane % 8), sub)
    me = counts[2]
    n_own, n_all = counts[0], counts[1]

    def prepare(slot, _):
        ident = slot_id[slot] - 1
        used = ident >= 0
        ident = jnp.maximum(ident, 0)
        rank = owner[ident]
        slab = rank % 8
        shift = lax.rem(slab - me + 12, 8) - 4
        slot_d[slot] = jnp.where(used, rank // 8, 0)
        slot_r[slot] = jnp.where(used, anchor[ident] + PAD + 128 * shift, PAD)
        keep = reach < jnp.where(used, extent[ident], 0)
        for p in range(2):
            value = jnp.where(keep, p_ref[ident, pl.ds(8 * p, 8), :], 0.0)
            gain = jnp.where(first_half, coupling[4 * ident + 2 * p], coupling[4 * ident + 2 * p + 1])
            pm[slot, pl.ds(8 * p, 8), :] = value
            pg[slot, pl.ds(8 * p, 8), :] = value * gain
        return 0

    lax.fori_loop(0, n_all, prepare, 0)

    row = lax.broadcasted_iota(jnp.int32, (128, 128), 0)
    col = lax.broadcasted_iota(jnp.int32, (128, 128), 1)
    ones = ((row < 64) == (col < 64)).astype(F32).astype(BF16)

    def apply(now, old, new, offset, base, rows, alpha, beta, count):
        def split(dx, _):
            for u in range(2):
                for h in range(2):
                    for r in range(0, rows, 16):
                        v = now[4 * dx + 2 * u + h, pl.ds(base + r, 16), :]
                        top = v.astype(BF16)
                        hi[u, dx, pl.ds(r, 16), pl.ds(128 * h, 128)] = top
                        lo[u, dx, pl.ds(r, 16), pl.ds(128 * h, 128)] = (v - top.astype(F32)).astype(BF16)
            return 0

        lax.fori_loop(0, 4, split, 0)

        def stencil(it, _):
            u, dx = it // 4, it % 4
            below, above = lax.rem(dx + 3, 4), lax.rem(dx + 1, 4)
            blocks = []
            for part in (hi, lo):
                for uu, xx in ((u, dx), (1 - u, dx), (u, below), (u, above)):
                    blocks.append(part[uu, xx, pl.ds(0, rows), :])
            acc = jnp.dot(jnp.concatenate(blocks, axis=1), w_ref[...], preferred_element_type=F32)
            for h in range(2):
                d = 4 * dx + 2 * u + h
                for r in range(0, rows, 8):
                    s = base + r
                    mid = now[d, pl.ds(s, 8), :]
                    val = acc[r : r + 8, 128 * h : 128 * h + 128] * (alpha * KIN / WSCALE)
                    val = val + (alpha * v_ref[d, pl.ds(s, 8), :]) * mid
                    for m in range(1, 7):
                        val = val + (alpha * KIN * STENCIL[m]) * (
                            now[d, pl.ds(s + m, 8), :] + now[d, pl.ds(s - m, 8), :]
                        )
                    if beta:
                        val = val - beta * old[d, pl.ds(s, 8), :]
                    new[d, pl.ds(s - offset, 8), :] = val
            return 0

        lax.fori_loop(0, 8, stencil, 0)

        def project(pair, _):
            prods = []
            for k in range(2):
                slot = 2 * pair + k
                box = now[slot_d[slot], pl.ds(slot_r[slot], 8), :]
                swapped = pltpu.roll(box, 64, 1)
                for p in range(2):
                    proj = pm[slot, pl.ds(8 * p, 8), :]
                    prods += [proj * box, proj * swapped]
            merged = []
            for i in range(4):
                a, b = prods[i], prods[i + 4]
                t = jnp.where(upper, a, b) + pltpu.roll(jnp.where(upper, b, a), 4, 0)
                t = t + pltpu.roll(t, 7, 0)
                merged.append(t + pltpu.roll(t, 6, 0))
            low = sub % 4
            out = merged[0]
            for i in range(1, 4):
                out = jnp.where(low == i, pltpu.roll(merged[i], i, 0), out)
            rows_ref[pl.ds(pl.multiple_of(8 * pair, 8), 8), :] = out
            return 0

        lax.fori_loop(0, count // 2, project, 0, unroll=False)

        def reduce(chunk, _):
            at = pl.multiple_of(32 * chunk, 32)
            v = rows_ref[pl.ds(at, 32), :]
            top = v.astype(BF16)
            rest = (v - top.astype(F32)).astype(BF16)
            both = jnp.dot(jnp.concatenate([top, rest], axis=0), ones, preferred_element_type=F32)
            coef_ref[pl.ds(at, 32), :] = alpha * (both[:32] + both[32:])
            return 0

        lax.fori_loop(0, count // 8, reduce, 0)

        def spread(slot, _):
            at = 4 * slot
            pieces = [
                jnp.broadcast_to(coef_ref[pl.ds(at + i, 1), :], (8, 128)) for i in range(4)
            ]
            p0, p1 = pg[slot, pl.ds(0, 8), :], pg[slot, pl.ds(8, 8), :]
            w = p0 * pieces[0] + p1 * pieces[2] + pltpu.roll(p0 * pieces[1] + p1 * pieces[3], 64, 1)
            d, r = slot_d[slot], slot_r[slot] - offset
            new[d, pl.ds(r, 8), :] = new[d, pl.ds(r, 8), :] + w
            return 0

        lax.fori_loop(0, count, spread, 0)

    plan = steps()
    chain = ((x_ref, None, bufb, 0, n_all), (bufb, x_ref, bufa, 0, n_all),
             (bufa, bufb, bufb, 0, n_all), (bufb, bufa, o_ref, PAD, n_own))
    for (now, old, new, offset, count), (base, rows), (alpha, beta) in zip(chain, RANGES, plan):
        apply(now, old, new, offset, base, rows, alpha, beta, count)


def run_filter(counts, slot_id, owner, anchor, extent, coupling, x, v, p, w):
    smem = pl.BlockSpec(memory_space=pltpu.SMEM)
    vmem = pl.BlockSpec(memory_space=pltpu.VMEM)
    return pl.pallas_call(
        filter_kernel,
        out_shape=jax.ShapeDtypeStruct((G, 128, 128), F32),
        in_specs=[smem] * 6 + [vmem] * 4,
        out_specs=vmem,
        scratch_shapes=[
            pltpu.VMEM((G, ROWS, 128), F32),
            pltpu.VMEM((G, ROWS, 128), F32),
            pltpu.VMEM((2, 4, RANGES[0][1], 256), BF16),
            pltpu.VMEM((2, 4, RANGES[0][1], 256), BF16),
            pltpu.VMEM((SLOTS, 16, 128), F32),
            pltpu.VMEM((SLOTS, 16, 128), F32),
            pltpu.VMEM((4 * SLOTS, 128), F32),
            pltpu.VMEM((4 * SLOTS, 128), F32),
            pltpu.SMEM((SLOTS,), jnp.int32),
            pltpu.SMEM((SLOTS,), jnp.int32),
        ],
        compiler_params=pltpu.CompilerParams(vmem_limit_bytes=56 * 2**20),
        name="chebyshev",
    )(counts, slot_id, owner, anchor, extent, coupling, x, v, p, w)


def slots(owner, anchor_z, me):
    slab = owner % 8
    own = slab == me
    before = (slab == (me + 7) % 8) & (anchor_z + MARGIN >= 128)
    after = (slab == (me + 1) % 8) & (anchor_z + B <= MARGIN)
    near = before | after
    ids = jnp.arange(owner.shape[0], dtype=jnp.int32)
    earlier = ids[None, :] < ids[:, None]
    n_own = jnp.sum(own.astype(jnp.int32))
    first = (n_own + 7) // 8 * 8
    n_all = first + (jnp.sum(near.astype(jnp.int32)) + 7) // 8 * 8
    at_own = jnp.sum((earlier & own[None, :]).astype(jnp.int32), axis=1)
    at_near = jnp.sum((earlier & near[None, :]).astype(jnp.int32), axis=1) + first
    at = jnp.where(own, at_own, jnp.where(near, at_near, -1))
    table = jnp.sum(
        jnp.where(at[None, :] == jnp.arange(SLOTS, dtype=jnp.int32)[:, None], ids[None, :] + 1, 0), axis=1
    )
    return jnp.stack([first, n_all, me]), table


def body(orbitals, potential, projectors, owner_rank, box_anchor, box_extent, coupling):
    plane = ("gx", "gy")
    me = lax.axis_index("gz")
    states = orbitals.shape[0]
    sent = jnp.swapaxes(orbitals.reshape(G, 128, 128), 1, 2)
    x = lax.all_to_all(sent, plane, 0, 0, tiled=True)
    v = jnp.swapaxes(potential.reshape(1, 64, 128), 1, 2) + DIAG
    v = lax.all_gather(v, plane, axis=0, tiled=True)
    p = projectors.reshape(8, 2, 2, 64, 8).transpose(0, 1, 4, 2, 3).reshape(8, 16, 128)
    p = lax.all_gather(p, ("gx", "gy", "gz"), axis=0, tiled=True)

    def extend(a):
        n = lax.axis_size("gz")
        up = lax.ppermute(a[:, 128 - HALO :], "gz", [(i, (i + 1) % n) for i in range(n)])
        down = lax.ppermute(a[:, :HALO], "gz", [((i + 1) % n, i) for i in range(n)])
        edge = jnp.zeros((G, PAD - HALO, a.shape[2]), F32)
        return jnp.concatenate([edge, up, a, down, edge], axis=1)

    x = extend(x)
    v = extend(v)
    v = jnp.concatenate([v, v], axis=2)
    counts, table = slots(owner_rank, box_anchor[2], me)
    w = weights()
    w = jnp.asarray(np.concatenate([w, w], axis=0)).astype(BF16)
    y = run_filter(
        counts, table, owner_rank, box_anchor[2], box_extent, coupling.reshape(-1), x, v, p, w
    )
    back = lax.all_to_all(y, plane, 0, 0, tiled=True)
    filtered = jnp.swapaxes(back, 1, 2).reshape(states, 8, 8, 128)
    flat = filtered.reshape(states, -1)
    part = jnp.dot(flat, flat.T, precision=lax.Precision.HIGHEST)
    total = lax.psum(part, ("gx", "gy", "gz")) / (32 * 32 * 1024)
    return filtered, total


def solution(mesh):
    return jax.shard_map(
        body,
        mesh=mesh,
        in_specs=(
            P(None, "gx", "gy", "gz"),
            P("gx", "gy", "gz"),
            P(("gx", "gy", "gz"), None, None),
            P(),
            P(),
            P(),
            P(),
        ),
        out_specs=(P(None, "gx", "gy", "gz"), P()),
        check_vma=False,
    )
```

```python
import functools

import jax
import jax.numpy as jnp
import numpy as np
from jax import lax
from jax.experimental import pallas as pl
from jax.experimental.pallas import tpu as pltpu
from jax.sharding import PartitionSpec as P

B = 8
DEGREE = 4
STENCIL = (
    -5369.0 / 1800.0,
    12.0 / 7.0,
    -15.0 / 56.0,
    10.0 / 189.0,
    -1.0 / 112.0,
    2.0 / 1925.0,
    -1.0 / 16632.0,
)
SPACING = 0.5
LOW_EDGE = -2.5
CUTOFF = 4.0
UPPER = 60.0
HALF = (UPPER - CUTOFF) / 2.0
MIDDLE = (UPPER + CUTOFF) / 2.0

G = 16
PAD = 40
ROWS = 208
HALO = 32
MARGIN = 27
RANGES = ((16, 176), (24, 160), (32, 144), (40, 128))
WSCALE = 35.0 / 32.0
KIN = -0.5 / (SPACING * SPACING)
DIAG = KIN * 3.0 * STENCIL[0] - MIDDLE
SLOTS = 1088
CHUNK = 256
F32 = jnp.float32
BF16 = jnp.bfloat16


def steps():
    sigma_one = HALF / (LOW_EDGE - MIDDLE)
    sigma = sigma_one
    out = [(sigma_one / HALF, 0.0)]
    for _ in range(1, DEGREE):
        nxt = 1.0 / (2.0 / sigma_one - sigma)
        out.append((2.0 * nxt / HALF, sigma * nxt))
        sigma = nxt
    return out


def weights():
    c = np.asarray(STENCIL, np.float64) * WSCALE

    def coef(m):
        m = abs(m)
        return c[m] if 1 <= m <= 6 else 0.0

    eye = np.eye(8)
    band = {s: np.array([[coef(8 * s + a - b) for b in range(8)] for a in range(8)]) for s in (-1, 0, 1)}
    two = np.eye(2)
    centre = np.kron(two, np.kron(band[0], eye) + np.kron(eye, band[0]))
    ym, yp = (np.kron(two, np.kron(eye, band[s])) for s in (-1, 1))
    xm, xp = (np.kron(two, np.kron(band[s], eye)) for s in (-1, 1))
    zero = np.zeros_like(centre)
    own = np.block([[centre, ym], [yp, centre]])
    other = np.block([[zero, yp], [ym, zero]])
    left = np.block([[xm, zero], [zero, xm]])
    right = np.block([[xp, zero], [zero, xp]])
    return np.concatenate([own, other, left, right], axis=0).astype(np.float32)


def filter_kernel(
    counts, slot_id, owner, anchor, extent, coupling,
    x_ref, vp_ref, p_ref, w_ref, o_ref,
    v_ref, bufa, bufb, hi, lo, pm, pg, rows_ref, coef_ref, slot_d, slot_r,
):
    lane = lax.broadcasted_iota(jnp.int32, (8, 128), 1)
    sub = lax.broadcasted_iota(jnp.int32, (8, 128), 0)
    first_half = lane < 64
    upper = sub < 4
    reach = jnp.maximum(jnp.maximum((lane % 64) // 8, lane % 8), sub)
    me = counts[2]
    n_own, n_all = counts[0], counts[1]

    def prepare(slot, _):
        ident = slot_id[slot] - 1
        used = ident >= 0
        ident = jnp.maximum(ident, 0)
        rank = owner[ident]
        slab = rank % 8
        shift = lax.rem(slab - me + 12, 8) - 4
        slot_d[slot] = jnp.where(used, rank // 8, 0)
        slot_r[slot] = jnp.where(used, anchor[ident] + PAD + 128 * shift, PAD)
        keep = reach < jnp.where(used, extent[ident], 0)
        for p in range(2):
            value = jnp.where(keep, p_ref[ident, pl.ds(8 * p, 8), :], 0.0)
            gain = jnp.where(first_half, coupling[4 * ident + 2 * p], coupling[4 * ident + 2 * p + 1])
            pm[slot, pl.ds(8 * p, 8), :] = value
            pg[slot, pl.ds(8 * p, 8), :] = value * gain
        return 0

    lax.fori_loop(0, n_all, prepare, 0)

    def unpack(d, _):
        for r in range(0, 96, 8):
            pair = vp_ref[d, pl.ds(r, 8), :]
            swapped = pltpu.roll(pair, 64, 1)
            v_ref[d, pl.ds(8 + 2 * r, 8, stride=2), :] = jnp.where(first_half, pair, swapped) + DIAG
            v_ref[d, pl.ds(9 + 2 * r, 8, stride=2), :] = jnp.where(first_half, swapped, pair) + DIAG
        return 0

    lax.fori_loop(0, G, unpack, 0)

    row = lax.broadcasted_iota(jnp.int32, (128, 128), 0)
    col = lax.broadcasted_iota(jnp.int32, (128, 128), 1)
    ones = ((row < 64) == (col < 64)).astype(F32).astype(BF16)

    def apply(now, old, new, offset, base, rows, alpha, beta, count):
        def split(dx, _):
            for u in range(2):
                for h in range(2):
                    for r in range(0, rows, 16):
                        v = now[4 * dx + 2 * u + h, pl.ds(base + r, 16), :]
                        top = v.astype(BF16)
                        hi[u, dx, pl.ds(r, 16), pl.ds(128 * h, 128)] = top
                        lo[u, dx, pl.ds(r, 16), pl.ds(128 * h, 128)] = (v - top.astype(F32)).astype(BF16)
            return 0

        lax.fori_loop(0, 4, split, 0)

        def stencil(it, _):
            u, dx = it // 4, it % 4
            below, above = lax.rem(dx + 3, 4), lax.rem(dx + 1, 4)
            blocks = []
            for part in (hi, lo):
                for uu, xx in ((u, dx), (1 - u, dx), (u, below), (u, above)):
                    blocks.append(part[uu, xx, pl.ds(0, rows), :])
            acc = jnp.dot(jnp.concatenate(blocks, axis=1), w_ref[...], preferred_element_type=F32)
            for h in range(2):
                d = 4 * dx + 2 * u + h
                for r in range(0, rows, 8):
                    s = base + r
                    mid = now[d, pl.ds(s, 8), :]
                    val = acc[r : r + 8, 128 * h : 128 * h + 128] * (alpha * KIN / WSCALE)
                    val = val + (alpha * v_ref[d, pl.ds(s, 8), :]) * mid
                    for m in range(1, 7):
                        val = val + (alpha * KIN * STENCIL[m]) * (
                            now[d, pl.ds(s + m, 8), :] + now[d, pl.ds(s - m, 8), :]
                        )
                    if beta:
                        val = val - beta * old[d, pl.ds(s, 8), :]
                    new[d, pl.ds(s - offset, 8), :] = val
            return 0

        lax.fori_loop(0, 8, stencil, 0)

        low = sub % 4

        def project(group, _):
            for q in range(4):
                prods = []
                for k in range(2):
                    slot = 8 * group + 2 * q + k
                    box = now[slot_d[slot], pl.ds(slot_r[slot], 8), :]
                    swapped = pltpu.roll(box, 64, 1)
                    for p in range(2):
                        proj = pm[slot, pl.ds(8 * p, 8), :]
                        prods += [proj * box, proj * swapped]
                out = None
                for i in range(4):
                    a, b = prods[i], prods[i + 4]
                    t = jnp.where(upper, a, b) + pltpu.roll(jnp.where(upper, b, a), 4, 0)
                    t = t + pltpu.roll(t, 7, 0)
                    t = t + pltpu.roll(t, 6, 0)
                    out = t if i == 0 else jnp.where(low == i, pltpu.roll(t, i, 0), out)
                rows_ref[pl.ds(pl.multiple_of(32 * group, 32) + 8 * q, 8), :] = out
            return 0

        lax.fori_loop(0, count // 8, project, 0)

        def reduce(chunk, _):
            at = pl.multiple_of(CHUNK * chunk, CHUNK)
            v = rows_ref[pl.ds(at, CHUNK), :]
            top = v.astype(BF16)
            rest = (v - top.astype(F32)).astype(BF16)
            both = jnp.dot(jnp.concatenate([top, rest], axis=0), ones, preferred_element_type=F32)
            coef_ref[pl.ds(at, CHUNK), :] = alpha * (both[:CHUNK] + both[CHUNK:])
            return 0

        lax.fori_loop(0, (4 * count + CHUNK - 1) // CHUNK, reduce, 0)

        def spread(group, _):
            adds = []
            for q in range(8):
                slot = 8 * group + q
                at = 4 * slot
                pieces = [
                    jnp.broadcast_to(coef_ref[pl.ds(at + i, 1), :], (8, 128)) for i in range(4)
                ]
                p0, p1 = pg[slot, pl.ds(0, 8), :], pg[slot, pl.ds(8, 8), :]
                w = p0 * pieces[0] + p1 * pieces[2]
                adds.append(w + pltpu.roll(p0 * pieces[1] + p1 * pieces[3], 64, 1))
            for q in range(8):
                slot = 8 * group + q
                d, r = slot_d[slot], slot_r[slot] - offset
                new[d, pl.ds(r, 8), :] = new[d, pl.ds(r, 8), :] + adds[q]
            return 0

        lax.fori_loop(0, count // 8, spread, 0)

    plan = steps()
    chain = ((x_ref, None, bufb, 0, n_all), (bufb, x_ref, bufa, 0, n_all),
             (bufa, bufb, bufb, 0, n_all), (bufb, bufa, o_ref, PAD, n_own))
    for (now, old, new, offset, count), (base, rows), (alpha, beta) in zip(chain, RANGES, plan):
        apply(now, old, new, offset, base, rows, alpha, beta, count)


def run_filter(counts, slot_id, owner, anchor, extent, coupling, x, v, p, w):
    smem = pl.BlockSpec(memory_space=pltpu.SMEM)
    vmem = pl.BlockSpec(memory_space=pltpu.VMEM)
    return pl.pallas_call(
        filter_kernel,
        out_shape=jax.ShapeDtypeStruct((G, 128, 128), F32),
        in_specs=[smem] * 6 + [vmem] * 4,
        out_specs=vmem,
        scratch_shapes=[
            pltpu.VMEM((G, ROWS, 128), F32),
            pltpu.VMEM((G, ROWS, 128), F32),
            pltpu.VMEM((G, ROWS, 128), F32),
            pltpu.VMEM((2, 4, RANGES[0][1], 256), BF16),
            pltpu.VMEM((2, 4, RANGES[0][1], 256), BF16),
            pltpu.VMEM((SLOTS, 16, 128), F32),
            pltpu.VMEM((SLOTS, 16, 128), F32),
            pltpu.VMEM((4 * SLOTS, 128), F32),
            pltpu.VMEM((4 * SLOTS, 128), F32),
            pltpu.SMEM((SLOTS,), jnp.int32),
            pltpu.SMEM((SLOTS,), jnp.int32),
        ],
        compiler_params=pltpu.CompilerParams(vmem_limit_bytes=56 * 2**20),
        name="chebyshev",
    )(counts, slot_id, owner, anchor, extent, coupling, x, v, p, w)


MESH = pl.DeviceIdType.MESH
PARTS = ((0, 48, 24, (0, 1, 2)), (48, 40, 24, (1, 2, 0)), (88, 40, 24, (2, 0, 1)))
V_PARTS = ((0, 32, 16, (0, 1)), (32, 32, 16, (1, 0)))


def position():
    return lax.axis_index("gx"), lax.axis_index("gy"), lax.axis_index("gz")


def plane_peer(offset):
    gx, gy, gz = position()
    return (lax.rem(gx + offset // 4, 4), lax.rem(gy + offset % 4, 4), gz)


def plane_source(offset):
    gx, gy, _ = position()
    return 4 * lax.rem(gx + 4 - offset // 4, 4) + lax.rem(gy + 4 - offset % 4, 4)


def line_peer(offset):
    gx, gy, gz = position()
    return (gx, gy, lax.rem(gz + offset, 8))


def greet():
    sem = pltpu.get_barrier_semaphore()

    def plane(o, _):
        pl.semaphore_signal(sem, inc=1, device_id=plane_peer(o), device_id_type=MESH)
        return 0

    def line(o, _):
        pl.semaphore_signal(sem, inc=1, device_id=line_peer(o), device_id_type=MESH)
        return 0

    lax.fori_loop(1, 16, plane, 0)
    lax.fori_loop(1, 8, line, 0)
    pl.semaphore_wait(sem, 22)


def remote(src, dst, send, recv, target):
    return pltpu.make_async_remote_copy(
        src_ref=src, dst_ref=dst, send_sem=send, recv_sem=recv, device_id=target, device_id_type=MESH
    )


def gather_kernel(
    sent, vown, pown, x_out, v_out, p_out,
    a2a_send, a2a_recv, p_send, p_recv, v_send, v_recv, twin_send, twin_recv, halo_send, halo_recv, here,
):
    gx, gy, gz = position()
    y, core = gz // 2, gz % 2
    mine = 4 * gx + gy
    local = [
        pltpu.make_async_copy(pown, p_out.at[gx, gy, y, core], here.at[0]),
        pltpu.make_async_copy(vown, v_out.at[gx, gy, pl.ds(16, 64)], here.at[1]),
        pltpu.make_async_copy(sent.at[mine], x_out.at[mine, pl.ds(PAD, 128)], here.at[2]),
    ]
    for copy in local:
        copy.start()
    greet()
    where = (gx, gy, y)
    sizes = (4, 4, 4)

    def neighbour(dim, step):
        at = list(where)
        at[dim] = lax.rem(at[dim] + step + 4, 4)
        return (at[0], at[1], 2 * at[2] + core)

    def p_view(held, dim, at, start, rows):
        idx = [pl.ds(0, 4) if k in held else where[k] for k in range(3)]
        if dim is not None:
            idx[dim] = at
        return p_out.at[idx[0], idx[1], idx[2], core, pl.ds(start, rows)]

    def v_view(held, dim, at, start, rows):
        idx = [pl.ds(0, 4) if k in held else where[k] for k in range(2)]
        if dim is not None:
            idx[dim] = at
        return v_out.at[idx[0], idx[1], pl.ds(16 + start, rows)]

    def phase_copies(view, part, phase, send, recv):
        start, rows, half, order = part
        dim, held = order[phase], order[:phase]
        me = where[dim]
        below, above = lax.rem(me + 3, 4), lax.rem(me + 1, 4)
        base = 4 * phase

        def make(k, src, target):
            return remote(src, src, send.at[base + k], recv.at[base + k], target)

        own = view(held, dim, me, start, rows)
        first = [make(0, own, neighbour(dim, 1)), make(1, own, neighbour(dim, -1))]
        second = [
            make(2, view(held, dim, below, start, half), neighbour(dim, 1)),
            make(3, view(held, dim, above, start + half, rows - half), neighbour(dim, -1)),
        ]
        return first, second

    def a2a(o):
        peer = plane_peer(o)
        target = 4 * peer[0] + peer[1]
        return remote(
            sent.at[target], x_out.at[mine, pl.ds(PAD, 128)], a2a_send.at[o], a2a_recv.at[o], peer
        )

    def send_a2a(lo_o, hi_o):
        def step(o, _):
            a2a(o).start()
            return 0

        lax.fori_loop(lo_o, hi_o, step, 0)

    for copy in local:
        copy.wait()
    partner = (gx, gy, gz + 1 - 2 * core)

    def twin(k, part, view_args):
        src = p_view(*view_args)
        return remote(src, src, twin_send.at[k, part], twin_recv.at[k, part], partner)

    p_steps = [[phase_copies(p_view, part, ph, p_send.at[i], p_recv.at[i]) for ph in range(3)]
               for i, part in enumerate(PARTS)]
    v_steps = [[phase_copies(v_view, part, ph, v_send.at[i], v_recv.at[i]) for ph in range(2)]
               for i, part in enumerate(V_PARTS)]
    twins = []
    cuts = [1, 4, 7, 10, 13, 16, 16]
    for ph in range(3):
        for st in range(2):
            k = 2 * ph + st
            group = [p_steps[i][ph][st] for i in range(3)]
            if ph < 2:
                group += [v_steps[i][ph][st] for i in range(2)]
            for copies in group:
                for copy in copies:
                    copy.start()
            if cuts[k] < cuts[k + 1]:
                send_a2a(cuts[k], cuts[k + 1])
            for copies in group:
                for copy in copies:
                    copy.wait()
            new = []
            for i, (start, rows, half, order) in enumerate(PARTS):
                d3, held = order[2], order[:2]
                me = where[d3]
                if k == 3:
                    new.append(twin(0, i, (held, d3, me, start, rows)))
                if k == 4:
                    new.append(twin(1, i, (held, d3, lax.rem(me + 1, 4), start, rows)))
                    new.append(twin(2, i, (held, d3, lax.rem(me + 3, 4), start, rows)))
                if k == 5:
                    new.append(twin(3, i, (held, d3, lax.rem(me + 2, 4), start, rows)))
            for copy in new:
                copy.start()
            twins += new

    def finish_a2a(o, _):
        a2a(o).wait()
        return 0

    lax.fori_loop(1, 16, finish_a2a, 0)
    right, left = line_peer(1), line_peer(7)
    whole = pl.ds(0, 4)
    halos = [
        remote(x_out.at[pl.ds(0, G), pl.ds(PAD + 128 - HALO, HALO)], x_out.at[pl.ds(0, G), pl.ds(PAD - HALO, HALO)],
               halo_send.at[0], halo_recv.at[0], right),
        remote(x_out.at[pl.ds(0, G), pl.ds(PAD, HALO)], x_out.at[pl.ds(0, G), pl.ds(PAD + 128, HALO)],
               halo_send.at[1], halo_recv.at[1], left),
        remote(v_out.at[whole, whole, pl.ds(64, 16)], v_out.at[whole, whole, pl.ds(0, 16)],
               halo_send.at[2], halo_recv.at[2], right),
        remote(v_out.at[whole, whole, pl.ds(16, 16)], v_out.at[whole, whole, pl.ds(80, 16)],
               halo_send.at[3], halo_recv.at[3], left),
    ]
    for copy in halos:
        copy.start()
    for copy in halos + twins:
        copy.wait()


def run_gather(sent, vown, pown):
    vmem = pl.BlockSpec(memory_space=pltpu.VMEM)
    hbm = pl.BlockSpec(memory_space=pltpu.HBM)
    dma = pltpu.SemaphoreType.DMA
    return pl.pallas_call(
        gather_kernel,
        out_shape=(
            jax.ShapeDtypeStruct((G, ROWS, 128), F32),
            jax.ShapeDtypeStruct((4, 4, 96, 128), F32),
            jax.ShapeDtypeStruct((4, 4, 4, 2, 128, 128), F32),
        ),
        in_specs=[vmem] * 3,
        out_specs=(hbm, hbm, hbm),
        scratch_shapes=[
            dma((16,)), dma((16,)), dma((3, 12)), dma((3, 12)), dma((2, 8)), dma((2, 8)),
            dma((4, 3)), dma((4, 3)), dma((4,)), dma((4,)), dma((3,)),
        ],
        compiler_params=pltpu.CompilerParams(collective_id=1, has_side_effects=True),
        name="gather",
    )(sent, vown, pown)


def return_kernel(
    y, out, total, recv, gram_a, gram_b, a2a_send, a2a_recv, a_send, a_recv, b_send, b_recv, here,
):
    gx, gy, gz = position()
    mine = 4 * gx + gy
    own = pltpu.make_async_copy(y.at[mine], recv.at[mine], here.at[0])
    own.start()
    greet()

    def a2a(o):
        peer = plane_peer(o)
        return remote(
            y.at[4 * peer[0] + peer[1]], recv.at[mine], a2a_send.at[o], a2a_recv.at[o], peer
        )

    def send(o, _):
        a2a(o).start()
        return 0

    lax.fori_loop(1, 16, send, 0)

    def place(source):
        out[pl.ds(pl.multiple_of(128 * source, 128), 128), :] = recv[source].T

    own.wait()
    place(mine)

    def receive(o, _):
        a2a(o).wait()
        place(plane_source(o))
        return 0

    lax.fori_loop(1, 16, receive, 0)

    def gram(c, acc):
        cells = jnp.concatenate([out[pl.ds(8 * c + i, 32, stride=64), :] for i in range(8)], axis=1)
        top = cells.astype(BF16)
        rest = (cells - top.astype(F32)).astype(BF16)
        both = jnp.concatenate([top, rest], axis=0)
        return acc + lax.dot_general(both, both, (((1,), (1,)), ((), ())), preferred_element_type=F32)

    acc = lax.fori_loop(0, 8, gram, jnp.zeros((64, 64), F32))
    g = acc[:32, :32] + (acc[:32, 32:] + acc[32:, :32])
    gram_a[mine] = jnp.concatenate([g[8 * b : 8 * b + 8] for b in range(4)], axis=1)

    def plane(o):
        return remote(gram_a.at[mine], gram_a.at[mine], a_send.at[o], a_recv.at[o], plane_peer(o))

    def line(o):
        return remote(gram_b.at[gz], gram_b.at[gz], b_send.at[o], b_recv.at[o], line_peer(o))

    def start_plane(o, _):
        plane(o).start()
        return 0

    def wait_plane(o, _):
        plane(o).wait()
        return 0

    def start_line(o, _):
        line(o).start()
        return 0

    def wait_line(o, _):
        line(o).wait()
        return 0

    lax.fori_loop(1, 16, start_plane, 0)
    lax.fori_loop(1, 16, wait_plane, 0)
    acc = gram_a[0]
    for i in range(1, 16):
        acc = acc + gram_a[i]
    gram_b[gz] = acc
    lax.fori_loop(1, 8, start_line, 0)
    lax.fori_loop(1, 8, wait_line, 0)
    acc = gram_b[0]
    for i in range(1, 8):
        acc = acc + gram_b[i]
    acc = acc * (1.0 / (32 * 32 * 1024))
    for b in range(4):
        total[pl.ds(8 * b, 8), :] = acc[:, 32 * b : 32 * b + 32]


def run_return(y):
    vmem = pl.BlockSpec(memory_space=pltpu.VMEM)
    dma = pltpu.SemaphoreType.DMA
    return pl.pallas_call(
        return_kernel,
        out_shape=(jax.ShapeDtypeStruct((2048, 128), F32), jax.ShapeDtypeStruct((32, 32), F32)),
        in_specs=[vmem],
        out_specs=(vmem, vmem),
        scratch_shapes=[
            pltpu.VMEM((G, 128, 128), F32),
            pltpu.VMEM((G, 8, 128), F32),
            pltpu.VMEM((8, 8, 128), F32),
            dma((16,)), dma((16,)), dma((16,)), dma((16,)), dma((8,)), dma((8,)), dma((1,)),
        ],
        compiler_params=pltpu.CompilerParams(collective_id=2, has_side_effects=True),
        name="giveback",
    )(y)


def slots(owner, anchor_z, me):
    slab = owner % 8
    own = slab == me
    before = (slab == (me + 7) % 8) & (anchor_z + MARGIN >= 128)
    after = (slab == (me + 1) % 8) & (anchor_z + B <= MARGIN)
    near = before | after
    ids = jnp.arange(owner.shape[0], dtype=jnp.int32)
    earlier = ids[None, :] < ids[:, None]
    n_own = jnp.sum(own.astype(jnp.int32))
    first = (n_own + 7) // 8 * 8
    n_all = first + (jnp.sum(near.astype(jnp.int32)) + 7) // 8 * 8
    at_own = jnp.sum((earlier & own[None, :]).astype(jnp.int32), axis=1)
    at_near = jnp.sum((earlier & near[None, :]).astype(jnp.int32), axis=1) + first
    at = jnp.where(own, at_own, jnp.where(near, at_near, -1))
    table = jnp.sum(
        jnp.where(at[None, :] == jnp.arange(SLOTS, dtype=jnp.int32)[:, None], ids[None, :] + 1, 0), axis=1
    )
    return jnp.stack([first, n_all, me]), table


def body(orbitals, potential, projectors, owner_rank, box_anchor, box_extent, coupling):
    me = lax.axis_index("gz")
    states = orbitals.shape[0]
    sent = jnp.swapaxes(orbitals.reshape(G, 128, 128), 1, 2)
    v = jnp.swapaxes(potential.reshape(64, 128), 0, 1).reshape(64, 128)
    p = projectors.reshape(8, 2, 2, 64, 8).transpose(0, 1, 4, 2, 3).reshape(128, 128)
    x, v, p = run_gather(sent, v, p)
    counts, table = slots(owner_rank, box_anchor[2], me)
    w = weights()
    w = jnp.asarray(np.concatenate([w, w], axis=0)).astype(BF16)
    y = run_filter(
        counts, table, owner_rank, box_anchor[2], box_extent, coupling.reshape(-1),
        x, v.reshape(G, 96, 128), p.reshape(1024, 16, 128), w,
    )
    filtered, total = run_return(y)
    return filtered.reshape(states, 8, 8, 128), total


def solution(mesh):
    return jax.shard_map(
        body,
        mesh=mesh,
        in_specs=(
            P(None, "gx", "gy", "gz"),
            P("gx", "gy", "gz"),
            P(("gx", "gy", "gz"), None, None),
            P(),
            P(),
            P(),
            P(),
        ),
        out_specs=(P(None, "gx", "gy", "gz"), P()),
        check_vma=False,
    )
```

```python
import functools

import jax
import jax.numpy as jnp
import numpy as np
from jax import lax
from jax.experimental import pallas as pl
from jax.experimental.pallas import tpu as pltpu
from jax.sharding import PartitionSpec as P

B = 8
DEGREE = 4
STENCIL = (
    -5369.0 / 1800.0,
    12.0 / 7.0,
    -15.0 / 56.0,
    10.0 / 189.0,
    -1.0 / 112.0,
    2.0 / 1925.0,
    -1.0 / 16632.0,
)
SPACING = 0.5
LOW_EDGE = -2.5
CUTOFF = 4.0
UPPER = 60.0
HALF = (UPPER - CUTOFF) / 2.0
MIDDLE = (UPPER + CUTOFF) / 2.0

G = 16
PAD = 40
ROWS = 208
HALO = 32
MARGIN = 27
RANGES = ((16, 176), (24, 160), (32, 144), (40, 128))
WSCALE = 35.0 / 32.0
KIN = -0.5 / (SPACING * SPACING)
DIAG = KIN * 3.0 * STENCIL[0] - MIDDLE
SLOTS = 1040
F32 = jnp.float32
BF16 = jnp.bfloat16


def steps():
    sigma_one = HALF / (LOW_EDGE - MIDDLE)
    sigma = sigma_one
    out = [(sigma_one / HALF, 0.0)]
    for _ in range(1, DEGREE):
        nxt = 1.0 / (2.0 / sigma_one - sigma)
        out.append((2.0 * nxt / HALF, sigma * nxt))
        sigma = nxt
    return out


def weights():
    c = np.asarray(STENCIL, np.float64) * WSCALE

    def coef(m):
        m = abs(m)
        return c[m] if 1 <= m <= 6 else 0.0

    eye = np.eye(8)
    band = {s: np.array([[coef(8 * s + a - b) for b in range(8)] for a in range(8)]) for s in (-1, 0, 1)}
    two = np.eye(2)
    centre = np.kron(two, np.kron(band[0], eye) + np.kron(eye, band[0]))
    ym, yp = (np.kron(two, np.kron(eye, band[s])) for s in (-1, 1))
    xm, xp = (np.kron(two, np.kron(band[s], eye)) for s in (-1, 1))
    zero = np.zeros_like(centre)
    own = np.block([[centre, zero], [zero, centre]])
    across_x = np.block([[xp, xm], [xm, xp]])
    across_y = np.block([[yp, ym], [ym, yp]])
    both = [np.concatenate([own, across_x]), across_y]
    return np.concatenate([both[0], both[0], both[1], both[1]], axis=0).astype(np.float32)


def filter_kernel(
    table, owner, anchor, extent, coupling,
    x_ref, vp_ref, p_hbm, w_ref, o_ref,
    p_ref, v_ref, bufa, bufb, hi, lo, pm, gains, prods, slot_d, slot_r, load_sem,
):
    lane = lax.broadcasted_iota(jnp.int32, (8, 128), 1)
    sub = lax.broadcasted_iota(jnp.int32, (8, 128), 0)
    first_half = lane < 64
    upper = sub < 4
    low = sub % 4
    reach = jnp.maximum(jnp.maximum((lane % 64) // 8, lane % 8), sub)
    me = lax.axis_index("gz")
    n_own, n_all = table[15, 0], table[15, 1]

    load = pltpu.make_async_copy(p_hbm, p_ref, load_sem)
    load.start()

    def prepare(group, _):
        for q in range(8):
            slot = 8 * group + q
            ident = table[slot // 128, slot % 128] - 1
            used = ident >= 0
            ident = jnp.maximum(ident, 0)
            rank = owner[ident]
            shift = lax.rem(rank % 8 - me + 12, 8) - 4
            slot_d[slot] = jnp.where(used, rank // 8, 0)
            slot_r[slot] = jnp.where(used, anchor[2, ident] + PAD + 128 * shift, PAD)
            keep = reach < jnp.where(used, extent[ident], 0)
            lines = []
            for p in range(2):
                value = jnp.where(keep, p_ref[ident, pl.ds(8 * p, 8), :], 0.0)
                pm[slot, pl.ds(16 * p, 8), :] = value
                pm[slot, pl.ds(16 * p + 8, 8), :] = pltpu.roll(value, 64, 1)
                g0, g1 = coupling[2 * p, ident], coupling[2 * p + 1, ident]
                lines += [jnp.where(first_half, g0, g1), jnp.where(first_half, g1, g0)]
            four = jnp.where(low % 2 == 0, jnp.where(low < 2, lines[0], lines[2]), jnp.where(low < 2, lines[1], lines[3]))
            if q % 2 == 0:
                held = four
            else:
                gains[pl.ds(pl.multiple_of(32 * group, 32) + 4 * (q - 1), 8), :] = jnp.where(upper, held, four)
        return 0

    def unpack(d, _):
        for r in range(0, 96, 8):
            pair = vp_ref[d, pl.ds(r, 8), :]
            swapped = pltpu.roll(pair, 64, 1)
            v_ref[d, pl.ds(8 + 2 * r, 8, stride=2), :] = jnp.where(first_half, pair, swapped) + DIAG
            v_ref[d, pl.ds(9 + 2 * r, 8, stride=2), :] = jnp.where(first_half, swapped, pair) + DIAG
        return 0

    lax.fori_loop(0, G, unpack, 0)

    def apply(now, old, new, offset, base, rows, alpha, beta, count):
        def split(d, _):
            for r in range(0, rows, 16):
                v = now[d, pl.ds(base + r, 16), :]
                top = v.astype(BF16)
                hi[d, pl.ds(r, 16), :] = top
                lo[d, pl.ds(r, 16), :] = (v - top.astype(F32)).astype(BF16)
            return 0

        lax.fori_loop(0, G, split, 0)

        def stencil(it, _):
            px, py = it // 2, it % 2

            def dom(kx, ky):
                return 4 * lax.rem(px + kx, 4) + lax.rem(py + ky, 4)

            def pair(part, a, b):
                return jnp.concatenate([part[a, pl.ds(0, rows), :], part[b, pl.ds(0, rows), :]], axis=1)

            def stack(cases):
                return jnp.concatenate(
                    [jnp.concatenate([pair(part, *c) for part in (hi, lo) for c in case], axis=1) for case in cases],
                    axis=0,
                )

            lhs_x = stack([((dom(0, k), dom(2, k)), (dom(1, k), dom(3, k))) for k in (0, 2)])
            lhs_y = stack([((dom(k, 1), dom(k, 3)),) for k in (0, 2)])
            acc_x = jnp.dot(lhs_x, w_ref[pl.ds(0, 1024), :], preferred_element_type=F32)
            acc_y = jnp.dot(lhs_y, w_ref[pl.ds(1024, 512), :], preferred_element_type=F32)
            for kx in range(2):
                for ky in range(2):
                    d = dom(2 * kx, 2 * ky)
                    for r in range(0, rows, 8):
                        s = base + r
                        mid = now[d, pl.ds(s, 8), :]
                        val = acc_x[rows * ky + r : rows * ky + r + 8, 128 * kx : 128 * kx + 128]
                        val = val + acc_y[rows * kx + r : rows * kx + r + 8, 128 * ky : 128 * ky + 128]
                        val = val * (alpha * KIN / WSCALE)
                        val = val + (alpha * v_ref[d, pl.ds(s, 8), :]) * mid
                        for m in range(1, 7):
                            val = val + (alpha * KIN * STENCIL[m]) * (
                                now[d, pl.ds(s + m, 8), :] + now[d, pl.ds(s - m, 8), :]
                            )
                        if beta:
                            val = val - beta * old[d, pl.ds(s, 8), :]
                        new[d, pl.ds(s - offset, 8), :] = val
            return 0

        lax.fori_loop(0, 4, stencil, 0)

        if old is None:
            load.wait()
            lax.fori_loop(0, n_all // 8, prepare, 0)

        def project(group):
            for q in range(8):
                slot = 8 * group + q
                box = now[slot_d[slot], pl.ds(slot_r[slot], 8), :]
                for i in range(4):
                    prods[pl.ds(32 * q + 8 * i, 8), :] = pm[slot, pl.ds(8 * i, 8), :] * box
            out = []
            for t in range(4):
                v = prods[pl.ds(64 * t, 8, stride=8), :]
                for i in range(1, 8):
                    v = v + prods[pl.ds(64 * t + i, 8, stride=8), :]
                one = jnp.sum(jnp.where(first_half, v, 0.0), axis=1, keepdims=True)
                two = jnp.sum(jnp.where(first_half, 0.0, v), axis=1, keepdims=True)
                gain = gains[pl.ds(pl.multiple_of(32 * group, 32) + 8 * t, 8), :]
                out.append(alpha * gain * jnp.where(first_half, one, two))
            return tuple(out)

        def spread(group, coef):
            adds = []
            for q in range(8):
                slot = 8 * group + q
                w = None
                for i in range(4):
                    k = 4 * (q % 2) + i
                    piece = jnp.broadcast_to(coef[q // 2][k : k + 1, :], (8, 128))
                    term = pm[slot, pl.ds(8 * i, 8), :] * piece
                    w = term if w is None else w + term
                adds.append(w)
            for q in range(8):
                slot = 8 * group + q
                d, r = slot_d[slot], slot_r[slot] - offset
                new[d, pl.ds(r, 8), :] = new[d, pl.ds(r, 8), :] + adds[q]

        groups = count // 8

        def both_halves(group, coef):
            nxt = project(group)
            spread(group - 1, coef)
            return nxt

        @pl.when(groups > 0)
        def _():
            spread(groups - 1, lax.fori_loop(1, groups, both_halves, project(0)))

    plan = steps()
    chain = ((x_ref, None, bufb, 0, n_all), (bufb, x_ref, bufa, 0, n_all),
             (bufa, bufb, bufb, 0, n_all), (bufb, bufa, o_ref, PAD, n_own))
    for (now, old, new, offset, count), (base, rows), (alpha, beta) in zip(chain, RANGES, plan):
        apply(now, old, new, offset, base, rows, alpha, beta, count)


def run_filter(table, owner, anchor, extent, coupling, x, v, p, w):
    smem = pl.BlockSpec(memory_space=pltpu.SMEM)
    vmem = pl.BlockSpec(memory_space=pltpu.VMEM)
    return pl.pallas_call(
        filter_kernel,
        out_shape=jax.ShapeDtypeStruct((G, 128, 128), F32),
        in_specs=[smem] * 5 + [vmem] * 2 + [pl.BlockSpec(memory_space=pltpu.HBM), vmem],
        out_specs=vmem,
        scratch_shapes=[
            pltpu.VMEM((1024, 16, 128), F32),
            pltpu.VMEM((G, ROWS, 128), F32),
            pltpu.VMEM((G, ROWS, 128), F32),
            pltpu.VMEM((G, ROWS, 128), F32),
            pltpu.VMEM((G, RANGES[0][1], 128), BF16),
            pltpu.VMEM((G, RANGES[0][1], 128), BF16),
            pltpu.VMEM((SLOTS, 32, 128), F32),
            pltpu.VMEM((4 * SLOTS, 128), F32),
            pltpu.VMEM((256, 128), F32),
            pltpu.SMEM((SLOTS,), jnp.int32),
            pltpu.SMEM((SLOTS,), jnp.int32),
            pltpu.SemaphoreType.DMA,
        ],
        compiler_params=pltpu.CompilerParams(vmem_limit_bytes=56 * 2**20),
        name="chebyshev",
    )(table, owner, anchor, extent, coupling, x, v, p, w)


MESH = pl.DeviceIdType.MESH
PARTS = ((0, 48, 24, (0, 1, 2)), (48, 40, 24, (1, 2, 0)), (88, 40, 24, (2, 0, 1)))
V_PARTS = ((0, 32, 16, (0, 1)), (32, 32, 16, (1, 0)))


def position():
    return lax.axis_index("gx"), lax.axis_index("gy"), lax.axis_index("gz")


def plane_peer(offset):
    gx, gy, gz = position()
    return (lax.rem(gx + offset // 4, 4), lax.rem(gy + offset % 4, 4), gz)


def plane_source(offset):
    gx, gy, _ = position()
    return 4 * lax.rem(gx + 4 - offset // 4, 4) + lax.rem(gy + 4 - offset % 4, 4)


def line_peer(offset):
    gx, gy, gz = position()
    return (gx, gy, lax.rem(gz + offset, 8))


def greet():
    sem = pltpu.get_barrier_semaphore()

    def plane(o, _):
        pl.semaphore_signal(sem, inc=1, device_id=plane_peer(o), device_id_type=MESH)
        return 0

    def line(o, _):
        pl.semaphore_signal(sem, inc=1, device_id=line_peer(o), device_id_type=MESH)
        return 0

    lax.fori_loop(1, 16, plane, 0)
    lax.fori_loop(1, 8, line, 0)


def remote(src, dst, send, recv, target):
    return pltpu.make_async_remote_copy(
        src_ref=src, dst_ref=dst, send_sem=send, recv_sem=recv, device_id=target, device_id_type=MESH
    )


def pack(orb, pot, proj, perm, sent, vown, pown, cells, pair):
    first_half = lax.broadcasted_iota(jnp.int32, (16, 128), 1) < 64
    for q in range(G):
        sent[q] = orb[pl.ds(128 * q, 128), :].T
    pair[...] = pot[...].T
    vown[...] = jnp.concatenate([pair[pl.ds(0, 64, stride=2), :], pair[pl.ds(1, 64, stride=2), :]], axis=1)
    x = proj[...]
    top = x.astype(BF16)
    rest = x - top.astype(F32)
    mid = rest.astype(BF16)
    low = (rest - mid.astype(F32)).astype(BF16)
    parts = jnp.dot(jnp.concatenate([top, mid, low], axis=0), perm[...], preferred_element_type=F32)
    moved = (parts[:32] + parts[32:64]) + parts[64:]
    for t in range(4):
        cells[t] = moved[:, 128 * t : 128 * t + 128]
    for t in range(4):
        even, odd = cells[t, pl.ds(0, 16, stride=2), :], cells[t, pl.ds(1, 16, stride=2), :]
        pown[pl.ds(2 * t, 16, stride=8), :] = jnp.where(first_half, even, pltpu.roll(odd, 64, 1))
        pown[pl.ds(2 * t + 1, 16, stride=8), :] = jnp.where(first_half, pltpu.roll(even, 64, 1), odd)


def list_atoms(owner, anchor, gz):
    rank = owner[...]
    z = jnp.concatenate([anchor[2:3, 128 * r : 128 * r + 128] for r in range(8)], axis=0)
    slab = rank % 8
    own = slab == gz
    near = ((slab == (gz + 7) % 8) & (z + MARGIN >= 128)) | ((slab == (gz + 1) % 8) & (z + B <= MARGIN))
    row = lax.broadcasted_iota(jnp.int32, (128, 128), 0)
    col = lax.broadcasted_iota(jnp.int32, (128, 128), 1)
    sub = lax.broadcasted_iota(jnp.int32, (8, 128), 0)
    before = (row < col).astype(F32)

    def ranks(mask):
        m = mask.astype(F32)
        inside = jnp.dot(m.astype(BF16), before.astype(BF16), preferred_element_type=F32)
        counts = jnp.sum(m, axis=1, keepdims=True)
        base = jnp.zeros((1, 1), F32)
        bases = []
        for r in range(8):
            bases.append(base)
            base = base + counts[r : r + 1]
        return inside + jnp.concatenate(bases, axis=0), base

    at_own, n_own = ranks(own)
    at_near, n_near = ranks(near)
    first = jnp.floor((n_own + 7.0) * 0.125) * 8.0
    last = first + jnp.floor((n_near + 7.0) * 0.125) * 8.0
    at = jnp.where(own, at_own, jnp.where(near, at_near + first, -1.0)).astype(jnp.int32)
    high = jnp.where(at >= 0, at // 128, -1)
    low = (at % 128).astype(F32).T
    ident = 128 * sub + lax.broadcasted_iota(jnp.int32, (8, 128), 1) + 1
    slot_row = lax.broadcasted_iota(jnp.int32, (16, 128), 0)
    big = jnp.zeros((16, 128), F32)
    small = jnp.zeros((16, 128), F32)
    for r in range(8):
        hit = slot_row == high[r : r + 1]
        right = (low[:, r : r + 1] == col.astype(F32)).astype(BF16)
        one = ident[r : r + 1]
        big = big + jnp.dot(jnp.where(hit, (one // 32).astype(F32), 0.0).astype(BF16), right, preferred_element_type=F32)
        small = small + jnp.dot(jnp.where(hit, (one % 32).astype(F32), 0.0).astype(BF16), right, preferred_element_type=F32)
    table = big * 32.0 + small
    lane = lax.broadcasted_iota(jnp.int32, (16, 128), 1)
    table = jnp.where(slot_row == 15, jnp.where(lane == 0, first, jnp.where(lane == 1, last, 0.0)), table)
    return table.astype(jnp.int32)


def gather_kernel(
    orb, pot, proj, perm, owner, anchor, x_out, v_out, p_out, table,
    sent, vown, pown, cells, pair,
    a2a_send, a2a_recv, p_send, p_recv, v_send, v_recv, twin_send, twin_recv, halo_send, halo_recv, here,
):
    gx, gy, gz = position()
    y, core = gz // 2, gz % 2
    mine = 4 * gx + gy
    greet()
    pack(orb, pot, proj, perm, sent, vown, pown, cells, pair)
    pl.semaphore_wait(pltpu.get_barrier_semaphore(), 22)
    local = [
        pltpu.make_async_copy(pown, p_out.at[gx, gy, y, core], here.at[0]),
        pltpu.make_async_copy(vown, v_out.at[gx, gy, pl.ds(16, 64)], here.at[1]),
        pltpu.make_async_copy(sent.at[mine], x_out.at[mine, pl.ds(PAD, 128)], here.at[2]),
    ]
    for copy in local:
        copy.start()
    where = (gx, gy, y)

    def near(dim, step):
        return lax.rem(where[dim] + step + 4, 4)

    def neighbour(dim, step):
        at = list(where)
        at[dim] = near(dim, step)
        return (at[0], at[1], 2 * at[2] + core)

    def p_view(part, at2, at3, rows, at1=None):
        start, _, _, (d1, d2, d3) = PARTS[part]
        idx = [None, None, None]
        idx[d1] = pl.ds(0, 4) if at1 is None else at1
        idx[d2] = at2
        idx[d3] = at3
        return p_out.at[idx[0], idx[1], idx[2], core, pl.ds(start + rows[0], rows[1])]

    def v_view(held, dim, at, start, rows):
        idx = [pl.ds(0, 4) if k in held else where[k] for k in range(2)]
        idx[dim] = at
        return v_out.at[idx[0], idx[1], pl.ds(16 + start, rows)]

    used = [0, 0, 0]

    def p_copy(part, src, dim, step):
        k = used[part]
        used[part] += 1
        return remote(src, src, p_send.at[part, k], p_recv.at[part, k], neighbour(dim, step))

    partner = (gx, gy, gz + 1 - 2 * core)
    twins = []

    def twin(part, at2, at3):
        k = sum(1 for t in twins if t[0] == part)
        src = p_view(part, at2, at3, (0, PARTS[part][1]))
        copy = remote(src, src, twin_send.at[part, k], twin_recv.at[part, k], partner)
        copy.start()
        twins.append((part, copy))

    def start(copies):
        for copy in copies:
            copy.start()
        return copies

    def wait(copies):
        for copy in copies:
            copy.wait()

    def a2a(o):
        peer = plane_peer(o)
        return remote(
            sent.at[4 * peer[0] + peer[1]], x_out.at[mine, pl.ds(PAD, 128)], a2a_send.at[o], a2a_recv.at[o], peer
        )

    def send_a2a(lo_o, hi_o):
        def step(o, _):
            a2a(o).start()
            return 0

        lax.fori_loop(lo_o, hi_o, step, 0)

    def v_copies(phase, second):
        out = []
        for i, (at, rows, half, order) in enumerate(V_PARTS):
            dim, held = order[phase], order[:phase]
            base = 4 * phase
            if not second:
                own = v_view(held, dim, where[dim], at, rows)
                for k, step in ((0, 1), (1, -1)):
                    out.append(remote(own, own, v_send.at[i, base + k], v_recv.at[i, base + k], neighbour(dim, step)))
            else:
                for k, step, lo_r, n_r in ((2, 1, 0, half), (3, -1, half, rows - half)):
                    src = v_view(held, dim, near(dim, -step), at + lo_r, n_r)
                    out.append(remote(src, src, v_send.at[i, base + k], v_recv.at[i, base + k], neighbour(dim, step)))
        return out

    def along3(part, at2):
        d3 = PARTS[part][3][2]
        src = p_view(part, at2, where[d3], (0, PARTS[part][1]))
        return [p_copy(part, src, d3, 1), p_copy(part, src, d3, -1)]

    def forward3(part, at2):
        rows, half, d3 = PARTS[part][1], PARTS[part][2], PARTS[part][3][2]
        return [
            p_copy(part, p_view(part, at2, near(d3, -1), (0, half)), d3, 1),
            p_copy(part, p_view(part, at2, near(d3, 1), (half, rows - half)), d3, -1),
        ]

    three = range(3)
    dims = [part[3] for part in PARTS]
    wait(local)

    m1 = []
    for i in three:
        d1, d2, d3 = dims[i]
        own = p_view(i, where[d2], where[d3], (0, PARTS[i][1]), where[d1])
        m1 += [p_copy(i, own, d1, 1), p_copy(i, own, d1, -1)]
    start(m1)
    v = start(v_copies(0, False))
    send_a2a(1, 4)
    wait(m1)
    m2 = []
    for i in three:
        d1, d2, d3 = dims[i]
        rows, half = PARTS[i][1], PARTS[i][2]
        m2 += [
            p_copy(i, p_view(i, where[d2], where[d3], (0, half), near(d1, -1)), d1, 1),
            p_copy(i, p_view(i, where[d2], where[d3], (half, rows - half), near(d1, 1)), d1, -1),
        ]
    start(m2)
    wait(v)
    v = start(v_copies(0, True))
    send_a2a(4, 7)
    wait(m2)
    s3 = []
    for i in three:
        d1, d2, d3 = dims[i]
        row = p_view(i, where[d2], where[d3], (0, PARTS[i][1]))
        s3 += [p_copy(i, row, d2, 1), p_copy(i, row, d2, -1)]
    start(s3)
    a5 = start([c for i in three for c in along3(i, where[dims[i][1]])])
    for i in three:
        twin(i, where[dims[i][1]], where[dims[i][2]])
    wait(v)
    v = start(v_copies(1, False))
    send_a2a(7, 10)
    wait(s3)
    s4 = []
    for i in three:
        d1, d2, d3 = dims[i]
        rows, half = PARTS[i][1], PARTS[i][2]
        s4 += [
            p_copy(i, p_view(i, near(d2, -1), where[d3], (0, half)), d2, 1),
            p_copy(i, p_view(i, near(d2, 1), where[d3], (half, rows - half)), d2, -1),
        ]
    start(s4)
    b5 = start([c for i in three for k in (1, -1) for c in along3(i, near(dims[i][1], k))])
    for i in three:
        for k in (1, -1):
            twin(i, near(dims[i][1], k), where[dims[i][2]])
    wait(v)
    v = start(v_copies(1, True))
    wait(a5)
    a6 = start([c for i in three for c in forward3(i, where[dims[i][1]])])
    for i in three:
        for k in (1, -1):
            twin(i, where[dims[i][1]], near(dims[i][2], k))
    send_a2a(10, 13)
    wait(s4)
    c5 = start([c for i in three for c in along3(i, near(dims[i][1], 2))])
    for i in three:
        twin(i, near(dims[i][1], 2), where[dims[i][2]])
    send_a2a(13, 16)
    wait(v)
    right, left = line_peer(1), line_peer(7)
    whole = pl.ds(0, 4)
    halos = start([
        remote(v_out.at[whole, whole, pl.ds(64, 16)], v_out.at[whole, whole, pl.ds(0, 16)],
               halo_send.at[2], halo_recv.at[2], right),
        remote(v_out.at[whole, whole, pl.ds(16, 16)], v_out.at[whole, whole, pl.ds(80, 16)],
               halo_send.at[3], halo_recv.at[3], left),
    ])
    wait(b5)
    b6 = start([c for i in three for k in (1, -1) for c in forward3(i, near(dims[i][1], k))])
    for i in three:
        for m in (1, -1):
            for k in (1, -1):
                twin(i, near(dims[i][1], m), near(dims[i][2], k))
    table[...] = list_atoms(owner, anchor, gz)
    wait(a6)
    for i in three:
        twin(i, where[dims[i][1]], near(dims[i][2], 2))
    wait(c5)
    c6 = start([c for i in three for c in forward3(i, near(dims[i][1], 2))])
    for i in three:
        for k in (1, -1):
            twin(i, near(dims[i][1], 2), near(dims[i][2], k))

    def finish_a2a(o, _):
        a2a(o).wait()
        return 0

    lax.fori_loop(1, 16, finish_a2a, 0)
    halos += start([
        remote(x_out.at[pl.ds(0, G), pl.ds(PAD + 128 - HALO, HALO)], x_out.at[pl.ds(0, G), pl.ds(PAD - HALO, HALO)],
               halo_send.at[0], halo_recv.at[0], right),
        remote(x_out.at[pl.ds(0, G), pl.ds(PAD, HALO)], x_out.at[pl.ds(0, G), pl.ds(PAD + 128, HALO)],
               halo_send.at[1], halo_recv.at[1], left),
    ])
    wait(b6)
    for i in three:
        for k in (1, -1):
            twin(i, near(dims[i][1], k), near(dims[i][2], 2))
    wait(c6)
    for i in three:
        twin(i, near(dims[i][1], 2), near(dims[i][2], 2))
    wait(halos)
    wait([copy for _, copy in twins])


def permutation():
    at = np.arange(512)
    perm = np.zeros((512, 512), np.float32)
    perm[at, (at % 8) * 64 + at // 8] = 1.0
    return perm


def run_gather(orb, pot, proj, perm, owner, anchor):
    vmem = pl.BlockSpec(memory_space=pltpu.VMEM)
    hbm = pl.BlockSpec(memory_space=pltpu.HBM)
    dma = pltpu.SemaphoreType.DMA
    return pl.pallas_call(
        gather_kernel,
        out_shape=(
            jax.ShapeDtypeStruct((G, ROWS, 128), F32),
            jax.ShapeDtypeStruct((4, 4, 96, 128), F32),
            jax.ShapeDtypeStruct((4, 4, 4, 2, 128, 128), F32),
            jax.ShapeDtypeStruct((16, 128), jnp.int32),
        ),
        in_specs=[vmem] * 6,
        out_specs=(hbm, hbm, hbm, vmem),
        scratch_shapes=[
            pltpu.VMEM((G, 128, 128), F32),
            pltpu.VMEM((64, 128), F32),
            pltpu.VMEM((128, 128), F32),
            pltpu.VMEM((4, 32, 128), F32),
            pltpu.VMEM((128, 64), F32),
            dma((16,)), dma((16,)), dma((3, 24)), dma((3, 24)), dma((2, 8)), dma((2, 8)),
            dma((3, 16)), dma((3, 16)), dma((4,)), dma((4,)), dma((3,)),
        ],
        compiler_params=pltpu.CompilerParams(collective_id=1, has_side_effects=True),
        name="gather",
    )(orb, pot, proj, perm, owner, anchor)


def return_kernel(
    y, out, total, recv, gram_a, gram_b, a2a_send, a2a_recv, a_send, a_recv, b_send, b_recv, here,
):
    gx, gy, gz = position()
    mine = 4 * gx + gy
    own = pltpu.make_async_copy(y.at[mine], recv.at[mine], here.at[0])
    own.start()
    greet()
    pl.semaphore_wait(pltpu.get_barrier_semaphore(), 22)

    def a2a(o):
        peer = plane_peer(o)
        return remote(
            y.at[4 * peer[0] + peer[1]], recv.at[mine], a2a_send.at[o], a2a_recv.at[o], peer
        )

    def send(o, _):
        a2a(o).start()
        return 0

    lax.fori_loop(1, 16, send, 0)

    def place(source):
        out[pl.ds(pl.multiple_of(128 * source, 128), 128), :] = recv[source].T

    own.wait()
    place(mine)

    def receive(o, _):
        a2a(o).wait()
        place(plane_source(o))
        return 0

    lax.fori_loop(1, 16, receive, 0)

    def gram(c, acc):
        cells = jnp.concatenate([out[pl.ds(8 * c + i, 32, stride=64), :] for i in range(8)], axis=1)
        top = cells.astype(BF16)
        rest = (cells - top.astype(F32)).astype(BF16)
        both = jnp.concatenate([top, rest], axis=0)
        return acc + lax.dot_general(both, both, (((1,), (1,)), ((), ())), preferred_element_type=F32)

    acc = lax.fori_loop(0, 8, gram, jnp.zeros((64, 64), F32))
    g = acc[:32, :32] + (acc[:32, 32:] + acc[32:, :32])
    gram_a[mine] = jnp.concatenate([g[8 * b : 8 * b + 8] for b in range(4)], axis=1)

    def plane(o):
        return remote(gram_a.at[mine], gram_a.at[mine], a_send.at[o], a_recv.at[o], plane_peer(o))

    def line(o):
        return remote(gram_b.at[gz], gram_b.at[gz], b_send.at[o], b_recv.at[o], line_peer(o))

    def start_plane(o, _):
        plane(o).start()
        return 0

    def wait_plane(o, _):
        plane(o).wait()
        return 0

    def start_line(o, _):
        line(o).start()
        return 0

    def wait_line(o, _):
        line(o).wait()
        return 0

    lax.fori_loop(1, 16, start_plane, 0)
    lax.fori_loop(1, 16, wait_plane, 0)
    acc = gram_a[0]
    for i in range(1, 16):
        acc = acc + gram_a[i]
    gram_b[gz] = acc
    lax.fori_loop(1, 8, start_line, 0)
    lax.fori_loop(1, 8, wait_line, 0)
    acc = gram_b[0]
    for i in range(1, 8):
        acc = acc + gram_b[i]
    acc = acc * (1.0 / (32 * 32 * 1024))
    for b in range(4):
        total[pl.ds(8 * b, 8), :] = acc[:, 32 * b : 32 * b + 32]


def run_return(y):
    vmem = pl.BlockSpec(memory_space=pltpu.VMEM)
    dma = pltpu.SemaphoreType.DMA
    return pl.pallas_call(
        return_kernel,
        out_shape=(jax.ShapeDtypeStruct((2048, 128), F32), jax.ShapeDtypeStruct((32, 32), F32)),
        in_specs=[vmem],
        out_specs=(vmem, vmem),
        scratch_shapes=[
            pltpu.VMEM((G, 128, 128), F32),
            pltpu.VMEM((G, 8, 128), F32),
            pltpu.VMEM((8, 8, 128), F32),
            dma((16,)), dma((16,)), dma((16,)), dma((16,)), dma((8,)), dma((8,)), dma((1,)),
        ],
        compiler_params=pltpu.CompilerParams(collective_id=2, has_side_effects=True),
        name="giveback",
    )(y)


def body(orbitals, potential, projectors, owner_rank, box_anchor, box_extent, coupling):
    perm = jnp.asarray(permutation()).astype(BF16)
    x, v, p, table = run_gather(
        orbitals.reshape(2048, 128), potential.reshape(64, 128), projectors.reshape(32, 512), perm,
        owner_rank.reshape(8, 128), box_anchor,
    )
    w = jnp.asarray(weights()).astype(BF16)
    y = run_filter(
        table, owner_rank, box_anchor, box_extent, coupling.T,
        x, v.reshape(G, 96, 128), p.reshape(1024, 16, 128), w,
    )
    filtered, total = run_return(y)
    return filtered.reshape(orbitals.shape), total


def solution(mesh):
    return jax.shard_map(
        body,
        mesh=mesh,
        in_specs=(
            P(None, "gx", "gy", "gz"),
            P("gx", "gy", "gz"),
            P(("gx", "gy", "gz"), None, None),
            P(),
            P(),
            P(),
            P(),
        ),
        out_specs=(P(None, "gx", "gy", "gz"), P()),
        check_vma=False,
    )
```

```python
import functools

import jax
import jax.numpy as jnp
import numpy as np
from jax import lax
from jax.experimental import pallas as pl
from jax.experimental.pallas import tpu as pltpu
from jax.sharding import PartitionSpec as P

B = 8
DEGREE = 4
STENCIL = (
    -5369.0 / 1800.0,
    12.0 / 7.0,
    -15.0 / 56.0,
    10.0 / 189.0,
    -1.0 / 112.0,
    2.0 / 1925.0,
    -1.0 / 16632.0,
)
SPACING = 0.5
LOW_EDGE = -2.5
CUTOFF = 4.0
UPPER = 60.0
HALF = (UPPER - CUTOFF) / 2.0
MIDDLE = (UPPER + CUTOFF) / 2.0

G = 16
PAD = 40
ROWS = 208
HALO = 32
MARGIN = 27
RANGES = ((16, 176), (24, 160), (32, 144), (40, 128))
WSCALE = 35.0 / 32.0
KIN = -0.5 / (SPACING * SPACING)
DIAG = KIN * 3.0 * STENCIL[0] - MIDDLE
GROUP = 16
SLOTS = 1024 + 2 * GROUP
F32 = jnp.float32
BF16 = jnp.bfloat16


def steps():
    sigma_one = HALF / (LOW_EDGE - MIDDLE)
    sigma = sigma_one
    out = [(sigma_one / HALF, 0.0)]
    for _ in range(1, DEGREE):
        nxt = 1.0 / (2.0 / sigma_one - sigma)
        out.append((2.0 * nxt / HALF, sigma * nxt))
        sigma = nxt
    return out


def weights():
    c = np.asarray(STENCIL, np.float64) * WSCALE

    def coef(m):
        m = abs(m)
        return c[m] if 1 <= m <= 6 else 0.0

    eye = np.eye(8)
    band = {s: np.array([[coef(8 * s + a - b) for b in range(8)] for a in range(8)]) for s in (-1, 0, 1)}
    two = np.eye(2)
    centre = np.kron(two, np.kron(band[0], eye) + np.kron(eye, band[0]))
    ym, yp = (np.kron(two, np.kron(eye, band[s])) for s in (-1, 1))
    xm, xp = (np.kron(two, np.kron(band[s], eye)) for s in (-1, 1))
    zero = np.zeros_like(centre)
    own = np.block([[centre, zero], [zero, centre]])
    across_x = np.block([[xp, xm], [xm, xp]])
    across_y = np.block([[yp, ym], [ym, yp]])
    both = [np.concatenate([own, across_x]), across_y]
    return np.concatenate([both[0], both[0], both[1], both[1]], axis=0).astype(np.float32)


def filter_kernel(
    table, coupling,
    x_ref, vp_ref, p_hbm, w_ref, o_ref,
    p_ref, v_ref, bufa, bufb, hi, lo, acc_x, acc_y, pm, gains, prods, load_sem,
):
    lane = lax.broadcasted_iota(jnp.int32, (8, 128), 1)
    sub = lax.broadcasted_iota(jnp.int32, (8, 128), 0)
    first_half = lane < 64
    upper = sub < 4
    low = sub % 4
    reach = jnp.maximum(jnp.maximum((lane % 64) // 8, lane % 8), sub)
    n_own, n_all = table[15, 0], table[15, 1]

    load = pltpu.make_async_copy(p_hbm, p_ref, load_sem)
    load.start()

    def place(group):
        per_row = 128 // GROUP
        return group // per_row, GROUP * lax.rem(group, per_row)

    def prepare(group, _):
        row, at = place(group)
        fours = []
        for q in range(GROUP):
            slot = GROUP * group + q
            ident = jnp.maximum(table[row, at + q] - 1, 0)
            keep = reach < table[48 + row, at + q]
            g = [coupling[k, ident] for k in range(4)]
            lines = []
            for p in range(2):
                value = jnp.where(keep, p_ref[ident, pl.ds(8 * p, 8), :], 0.0)
                pm[slot, pl.ds(16 * p, 8), :] = value
                pm[slot, pl.ds(16 * p + 8, 8), :] = pltpu.roll(value, 64, 1)
                lines += [jnp.where(first_half, g[2 * p], g[2 * p + 1]), jnp.where(first_half, g[2 * p + 1], g[2 * p])]
            even, odd = jnp.where(low < 2, lines[0], lines[2]), jnp.where(low < 2, lines[1], lines[3])
            fours.append(jnp.where(low % 2 == 0, even, odd))
        for t in range(GROUP // 2):
            gains[pl.ds(pl.multiple_of(4 * GROUP * group, 64) + 8 * t, 8), :] = jnp.where(
                upper, fours[2 * t], fours[2 * t + 1]
            )
        return 0

    def unpack(d, _):
        for r in range(0, 96, 8):
            pair = vp_ref[d, pl.ds(r, 8), :]
            swapped = pltpu.roll(pair, 64, 1)
            v_ref[d, pl.ds(8 + 2 * r, 8, stride=2), :] = jnp.where(first_half, pair, swapped) + DIAG
            v_ref[d, pl.ds(9 + 2 * r, 8, stride=2), :] = jnp.where(first_half, swapped, pair) + DIAG
        return 0

    lax.fori_loop(0, G, unpack, 0)

    def apply(now, old, new, offset, base, rows, alpha, beta, count):
        def split(d, _):
            for r in range(0, rows, 16):
                v = now[d, pl.ds(base + r, 16), :]
                top = v.astype(BF16)
                hi[d, pl.ds(r, 16), :] = top
                lo[d, pl.ds(r, 16), :] = (v - top.astype(F32)).astype(BF16)
            return 0

        lax.fori_loop(0, G, split, 0)

        def multiply(it):
            px, py = it // 2, it % 2

            def dom(kx, ky):
                return 4 * lax.rem(px + kx, 4) + lax.rem(py + ky, 4)

            def pair(part, a, b):
                return jnp.concatenate([part[a, pl.ds(0, rows), :], part[b, pl.ds(0, rows), :]], axis=1)

            def stack(cases):
                return jnp.concatenate(
                    [jnp.concatenate([pair(part, *c) for part in (hi, lo) for c in case], axis=1) for case in cases],
                    axis=0,
                )

            lhs_x = stack([((dom(0, k), dom(2, k)), (dom(1, k), dom(3, k))) for k in (0, 2)])
            lhs_y = stack([((dom(k, 1), dom(k, 3)),) for k in (0, 2)])
            acc_x[pl.ds(0, 2 * rows), :] = jnp.dot(lhs_x, w_ref[pl.ds(0, 1024), :], preferred_element_type=F32)
            acc_y[pl.ds(0, 2 * rows), :] = jnp.dot(lhs_y, w_ref[pl.ds(1024, 512), :], preferred_element_type=F32)

        def finish(it):
            px, py = it // 2, it % 2
            for kx in range(2):
                for ky in range(2):
                    d = 4 * (px + 2 * kx) + py + 2 * ky
                    for r in range(0, rows, 8):
                        s = base + r
                        mid = now[d, pl.ds(s, 8), :]
                        val = acc_x[pl.ds(rows * ky + r, 8), pl.ds(128 * kx, 128)]
                        val = val + acc_y[pl.ds(rows * kx + r, 8), pl.ds(128 * ky, 128)]
                        val = val * (alpha * KIN / WSCALE)
                        val = val + (alpha * v_ref[d, pl.ds(s, 8), :]) * mid
                        for m in range(1, 7):
                            val = val + (alpha * KIN * STENCIL[m]) * (
                                now[d, pl.ds(s + m, 8), :] + now[d, pl.ds(s - m, 8), :]
                            )
                        if beta:
                            val = val - beta * old[d, pl.ds(s, 8), :]
                        new[d, pl.ds(s - offset, 8), :] = val

        def both_parts(it, _):
            finish(it)
            multiply(it + 1)
            return 0

        multiply(0)
        lax.fori_loop(0, 3, both_parts, 0)
        finish(3)

        if old is None:
            load.wait()
            lax.fori_loop(0, n_all // GROUP, prepare, 0)

        def project(group):
            row, at = place(group)
            for q in range(GROUP):
                box = now[table[16 + row, at + q], pl.ds(table[32 + row, at + q], 8), :]
                for i in range(4):
                    prods[pl.ds(32 * q + 8 * i, 8), :] = pm[GROUP * group + q, pl.ds(8 * i, 8), :] * box
            out = []
            for t in range(GROUP // 2):
                v = [prods[pl.ds(64 * t + i, 8, stride=8), :] for i in range(8)]
                while len(v) > 1:
                    v = [v[i] + v[i + 1] for i in range(0, len(v), 2)]
                out.append(v[0])
            return tuple(out)

        def weigh(group, sums):
            out = []
            for t in range(GROUP // 2):
                v = sums[t]
                one = jnp.sum(jnp.where(first_half, v, 0.0), axis=1, keepdims=True)
                two = jnp.sum(jnp.where(first_half, 0.0, v), axis=1, keepdims=True)
                gain = gains[pl.ds(pl.multiple_of(4 * GROUP * group, 64) + 8 * t, 8), :]
                out.append(alpha * gain * jnp.where(first_half, one, two))
            return tuple(out)

        def spread(group, coef):
            row, at = place(group)
            adds = []
            for q in range(GROUP):
                terms = []
                for i in range(4):
                    k = 4 * (q % 2) + i
                    piece = jnp.broadcast_to(coef[q // 2][k : k + 1, :], (8, 128))
                    terms.append(pm[GROUP * group + q, pl.ds(8 * i, 8), :] * piece)
                adds.append((terms[0] + terms[1]) + (terms[2] + terms[3]))
            for q in range(GROUP):
                d, r = table[16 + row, at + q], table[32 + row, at + q] - offset
                new[d, pl.ds(r, 8), :] = new[d, pl.ds(r, 8), :] + adds[q]

        groups = count // GROUP

        def stages(group, carry):
            sums, coef = carry
            nxt = project(group)
            spread(jnp.maximum(group - 2, 0), coef)
            return nxt, weigh(group - 1, sums)

        @pl.when(groups > 0)
        def _():
            none = tuple(jnp.zeros((8, 128), F32) for _ in range(GROUP // 2))
            sums, coef = lax.fori_loop(1, groups, stages, (project(0), none))
            spread(jnp.maximum(groups - 2, 0), coef)
            spread(groups - 1, weigh(groups - 1, sums))

    plan = steps()
    chain = ((x_ref, None, bufb, 0, n_all), (bufb, x_ref, bufa, 0, n_all),
             (bufa, bufb, bufb, 0, n_all), (bufb, bufa, o_ref, PAD, n_own))
    for (now, old, new, offset, count), (base, rows), (alpha, beta) in zip(chain, RANGES, plan):
        apply(now, old, new, offset, base, rows, alpha, beta, count)


def run_filter(table, coupling, x, v, p, w):
    smem = pl.BlockSpec(memory_space=pltpu.SMEM)
    vmem = pl.BlockSpec(memory_space=pltpu.VMEM)
    return pl.pallas_call(
        filter_kernel,
        out_shape=jax.ShapeDtypeStruct((G, 128, 128), F32),
        in_specs=[smem] * 2 + [vmem] * 2 + [pl.BlockSpec(memory_space=pltpu.HBM), vmem],
        out_specs=vmem,
        scratch_shapes=[
            pltpu.VMEM((1024, 16, 128), F32),
            pltpu.VMEM((G, ROWS, 128), F32),
            pltpu.VMEM((G, ROWS, 128), F32),
            pltpu.VMEM((G, ROWS, 128), F32),
            pltpu.VMEM((G, RANGES[0][1], 128), BF16),
            pltpu.VMEM((G, RANGES[0][1], 128), BF16),
            pltpu.VMEM((2 * RANGES[0][1], 256), F32),
            pltpu.VMEM((2 * RANGES[0][1], 256), F32),
            pltpu.VMEM((SLOTS, 32, 128), F32),
            pltpu.VMEM((4 * SLOTS, 128), F32),
            pltpu.VMEM((32 * GROUP, 128), F32),
            pltpu.SemaphoreType.DMA,
        ],
        compiler_params=pltpu.CompilerParams(vmem_limit_bytes=56 * 2**20),
        name="chebyshev",
    )(table, coupling, x, v, p, w)


MESH = pl.DeviceIdType.MESH
PARTS = ((0, 24, 16, (0, 1, 2)), (24, 24, 16, (1, 0, 2)), (48, 40, 24, (1, 2, 0)), (88, 40, 24, (0, 2, 1)))
A2A_CUTS = (9, 16)
V_PARTS = ((0, 32, 16, (0, 1)), (32, 32, 16, (1, 0)))


def position():
    return lax.axis_index("gx"), lax.axis_index("gy"), lax.axis_index("gz")


def plane_peer(offset):
    gx, gy, gz = position()
    return (lax.rem(gx + offset // 4, 4), lax.rem(gy + offset % 4, 4), gz)


def plane_source(offset):
    gx, gy, _ = position()
    return 4 * lax.rem(gx + 4 - offset // 4, 4) + lax.rem(gy + 4 - offset % 4, 4)


def line_peer(offset):
    gx, gy, gz = position()
    return (gx, gy, lax.rem(gz + offset, 8))


def greet():
    sem = pltpu.get_barrier_semaphore()

    def plane(o, _):
        pl.semaphore_signal(sem, inc=1, device_id=plane_peer(o), device_id_type=MESH)
        return 0

    def line(o, _):
        pl.semaphore_signal(sem, inc=1, device_id=line_peer(o), device_id_type=MESH)
        return 0

    lax.fori_loop(1, 16, plane, 0)
    lax.fori_loop(1, 8, line, 0)


def remote(src, dst, send, recv, target):
    return pltpu.make_async_remote_copy(
        src_ref=src, dst_ref=dst, send_sem=send, recv_sem=recv, device_id=target, device_id_type=MESH
    )


def pack(orb, pot, proj, perm, sent, vown, pown, cells, pair):
    first_half = lax.broadcasted_iota(jnp.int32, (16, 128), 1) < 64
    for q in range(G):
        sent[q] = orb[pl.ds(128 * q, 128), :].T
    pair[...] = pot[...].T
    vown[...] = jnp.concatenate([pair[pl.ds(0, 64, stride=2), :], pair[pl.ds(1, 64, stride=2), :]], axis=1)
    x = jnp.concatenate([proj[a] for a in range(8)], axis=0)
    top = x.astype(BF16)
    rest = x - top.astype(F32)
    mid = rest.astype(BF16)
    low = (rest - mid.astype(F32)).astype(BF16)
    parts = jnp.dot(jnp.concatenate([top, mid, low], axis=0), perm[...], preferred_element_type=F32)
    moved = (parts[:32] + parts[32:64]) + parts[64:]
    for t in range(4):
        cells[t] = moved[:, 128 * t : 128 * t + 128]
    for t in range(4):
        even, odd = cells[t, pl.ds(0, 16, stride=2), :], cells[t, pl.ds(1, 16, stride=2), :]
        pown[pl.ds(2 * t, 16, stride=8), :] = jnp.where(first_half, even, pltpu.roll(odd, 64, 1))
        pown[pl.ds(2 * t + 1, 16, stride=8), :] = jnp.where(first_half, pltpu.roll(even, 64, 1), odd)


def list_atoms(owner, anchor, extent, gz):
    rank = owner[...]
    z = jnp.concatenate([anchor[2:3, 128 * r : 128 * r + 128] for r in range(8)], axis=0)
    slab = rank % 8
    own = slab == gz
    near = ((slab == (gz + 7) % 8) & (z + MARGIN >= 128)) | ((slab == (gz + 1) % 8) & (z + B <= MARGIN))
    row = lax.broadcasted_iota(jnp.int32, (128, 128), 0)
    col = lax.broadcasted_iota(jnp.int32, (128, 128), 1)
    sub = lax.broadcasted_iota(jnp.int32, (8, 128), 0)
    before = (row < col).astype(F32)

    def ranks(mask):
        m = mask.astype(F32)
        inside = jnp.dot(m.astype(BF16), before.astype(BF16), preferred_element_type=F32)
        counts = jnp.sum(m, axis=1, keepdims=True)
        base = jnp.zeros((1, 1), F32)
        bases = []
        for r in range(8):
            bases.append(base)
            base = base + counts[r : r + 1]
        return inside + jnp.concatenate(bases, axis=0), base

    at_own, n_own = ranks(own)
    at_near, n_near = ranks(near)
    first = jnp.floor((n_own + (GROUP - 1.0)) * (1.0 / GROUP)) * GROUP
    last = first + jnp.floor((n_near + (GROUP - 1.0)) * (1.0 / GROUP)) * GROUP
    at = jnp.where(own, at_own, jnp.where(near, at_near + first, -1.0)).astype(jnp.int32)
    high = jnp.where(at >= 0, at // 128, -1)
    low = (at % 128).astype(F32).T
    ident = 128 * sub + lax.broadcasted_iota(jnp.int32, (8, 128), 1) + 1
    slot_row = lax.broadcasted_iota(jnp.int32, (16, 128), 0)
    shift = jnp.where(near, jnp.where(slab == (gz + 1) % 8, 128, -128), 0)
    fields = [ident // 32, ident % 32, rank // 8, z + shift + PAD, extent[...]]
    found = jnp.zeros((80, 128), F32)
    for r in range(8):
        hit = slot_row == high[r : r + 1]
        right = (low[:, r : r + 1] == col.astype(F32)).astype(BF16)
        left = [jnp.where(hit, f[r : r + 1].astype(F32), 0.0).astype(BF16) for f in fields]
        found = found + jnp.dot(jnp.concatenate(left, axis=0), right, preferred_element_type=F32)
    table = found[:16] * 32.0 + found[16:32]
    lane = lax.broadcasted_iota(jnp.int32, (16, 128), 1)
    start = jnp.where(table > 0.0, found[48:64], float(PAD))
    table = jnp.where(slot_row == 15, jnp.where(lane == 0, first, jnp.where(lane == 1, last, 0.0)), table)
    return jnp.concatenate([table, found[32:48], start, found[64:80]], axis=0).astype(jnp.int32)


def gather_kernel(
    orb, pot, proj, perm, owner, anchor, extent, x_out, v_out, p_out, table,
    sent, vown, pown, cells, pair,
    a2a_send, a2a_recv, p_send, p_recv, v_send, v_recv, twin_send, twin_recv, halo_send, halo_recv, here,
):
    gx, gy, gz = position()
    y, core = gz // 2, gz % 2
    mine = 4 * gx + gy
    greet()
    pack(orb, pot, proj, perm, sent, vown, pown, cells, pair)
    pl.semaphore_wait(pltpu.get_barrier_semaphore(), 22)
    local = [
        pltpu.make_async_copy(pown, p_out.at[gx, gy, y, core], here.at[0]),
        pltpu.make_async_copy(vown, v_out.at[gx, gy, pl.ds(16, 64)], here.at[1]),
        pltpu.make_async_copy(sent.at[mine], x_out.at[mine, pl.ds(PAD, 128)], here.at[2]),
    ]
    for copy in local:
        copy.start()
    where = (gx, gy, y)

    def near(dim, step):
        return lax.rem(where[dim] + step + 4, 4)

    def neighbour(dim, step):
        at = list(where)
        at[dim] = near(dim, step)
        return (at[0], at[1], 2 * at[2] + core)

    def p_view(part, at2, at3, rows, at1=None):
        start, _, _, (d1, d2, d3) = PARTS[part]
        idx = [None, None, None]
        idx[d1] = pl.ds(0, 4) if at1 is None else at1
        idx[d2] = at2
        idx[d3] = at3
        return p_out.at[idx[0], idx[1], idx[2], core, pl.ds(start + rows[0], rows[1])]

    def v_view(held, dim, at, start, rows):
        idx = [pl.ds(0, 4) if k in held else where[k] for k in range(2)]
        idx[dim] = at
        return v_out.at[idx[0], idx[1], pl.ds(16 + start, rows)]

    used = [0] * len(PARTS)

    def p_copy(part, src, dim, step):
        k = used[part]
        used[part] += 1
        return remote(src, src, p_send.at[part, k], p_recv.at[part, k], neighbour(dim, step))

    partner = (gx, gy, gz + 1 - 2 * core)
    twins = []

    def twin(part, at2, at3):
        k = sum(1 for t in twins if t[0] == part)
        src = p_view(part, at2, at3, (0, PARTS[part][1]))
        copy = remote(src, src, twin_send.at[part, k], twin_recv.at[part, k], partner)
        copy.start()
        twins.append((part, copy))

    def start(copies):
        for copy in copies:
            copy.start()
        return copies

    def wait(copies):
        for copy in copies:
            copy.wait()

    def a2a(o):
        peer = plane_peer(o)
        return remote(
            sent.at[4 * peer[0] + peer[1]], x_out.at[mine, pl.ds(PAD, 128)], a2a_send.at[o], a2a_recv.at[o], peer
        )

    def send_a2a(lo_o, hi_o):
        def step(o, _):
            a2a(o).start()
            return 0

        lax.fori_loop(lo_o, hi_o, step, 0)

    def v_copies(phase):
        out = []
        for i, (at, rows, half, order) in enumerate(V_PARTS):
            dim, held = order[phase], order[:phase]
            src = v_view(held, dim, where[dim], at, rows)
            for k in range(3):
                sems = (v_send.at[i, 3 * phase + k], v_recv.at[i, 3 * phase + k])
                out.append(remote(src, src, *sems, neighbour(dim, k + 1)))
        return out

    def along3(part, at2):
        d3 = PARTS[part][3][2]
        src = p_view(part, at2, where[d3], (0, PARTS[part][1]))
        return [p_copy(part, src, d3, 1), p_copy(part, src, d3, -1)]

    def forward3(part, at2):
        rows, half, d3 = PARTS[part][1], PARTS[part][2], PARTS[part][3][2]
        return [
            p_copy(part, p_view(part, at2, near(d3, -1), (0, half)), d3, 1),
            p_copy(part, p_view(part, at2, near(d3, 1), (half, rows - half)), d3, -1),
        ]

    every = range(len(PARTS))
    dims = [part[3] for part in PARTS]
    right, left = line_peer(1), line_peer(7)
    whole = pl.ds(0, 4)
    wait(local)

    first = []
    for i in every:
        d1, d2, d3 = dims[i]
        own = p_view(i, where[d2], where[d3], (0, PARTS[i][1]), where[d1])
        first += [p_copy(i, own, d1, k) for k in (1, 2, 3)]
    start(first)
    v = start(v_copies(0))
    send_a2a(1, A2A_CUTS[0])
    wait(first)
    second, a5 = [], []
    for i in every:
        d1, d2, d3 = dims[i]
        row = p_view(i, where[d2], where[d3], (0, PARTS[i][1]))
        second += [p_copy(i, row, d2, k) for k in (1, 2, 3)]
    start(second)
    for i in every:
        a5 += start(along3(i, where[dims[i][1]]))
    wait(v)
    v = start(v_copies(1))
    send_a2a(A2A_CUTS[0], A2A_CUTS[1])
    wait(second)
    b5 = []
    for i in every:
        for k in (1, 2, 3):
            b5 += start(along3(i, near(dims[i][1], k)))
    for i in every:
        twin(i, whole, where[dims[i][2]])
    wait(v)
    halos = start([
        remote(v_out.at[whole, whole, pl.ds(64, 16)], v_out.at[whole, whole, pl.ds(0, 16)],
               halo_send.at[2], halo_recv.at[2], right),
        remote(v_out.at[whole, whole, pl.ds(16, 16)], v_out.at[whole, whole, pl.ds(80, 16)],
               halo_send.at[3], halo_recv.at[3], left),
    ])
    wait(a5)
    last = []
    for i in every:
        last += start(forward3(i, where[dims[i][1]]))
    table[...] = list_atoms(owner, anchor, extent, gz)

    def finish_a2a(o, _):
        a2a(o).wait()
        return 0

    lax.fori_loop(1, 16, finish_a2a, 0)
    halos += start([
        remote(x_out.at[pl.ds(0, G), pl.ds(PAD + 128 - HALO, HALO)], x_out.at[pl.ds(0, G), pl.ds(PAD - HALO, HALO)],
               halo_send.at[0], halo_recv.at[0], right),
        remote(x_out.at[pl.ds(0, G), pl.ds(PAD, HALO)], x_out.at[pl.ds(0, G), pl.ds(PAD + 128, HALO)],
               halo_send.at[1], halo_recv.at[1], left),
    ])
    wait(b5)
    for i in every:
        for k in (1, 2, 3):
            last += start(forward3(i, near(dims[i][1], k)))
    for i in every:
        for k in (1, -1):
            twin(i, whole, near(dims[i][2], k))
    wait(last)
    for i in every:
        twin(i, whole, near(dims[i][2], 2))
    wait(halos)
    wait([copy for _, copy in twins])


def permutation():
    at = np.arange(512)
    perm = np.zeros((512, 512), np.float32)
    perm[at, (at % 8) * 64 + at // 8] = 1.0
    return perm


def run_gather(orb, pot, proj, perm, owner, anchor, extent):
    vmem = pl.BlockSpec(memory_space=pltpu.VMEM)
    hbm = pl.BlockSpec(memory_space=pltpu.HBM)
    dma = pltpu.SemaphoreType.DMA
    return pl.pallas_call(
        gather_kernel,
        out_shape=(
            jax.ShapeDtypeStruct((G, ROWS, 128), F32),
            jax.ShapeDtypeStruct((4, 4, 96, 128), F32),
            jax.ShapeDtypeStruct((4, 4, 4, 2, 128, 128), F32),
            jax.ShapeDtypeStruct((64, 128), jnp.int32),
        ),
        in_specs=[vmem] * 7,
        out_specs=(hbm, hbm, hbm, vmem),
        scratch_shapes=[
            pltpu.VMEM((G, 128, 128), F32),
            pltpu.VMEM((64, 128), F32),
            pltpu.VMEM((128, 128), F32),
            pltpu.VMEM((4, 32, 128), F32),
            pltpu.VMEM((128, 64), F32),
            dma((16,)), dma((16,)), dma((4, 22)), dma((4, 22)), dma((2, 6)), dma((2, 6)),
            dma((4, 4)), dma((4, 4)), dma((4,)), dma((4,)), dma((3,)),
        ],
        compiler_params=pltpu.CompilerParams(collective_id=1, has_side_effects=True),
        name="gather",
    )(orb, pot, proj, perm, owner, anchor, extent)


def return_kernel(
    y, out, total, recv, gram_a, gram_b, a2a_send, a2a_recv, a_send, a_recv, b_send, b_recv, here,
):
    gx, gy, gz = position()
    mine = 4 * gx + gy
    own = pltpu.make_async_copy(y.at[mine], recv.at[mine], here.at[0])
    own.start()
    greet()
    pl.semaphore_wait(pltpu.get_barrier_semaphore(), 22)

    def a2a(o):
        peer = plane_peer(o)
        return remote(
            y.at[4 * peer[0] + peer[1]], recv.at[mine], a2a_send.at[o], a2a_recv.at[o], peer
        )

    def send(o, _):
        a2a(o).start()
        return 0

    lax.fori_loop(1, 16, send, 0)

    def place(source):
        out[pl.ds(pl.multiple_of(128 * source, 128), 128), :] = recv[source].T

    own.wait()
    place(mine)

    def receive(o, _):
        a2a(o).wait()
        place(plane_source(o))
        return 0

    lax.fori_loop(1, 16, receive, 0)

    def gram(c, acc):
        cells = jnp.concatenate([out[pl.ds(8 * c + i, 32, stride=64), :] for i in range(8)], axis=1)
        top = cells.astype(BF16)
        rest = (cells - top.astype(F32)).astype(BF16)
        both = jnp.concatenate([top, rest], axis=0)
        return acc + lax.dot_general(both, both, (((1,), (1,)), ((), ())), preferred_element_type=F32)

    acc = lax.fori_loop(0, 8, gram, jnp.zeros((64, 64), F32))
    g = acc[:32, :32] + (acc[:32, 32:] + acc[32:, :32])
    gram_a[mine] = jnp.concatenate([g[8 * b : 8 * b + 8] for b in range(4)], axis=1)

    def plane(o):
        return remote(gram_a.at[mine], gram_a.at[mine], a_send.at[o], a_recv.at[o], plane_peer(o))

    def line(o):
        return remote(gram_b.at[gz], gram_b.at[gz], b_send.at[o], b_recv.at[o], line_peer(o))

    def start_plane(o, _):
        plane(o).start()
        return 0

    def wait_plane(o, _):
        plane(o).wait()
        return 0

    def start_line(o, _):
        line(o).start()
        return 0

    def wait_line(o, _):
        line(o).wait()
        return 0

    lax.fori_loop(1, 16, start_plane, 0)
    lax.fori_loop(1, 16, wait_plane, 0)
    acc = gram_a[0]
    for i in range(1, 16):
        acc = acc + gram_a[i]
    gram_b[gz] = acc
    lax.fori_loop(1, 8, start_line, 0)
    lax.fori_loop(1, 8, wait_line, 0)
    acc = gram_b[0]
    for i in range(1, 8):
        acc = acc + gram_b[i]
    acc = acc * (1.0 / (32 * 32 * 1024))
    for b in range(4):
        total[pl.ds(8 * b, 8), :] = acc[:, 32 * b : 32 * b + 32]


def run_return(y):
    vmem = pl.BlockSpec(memory_space=pltpu.VMEM)
    dma = pltpu.SemaphoreType.DMA
    return pl.pallas_call(
        return_kernel,
        out_shape=(jax.ShapeDtypeStruct((2048, 128), F32), jax.ShapeDtypeStruct((32, 32), F32)),
        in_specs=[vmem],
        out_specs=(vmem, vmem),
        scratch_shapes=[
            pltpu.VMEM((G, 128, 128), F32),
            pltpu.VMEM((G, 8, 128), F32),
            pltpu.VMEM((8, 8, 128), F32),
            dma((16,)), dma((16,)), dma((16,)), dma((16,)), dma((8,)), dma((8,)), dma((1,)),
        ],
        compiler_params=pltpu.CompilerParams(collective_id=2, has_side_effects=True),
        name="giveback",
    )(y)


def body(orbitals, potential, projectors, owner_rank, box_anchor, box_extent, coupling):
    perm = jnp.asarray(permutation()).astype(BF16)
    x, v, p, table = run_gather(
        orbitals.reshape(2048, 128), potential.reshape(64, 128), projectors, perm,
        owner_rank.reshape(8, 128), box_anchor, box_extent.reshape(8, 128),
    )
    w = jnp.asarray(weights()).astype(BF16)
    y = run_filter(
        table, coupling.T,
        x, v.reshape(G, 96, 128), p.reshape(1024, 16, 128), w,
    )
    filtered, total = run_return(y)
    return filtered.reshape(orbitals.shape), total


def solution(mesh):
    return jax.shard_map(
        body,
        mesh=mesh,
        in_specs=(
            P(None, "gx", "gy", "gz"),
            P("gx", "gy", "gz"),
            P(("gx", "gy", "gz"), None, None),
            P(),
            P(),
            P(),
            P(),
        ),
        out_specs=(P(None, "gx", "gy", "gz"), P()),
        check_vma=False,
    )
```

```python
import functools

import jax
import jax.numpy as jnp
import numpy as np
from jax import lax
from jax.experimental import pallas as pl
from jax.experimental.pallas import tpu as pltpu
from jax.sharding import PartitionSpec as P

B = 8
DEGREE = 4
STENCIL = (
    -5369.0 / 1800.0,
    12.0 / 7.0,
    -15.0 / 56.0,
    10.0 / 189.0,
    -1.0 / 112.0,
    2.0 / 1925.0,
    -1.0 / 16632.0,
)
SPACING = 0.5
LOW_EDGE = -2.5
CUTOFF = 4.0
UPPER = 60.0
HALF = (UPPER - CUTOFF) / 2.0
MIDDLE = (UPPER + CUTOFF) / 2.0

G = 16
PAD = 40
ROWS = 208
HALO = 32
MARGIN = 27
RANGES = ((16, 176), (24, 160), (32, 144), (40, 128))
WSCALE = 35.0 / 32.0
KIN = -0.5 / (SPACING * SPACING)
DIAG = KIN * 3.0 * STENCIL[0] - MIDDLE
GROUP = 16
SLOTS = 1024 + 2 * GROUP
F32 = jnp.float32
BF16 = jnp.bfloat16


def steps():
    sigma_one = HALF / (LOW_EDGE - MIDDLE)
    sigma = sigma_one
    out = [(sigma_one / HALF, 0.0)]
    for _ in range(1, DEGREE):
        nxt = 1.0 / (2.0 / sigma_one - sigma)
        out.append((2.0 * nxt / HALF, sigma * nxt))
        sigma = nxt
    return out


def weights():
    c = np.asarray(STENCIL, np.float64) * WSCALE

    def coef(m):
        m = abs(m)
        return c[m] if 1 <= m <= 6 else 0.0

    eye = np.eye(8)
    band = {s: np.array([[coef(8 * s + a - b) for b in range(8)] for a in range(8)]) for s in (-1, 0, 1)}
    two = np.eye(2)
    centre = np.kron(two, np.kron(band[0], eye) + np.kron(eye, band[0]))
    ym, yp = (np.kron(two, np.kron(eye, band[s])) for s in (-1, 1))
    xm, xp = (np.kron(two, np.kron(band[s], eye)) for s in (-1, 1))
    zero = np.zeros_like(centre)
    own = np.block([[centre, zero], [zero, centre]])
    across_x = np.block([[xp, xm], [xm, xp]])
    across_y = np.block([[yp, ym], [ym, yp]])
    both = [np.concatenate([own, across_x]), across_y]
    return np.concatenate([both[0], both[0], both[1], both[1]], axis=0).astype(np.float32)


def filter_kernel(
    table, coupling,
    x_ref, vp_ref, p_hbm, w_ref, o_ref,
    p_ref, v_ref, bufa, bufb, hi, lo, acc_x, acc_y, pm, gains, prods, load_sem,
):
    lane = lax.broadcasted_iota(jnp.int32, (8, 128), 1)
    sub = lax.broadcasted_iota(jnp.int32, (8, 128), 0)
    first_half = lane < 64
    upper = sub < 4
    low = sub % 4
    reach = jnp.maximum(jnp.maximum((lane % 64) // 8, lane % 8), sub)
    n_own, n_all = table[15, 0], table[15, 1]

    load = pltpu.make_async_copy(p_hbm, p_ref, load_sem)
    load.start()

    def place(group):
        per_row = 128 // GROUP
        return group // per_row, GROUP * lax.rem(group, per_row)

    def prepare(group, _):
        row, at = place(group)
        fours = []
        for q in range(GROUP):
            slot = GROUP * group + q
            ident = jnp.maximum(table[row, at + q] - 1, 0)
            keep = reach < table[48 + row, at + q]
            g = [coupling[k, ident] for k in range(4)]
            lines = []
            for p in range(2):
                value = jnp.where(keep, p_ref[ident, pl.ds(8 * p, 8), :], 0.0)
                pm[slot, pl.ds(16 * p, 8), :] = value
                pm[slot, pl.ds(16 * p + 8, 8), :] = pltpu.roll(value, 64, 1)
                lines += [jnp.where(first_half, g[2 * p], g[2 * p + 1]), jnp.where(first_half, g[2 * p + 1], g[2 * p])]
            even, odd = jnp.where(low < 2, lines[0], lines[2]), jnp.where(low < 2, lines[1], lines[3])
            fours.append(jnp.where(low % 2 == 0, even, odd))
        for t in range(GROUP // 2):
            gains[pl.ds(pl.multiple_of(4 * GROUP * group, 64) + 8 * t, 8), :] = jnp.where(
                upper, fours[2 * t], fours[2 * t + 1]
            )
        return 0

    def unpack(d, _):
        for r in range(0, 96, 8):
            pair = vp_ref[d, pl.ds(r, 8), :]
            swapped = pltpu.roll(pair, 64, 1)
            v_ref[d, pl.ds(8 + 2 * r, 8, stride=2), :] = jnp.where(first_half, pair, swapped) + DIAG
            v_ref[d, pl.ds(9 + 2 * r, 8, stride=2), :] = jnp.where(first_half, swapped, pair) + DIAG
        return 0

    lax.fori_loop(0, G, unpack, 0)

    def apply(now, old, new, offset, base, rows, alpha, beta, count):
        def split(d, _):
            for r in range(0, rows, 16):
                v = now[d, pl.ds(base + r, 16), :]
                top = v.astype(BF16)
                hi[d, pl.ds(r, 16), :] = top
                lo[d, pl.ds(r, 16), :] = (v - top.astype(F32)).astype(BF16)
            return 0

        lax.fori_loop(0, G, split, 0)

        def multiply(it):
            px, py = it // 2, it % 2

            def dom(kx, ky):
                return 4 * lax.rem(px + kx, 4) + lax.rem(py + ky, 4)

            def pair(part, a, b):
                return jnp.concatenate([part[a, pl.ds(0, rows), :], part[b, pl.ds(0, rows), :]], axis=1)

            def stack(cases):
                return jnp.concatenate(
                    [jnp.concatenate([pair(part, *c) for part in (hi, lo) for c in case], axis=1) for case in cases],
                    axis=0,
                )

            lhs_x = stack([((dom(0, k), dom(2, k)), (dom(1, k), dom(3, k))) for k in (0, 2)])
            lhs_y = stack([((dom(k, 1), dom(k, 3)),) for k in (0, 2)])
            acc_x[pl.ds(0, 2 * rows), :] = jnp.dot(lhs_x, w_ref[pl.ds(0, 1024), :], preferred_element_type=F32)
            acc_y[pl.ds(0, 2 * rows), :] = jnp.dot(lhs_y, w_ref[pl.ds(1024, 512), :], preferred_element_type=F32)

        def finish(it):
            px, py = it // 2, it % 2
            for kx in range(2):
                for ky in range(2):
                    d = 4 * (px + 2 * kx) + py + 2 * ky
                    for r in range(0, rows, 8):
                        s = base + r
                        mid = now[d, pl.ds(s, 8), :]
                        val = acc_x[pl.ds(rows * ky + r, 8), pl.ds(128 * kx, 128)]
                        val = val + acc_y[pl.ds(rows * kx + r, 8), pl.ds(128 * ky, 128)]
                        val = val * (alpha * KIN / WSCALE)
                        val = val + (alpha * v_ref[d, pl.ds(s, 8), :]) * mid
                        for m in range(1, 7):
                            val = val + (alpha * KIN * STENCIL[m]) * (
                                now[d, pl.ds(s + m, 8), :] + now[d, pl.ds(s - m, 8), :]
                            )
                        if beta:
                            val = val - beta * old[d, pl.ds(s, 8), :]
                        new[d, pl.ds(s - offset, 8), :] = val

        def both_parts(it, _):
            finish(it)
            multiply(it + 1)
            return 0

        multiply(0)
        lax.fori_loop(0, 3, both_parts, 0)
        finish(3)

        if old is None:
            load.wait()
            lax.fori_loop(0, n_all // GROUP, prepare, 0)

        def project(group):
            row, at = place(group)
            for q in range(GROUP):
                box = now[table[16 + row, at + q], pl.ds(table[32 + row, at + q], 8), :]
                for i in range(4):
                    prods[pl.ds(32 * q + 8 * i, 8), :] = pm[GROUP * group + q, pl.ds(8 * i, 8), :] * box
            out = []
            for t in range(GROUP // 2):
                v = [prods[pl.ds(64 * t + i, 8, stride=8), :] for i in range(8)]
                while len(v) > 1:
                    v = [v[i] + v[i + 1] for i in range(0, len(v), 2)]
                out.append(v[0])
            return tuple(out)

        def weigh(group, sums):
            out = []
            for t in range(GROUP // 2):
                v = sums[t]
                one = jnp.sum(jnp.where(first_half, v, 0.0), axis=1, keepdims=True)
                two = jnp.sum(jnp.where(first_half, 0.0, v), axis=1, keepdims=True)
                gain = gains[pl.ds(pl.multiple_of(4 * GROUP * group, 64) + 8 * t, 8), :]
                out.append(alpha * gain * jnp.where(first_half, one, two))
            return tuple(out)

        def spread(group, coef):
            row, at = place(group)
            adds = []
            for q in range(GROUP):
                terms = []
                for i in range(4):
                    k = 4 * (q % 2) + i
                    piece = jnp.broadcast_to(coef[q // 2][k : k + 1, :], (8, 128))
                    terms.append(pm[GROUP * group + q, pl.ds(8 * i, 8), :] * piece)
                adds.append((terms[0] + terms[1]) + (terms[2] + terms[3]))
            for q in range(GROUP):
                d, r = table[16 + row, at + q], table[32 + row, at + q] - offset
                new[d, pl.ds(r, 8), :] = new[d, pl.ds(r, 8), :] + adds[q]

        groups = count // GROUP

        def stages(group, carry):
            sums, coef = carry
            nxt = project(group)
            spread(jnp.maximum(group - 2, 0), coef)
            return nxt, weigh(group - 1, sums)

        @pl.when(groups > 0)
        def _():
            none = tuple(jnp.zeros((8, 128), F32) for _ in range(GROUP // 2))
            sums, coef = lax.fori_loop(1, groups, stages, (project(0), none))
            spread(jnp.maximum(groups - 2, 0), coef)
            spread(groups - 1, weigh(groups - 1, sums))

    plan = steps()
    chain = ((x_ref, None, bufb, 0, n_all), (bufb, x_ref, bufa, 0, n_all),
             (bufa, bufb, bufb, 0, n_all), (bufb, bufa, o_ref, PAD, n_own))
    for (now, old, new, offset, count), (base, rows), (alpha, beta) in zip(chain, RANGES, plan):
        apply(now, old, new, offset, base, rows, alpha, beta, count)


def run_filter(table, coupling, x, v, p, w):
    smem = pl.BlockSpec(memory_space=pltpu.SMEM)
    vmem = pl.BlockSpec(memory_space=pltpu.VMEM)
    return pl.pallas_call(
        filter_kernel,
        out_shape=jax.ShapeDtypeStruct((G, 128, 128), F32),
        in_specs=[smem] * 2 + [vmem] * 2 + [pl.BlockSpec(memory_space=pltpu.HBM), vmem],
        out_specs=vmem,
        scratch_shapes=[
            pltpu.VMEM((1024, 16, 128), F32),
            pltpu.VMEM((G, ROWS, 128), F32),
            pltpu.VMEM((G, ROWS, 128), F32),
            pltpu.VMEM((G, ROWS, 128), F32),
            pltpu.VMEM((G, RANGES[0][1], 128), BF16),
            pltpu.VMEM((G, RANGES[0][1], 128), BF16),
            pltpu.VMEM((2 * RANGES[0][1], 256), F32),
            pltpu.VMEM((2 * RANGES[0][1], 256), F32),
            pltpu.VMEM((SLOTS, 32, 128), F32),
            pltpu.VMEM((4 * SLOTS, 128), F32),
            pltpu.VMEM((32 * GROUP, 128), F32),
            pltpu.SemaphoreType.DMA,
        ],
        compiler_params=pltpu.CompilerParams(vmem_limit_bytes=56 * 2**20),
        name="chebyshev",
    )(table, coupling, x, v, p, w)


MESH = pl.DeviceIdType.MESH
PARTS = ((0, 24, 16, (0, 1, 2)), (24, 24, 16, (1, 0, 2)), (48, 40, 24, (1, 2, 0)), (88, 40, 24, (0, 2, 1)))
A2A_CUTS = (12, 16)
V_PARTS = ((0, 32, 16, (0, 1)), (32, 32, 16, (1, 0)))


def position():
    return lax.axis_index("gx"), lax.axis_index("gy"), lax.axis_index("gz")


def plane_peer(offset):
    gx, gy, gz = position()
    return (lax.rem(gx + offset // 4, 4), lax.rem(gy + offset % 4, 4), gz)


def plane_source(offset):
    gx, gy, _ = position()
    return 4 * lax.rem(gx + 4 - offset // 4, 4) + lax.rem(gy + 4 - offset % 4, 4)


def line_peer(offset):
    gx, gy, gz = position()
    return (gx, gy, lax.rem(gz + offset, 8))


def greet():
    sem = pltpu.get_barrier_semaphore()

    def plane(o, _):
        pl.semaphore_signal(sem, inc=1, device_id=plane_peer(o), device_id_type=MESH)
        return 0

    def line(o, _):
        pl.semaphore_signal(sem, inc=1, device_id=line_peer(o), device_id_type=MESH)
        return 0

    lax.fori_loop(1, 16, plane, 0)
    lax.fori_loop(1, 8, line, 0)


def remote(src, dst, send, recv, target):
    return pltpu.make_async_remote_copy(
        src_ref=src, dst_ref=dst, send_sem=send, recv_sem=recv, device_id=target, device_id_type=MESH
    )


def pack(orb, pot, proj, perm, sent, vown, pown, cells, pair):
    first_half = lax.broadcasted_iota(jnp.int32, (16, 128), 1) < 64
    for q in range(G):
        sent[q] = orb[pl.ds(128 * q, 128), :].T
    pair[...] = pot[...].T
    vown[...] = jnp.concatenate([pair[pl.ds(0, 64, stride=2), :], pair[pl.ds(1, 64, stride=2), :]], axis=1)
    x = jnp.concatenate([proj[a] for a in range(8)], axis=0)
    top = x.astype(BF16)
    rest = x - top.astype(F32)
    mid = rest.astype(BF16)
    low = (rest - mid.astype(F32)).astype(BF16)
    parts = jnp.dot(jnp.concatenate([top, mid, low], axis=0), perm[...], preferred_element_type=F32)
    moved = (parts[:32] + parts[32:64]) + parts[64:]
    for t in range(4):
        cells[t] = moved[:, 128 * t : 128 * t + 128]
    for t in range(4):
        even, odd = cells[t, pl.ds(0, 16, stride=2), :], cells[t, pl.ds(1, 16, stride=2), :]
        pown[pl.ds(2 * t, 16, stride=8), :] = jnp.where(first_half, even, pltpu.roll(odd, 64, 1))
        pown[pl.ds(2 * t + 1, 16, stride=8), :] = jnp.where(first_half, pltpu.roll(even, 64, 1), odd)


def list_atoms(owner, anchor, extent, gz):
    rank = owner[...]
    z = jnp.concatenate([anchor[2:3, 128 * r : 128 * r + 128] for r in range(8)], axis=0)
    slab = rank % 8
    own = slab == gz
    near = ((slab == (gz + 7) % 8) & (z + MARGIN >= 128)) | ((slab == (gz + 1) % 8) & (z + B <= MARGIN))
    row = lax.broadcasted_iota(jnp.int32, (128, 128), 0)
    col = lax.broadcasted_iota(jnp.int32, (128, 128), 1)
    sub = lax.broadcasted_iota(jnp.int32, (8, 128), 0)
    before = (row < col).astype(F32)

    def ranks(mask):
        m = mask.astype(F32)
        inside = jnp.dot(m.astype(BF16), before.astype(BF16), preferred_element_type=F32)
        counts = jnp.sum(m, axis=1, keepdims=True)
        base = jnp.zeros((1, 1), F32)
        bases = []
        for r in range(8):
            bases.append(base)
            base = base + counts[r : r + 1]
        return inside + jnp.concatenate(bases, axis=0), base

    at_own, n_own = ranks(own)
    at_near, n_near = ranks(near)
    first = jnp.floor((n_own + (GROUP - 1.0)) * (1.0 / GROUP)) * GROUP
    last = first + jnp.floor((n_near + (GROUP - 1.0)) * (1.0 / GROUP)) * GROUP
    at = jnp.where(own, at_own, jnp.where(near, at_near + first, -1.0)).astype(jnp.int32)
    high = jnp.where(at >= 0, at // 128, -1)
    low = (at % 128).astype(F32).T
    ident = 128 * sub + lax.broadcasted_iota(jnp.int32, (8, 128), 1) + 1
    slot_row = lax.broadcasted_iota(jnp.int32, (16, 128), 0)
    shift = jnp.where(near, jnp.where(slab == (gz + 1) % 8, 128, -128), 0)
    fields = [ident // 32, ident % 32, rank // 8, z + shift + PAD, extent[...]]
    found = jnp.zeros((80, 128), F32)
    for r in range(8):
        hit = slot_row == high[r : r + 1]
        right = (low[:, r : r + 1] == col.astype(F32)).astype(BF16)
        left = [jnp.where(hit, f[r : r + 1].astype(F32), 0.0).astype(BF16) for f in fields]
        found = found + jnp.dot(jnp.concatenate(left, axis=0), right, preferred_element_type=F32)
    table = found[:16] * 32.0 + found[16:32]
    lane = lax.broadcasted_iota(jnp.int32, (16, 128), 1)
    start = jnp.where(table > 0.0, found[48:64], float(PAD))
    table = jnp.where(slot_row == 15, jnp.where(lane == 0, first, jnp.where(lane == 1, last, 0.0)), table)
    return jnp.concatenate([table, found[32:48], start, found[64:80]], axis=0).astype(jnp.int32)


def gather_kernel(
    orb, pot, proj, perm, owner, anchor, extent, x_out, v_out, p_out, table,
    sent, vown, pown, cells, pair,
    a2a_send, a2a_recv, p_send, p_recv, v_send, v_recv, twin_send, twin_recv, halo_send, halo_recv, here,
):
    gx, gy, gz = position()
    y, core = gz // 2, gz % 2
    mine = 4 * gx + gy
    greet()
    pack(orb, pot, proj, perm, sent, vown, pown, cells, pair)
    pl.semaphore_wait(pltpu.get_barrier_semaphore(), 22)
    local = [
        pltpu.make_async_copy(pown, p_out.at[gx, gy, y, core], here.at[0]),
        pltpu.make_async_copy(vown, v_out.at[gx, gy, pl.ds(16, 64)], here.at[1]),
        pltpu.make_async_copy(sent.at[mine], x_out.at[mine, pl.ds(PAD, 128)], here.at[2]),
    ]
    for copy in local:
        copy.start()
    where = (gx, gy, y)

    def near(dim, step):
        return lax.rem(where[dim] + step + 4, 4)

    def neighbour(dim, step):
        at = list(where)
        at[dim] = near(dim, step)
        return (at[0], at[1], 2 * at[2] + core)

    def p_view(part, at2, at3, rows, at1=None):
        start, _, _, (d1, d2, d3) = PARTS[part]
        idx = [None, None, None]
        idx[d1] = pl.ds(0, 4) if at1 is None else at1
        idx[d2] = at2
        idx[d3] = at3
        return p_out.at[idx[0], idx[1], idx[2], core, pl.ds(start + rows[0], rows[1])]

    def v_view(held, dim, at, start, rows):
        idx = [pl.ds(0, 4) if k in held else where[k] for k in range(2)]
        idx[dim] = at
        return v_out.at[idx[0], idx[1], pl.ds(16 + start, rows)]

    used = [0] * len(PARTS)

    def p_copy(part, src, dim, step, dst=None):
        k = used[part]
        used[part] += 1
        return remote(src, src if dst is None else dst, p_send.at[part, k], p_recv.at[part, k], neighbour(dim, step))

    partner = (gx, gy, gz + 1 - 2 * core)
    twins = []

    def twin(part, at2, at3):
        k = sum(1 for t in twins if t[0] == part)
        src = p_view(part, at2, at3, (0, PARTS[part][1]))
        copy = remote(src, src, twin_send.at[part, k], twin_recv.at[part, k], partner)
        copy.start()
        twins.append((part, copy))

    def start(copies):
        for copy in copies:
            copy.start()
        return copies

    def wait(copies):
        for copy in copies:
            copy.wait()

    def a2a(o):
        peer = plane_peer(o)
        return remote(
            sent.at[4 * peer[0] + peer[1]], x_out.at[mine, pl.ds(PAD, 128)], a2a_send.at[o], a2a_recv.at[o], peer
        )

    def send_a2a(lo_o, hi_o):
        def step(o, _):
            a2a(o).start()
            return 0

        lax.fori_loop(lo_o, hi_o, step, 0)

    def v_copies(phase):
        out = []
        for i, (at, rows, half, order) in enumerate(V_PARTS):
            dim, held = order[phase], order[:phase]
            dst = v_view(held, dim, where[dim], at, rows)
            src = dst if phase else vown.at[pl.ds(at, rows)]
            for k in range(3):
                sems = (v_send.at[i, 3 * phase + k], v_recv.at[i, 3 * phase + k])
                out.append(remote(src, dst, *sems, neighbour(dim, k + 1)))
        return out

    def along3(part, at2):
        d3 = PARTS[part][3][2]
        src = p_view(part, at2, where[d3], (0, PARTS[part][1]))
        return [p_copy(part, src, d3, 1), p_copy(part, src, d3, -1)]

    def forward3(part, at2):
        rows, half, d3 = PARTS[part][1], PARTS[part][2], PARTS[part][3][2]
        return [
            p_copy(part, p_view(part, at2, near(d3, -1), (0, half)), d3, 1),
            p_copy(part, p_view(part, at2, near(d3, 1), (half, rows - half)), d3, -1),
        ]

    every = range(len(PARTS))
    dims = [part[3] for part in PARTS]
    right, left = line_peer(1), line_peer(7)
    whole = pl.ds(0, 4)
    first = []
    for i in every:
        d1, d2, d3 = dims[i]
        own = p_view(i, where[d2], where[d3], (0, PARTS[i][1]), where[d1])
        src = pown.at[pl.ds(PARTS[i][0], PARTS[i][1])]
        first += [p_copy(i, src, d1, k, own) for k in (1, 3, 2)]
    start(first)
    v = start(v_copies(0))
    send_a2a(1, A2A_CUTS[0])
    table[...] = list_atoms(owner, anchor, extent, gz)
    wait(local)
    wait(first)
    second, a5 = [], []
    for k in (1, 3, 2):
        for i in every:
            d1, d2, d3 = dims[i]
            second.append(p_copy(i, p_view(i, where[d2], where[d3], (0, PARTS[i][1])), d2, k))
    start(second)
    for i in every:
        a5 += start(along3(i, where[dims[i][1]]))
    wait(v)
    v = start(v_copies(1))
    send_a2a(A2A_CUTS[0], A2A_CUTS[1])
    b5 = []
    at = 0
    for k in (1, 3, 2):
        for i in every:
            wait(second[at : at + 1])
            at += 1
            b5 += start(along3(i, near(dims[i][1], -k)))
    for i in every:
        twin(i, whole, where[dims[i][2]])
    wait(v)
    halos = start([
        remote(v_out.at[whole, whole, pl.ds(64, 16)], v_out.at[whole, whole, pl.ds(0, 16)],
               halo_send.at[2], halo_recv.at[2], right),
        remote(v_out.at[whole, whole, pl.ds(16, 16)], v_out.at[whole, whole, pl.ds(80, 16)],
               halo_send.at[3], halo_recv.at[3], left),
    ])
    wait(a5)
    last = []
    for i in every:
        last += start(forward3(i, where[dims[i][1]]))

    def finish_a2a(o, _):
        a2a(o).wait()
        return 0

    at = 0
    for k in (1, 3, 2):
        for i in every:
            wait(b5[at : at + 2])
            at += 2
            last += start(forward3(i, near(dims[i][1], -k)))
    lax.fori_loop(1, 16, finish_a2a, 0)
    halos += start([
        remote(x_out.at[pl.ds(0, G), pl.ds(PAD + 128 - HALO, HALO)], x_out.at[pl.ds(0, G), pl.ds(PAD - HALO, HALO)],
               halo_send.at[0], halo_recv.at[0], right),
        remote(x_out.at[pl.ds(0, G), pl.ds(PAD, HALO)], x_out.at[pl.ds(0, G), pl.ds(PAD + 128, HALO)],
               halo_send.at[1], halo_recv.at[1], left),
    ])
    for i in every:
        for k in (1, -1):
            twin(i, whole, near(dims[i][2], k))
    wait(last)
    for i in every:
        twin(i, whole, near(dims[i][2], 2))
    wait(halos)
    wait([copy for _, copy in twins])


def permutation():
    at = np.arange(512)
    perm = np.zeros((512, 512), np.float32)
    perm[at, (at % 8) * 64 + at // 8] = 1.0
    return perm


def run_gather(orb, pot, proj, perm, owner, anchor, extent):
    vmem = pl.BlockSpec(memory_space=pltpu.VMEM)
    hbm = pl.BlockSpec(memory_space=pltpu.HBM)
    dma = pltpu.SemaphoreType.DMA
    return pl.pallas_call(
        gather_kernel,
        out_shape=(
            jax.ShapeDtypeStruct((G, ROWS, 128), F32),
            jax.ShapeDtypeStruct((4, 4, 96, 128), F32),
            jax.ShapeDtypeStruct((4, 4, 4, 2, 128, 128), F32),
            jax.ShapeDtypeStruct((64, 128), jnp.int32),
        ),
        in_specs=[vmem] * 7,
        out_specs=(hbm, hbm, hbm, vmem),
        scratch_shapes=[
            pltpu.VMEM((G, 128, 128), F32),
            pltpu.VMEM((64, 128), F32),
            pltpu.VMEM((128, 128), F32),
            pltpu.VMEM((4, 32, 128), F32),
            pltpu.VMEM((128, 64), F32),
            dma((16,)), dma((16,)), dma((4, 22)), dma((4, 22)), dma((2, 6)), dma((2, 6)),
            dma((4, 4)), dma((4, 4)), dma((4,)), dma((4,)), dma((3,)),
        ],
        compiler_params=pltpu.CompilerParams(collective_id=1, has_side_effects=True),
        name="gather",
    )(orb, pot, proj, perm, owner, anchor, extent)


def return_kernel(
    y, out, total, recv, gram_a, gram_b, a2a_send, a2a_recv, a_send, a_recv, b_send, b_recv, here,
):
    gx, gy, gz = position()
    mine = 4 * gx + gy
    own = pltpu.make_async_copy(y.at[mine], recv.at[mine], here.at[0])
    own.start()
    greet()
    pl.semaphore_wait(pltpu.get_barrier_semaphore(), 22)

    def a2a(o):
        peer = plane_peer(o)
        return remote(
            y.at[4 * peer[0] + peer[1]], recv.at[mine], a2a_send.at[o], a2a_recv.at[o], peer
        )

    def send(o, _):
        a2a(o).start()
        return 0

    lax.fori_loop(1, 16, send, 0)

    def place(source):
        out[pl.ds(pl.multiple_of(128 * source, 128), 128), :] = recv[source].T

    own.wait()
    place(mine)

    def receive(o, _):
        a2a(o).wait()
        place(plane_source(o))
        return 0

    lax.fori_loop(1, 16, receive, 0)

    def gram(c, acc):
        cells = jnp.concatenate([out[pl.ds(8 * c + i, 32, stride=64), :] for i in range(8)], axis=1)
        top = cells.astype(BF16)
        rest = (cells - top.astype(F32)).astype(BF16)
        both = jnp.concatenate([top, rest], axis=0)
        return acc + lax.dot_general(both, both, (((1,), (1,)), ((), ())), preferred_element_type=F32)

    acc = lax.fori_loop(0, 8, gram, jnp.zeros((64, 64), F32))
    g = acc[:32, :32] + (acc[:32, 32:] + acc[32:, :32])
    gram_a[mine] = jnp.concatenate([g[8 * b : 8 * b + 8] for b in range(4)], axis=1)

    def plane(o):
        return remote(gram_a.at[mine], gram_a.at[mine], a_send.at[o], a_recv.at[o], plane_peer(o))

    def line(o):
        return remote(gram_b.at[gz], gram_b.at[gz], b_send.at[o], b_recv.at[o], line_peer(o))

    def start_plane(o, _):
        plane(o).start()
        return 0

    def wait_plane(o, _):
        plane(o).wait()
        return 0

    def start_line(o, _):
        line(o).start()
        return 0

    def wait_line(o, _):
        line(o).wait()
        return 0

    lax.fori_loop(1, 16, start_plane, 0)
    lax.fori_loop(1, 16, wait_plane, 0)
    acc = gram_a[0]
    for i in range(1, 16):
        acc = acc + gram_a[i]
    gram_b[gz] = acc
    lax.fori_loop(1, 8, start_line, 0)
    lax.fori_loop(1, 8, wait_line, 0)
    acc = gram_b[0]
    for i in range(1, 8):
        acc = acc + gram_b[i]
    acc = acc * (1.0 / (32 * 32 * 1024))
    for b in range(4):
        total[pl.ds(8 * b, 8), :] = acc[:, 32 * b : 32 * b + 32]


def run_return(y):
    vmem = pl.BlockSpec(memory_space=pltpu.VMEM)
    dma = pltpu.SemaphoreType.DMA
    return pl.pallas_call(
        return_kernel,
        out_shape=(jax.ShapeDtypeStruct((2048, 128), F32), jax.ShapeDtypeStruct((32, 32), F32)),
        in_specs=[pl.BlockSpec(memory_space=pltpu.HBM)],
        out_specs=(vmem, vmem),
        scratch_shapes=[
            pltpu.VMEM((G, 128, 128), F32),
            pltpu.VMEM((G, 8, 128), F32),
            pltpu.VMEM((8, 8, 128), F32),
            dma((16,)), dma((16,)), dma((16,)), dma((16,)), dma((8,)), dma((8,)), dma((1,)),
        ],
        compiler_params=pltpu.CompilerParams(collective_id=2, has_side_effects=True),
        name="giveback",
    )(y)


def body(orbitals, potential, projectors, owner_rank, box_anchor, box_extent, coupling):
    perm = jnp.asarray(permutation()).astype(BF16)
    x, v, p, table = run_gather(
        orbitals.reshape(2048, 128), potential.reshape(64, 128), projectors, perm,
        owner_rank.reshape(8, 128), box_anchor, box_extent.reshape(8, 128),
    )
    w = jnp.asarray(weights()).astype(BF16)
    y = run_filter(
        table, coupling.T,
        x, v.reshape(G, 96, 128), p.reshape(1024, 16, 128), w,
    )
    filtered, total = run_return(y)
    return filtered.reshape(orbitals.shape), total


def solution(mesh):
    return jax.shard_map(
        body,
        mesh=mesh,
        in_specs=(
            P(None, "gx", "gy", "gz"),
            P("gx", "gy", "gz"),
            P(("gx", "gy", "gz"), None, None),
            P(),
            P(),
            P(),
            P(),
        ),
        out_specs=(P(None, "gx", "gy", "gz"), P()),
        check_vma=False,
    )
```

```python
import functools

import jax
import jax.numpy as jnp
import numpy as np
from jax import lax
from jax.experimental import pallas as pl
from jax.experimental.pallas import tpu as pltpu
from jax.sharding import PartitionSpec as P

B = 8
DEGREE = 4
STENCIL = (
    -5369.0 / 1800.0,
    12.0 / 7.0,
    -15.0 / 56.0,
    10.0 / 189.0,
    -1.0 / 112.0,
    2.0 / 1925.0,
    -1.0 / 16632.0,
)
SPACING = 0.5
LOW_EDGE = -2.5
CUTOFF = 4.0
UPPER = 60.0
HALF = (UPPER - CUTOFF) / 2.0
MIDDLE = (UPPER + CUTOFF) / 2.0

G = 16
PAD = 40
ROWS = 208
HALO = 32
MARGIN = 27
RANGES = ((16, 176), (24, 160), (32, 144), (40, 128))
WSCALE = 35.0 / 32.0
KIN = -0.5 / (SPACING * SPACING)
DIAG = KIN * 3.0 * STENCIL[0] - MIDDLE
GROUP = 16
SLOTS = 1024 + 2 * GROUP
F32 = jnp.float32
BF16 = jnp.bfloat16


def steps():
    sigma_one = HALF / (LOW_EDGE - MIDDLE)
    sigma = sigma_one
    out = [(sigma_one / HALF, 0.0)]
    for _ in range(1, DEGREE):
        nxt = 1.0 / (2.0 / sigma_one - sigma)
        out.append((2.0 * nxt / HALF, sigma * nxt))
        sigma = nxt
    return out


def weights():
    c = np.asarray(STENCIL, np.float64) * WSCALE

    def coef(m):
        m = abs(m)
        return c[m] if 1 <= m <= 6 else 0.0

    eye = np.eye(8)
    band = {s: np.array([[coef(8 * s + a - b) for b in range(8)] for a in range(8)]) for s in (-1, 0, 1)}
    two = np.eye(2)
    centre = np.kron(two, np.kron(band[0], eye) + np.kron(eye, band[0]))
    ym, yp = (np.kron(two, np.kron(eye, band[s])) for s in (-1, 1))
    xm, xp = (np.kron(two, np.kron(band[s], eye)) for s in (-1, 1))
    zero = np.zeros_like(centre)
    own = np.block([[centre, zero], [zero, centre]])
    across_x = np.block([[xp, xm], [xm, xp]])
    across_y = np.block([[yp, ym], [ym, yp]])
    both = [np.concatenate([own, across_x]), across_y]
    return np.concatenate([both[0], both[0], both[1], both[1]], axis=0).astype(np.float32)


def filter_kernel(
    table, coupling,
    x_ref, vp_ref, p_hbm, w_ref, o_ref,
    p_ref, v_ref, bufa, bufb, hi, lo, acc_x, acc_y, pm, gains, prods, load_sem,
):
    lane = lax.broadcasted_iota(jnp.int32, (8, 128), 1)
    sub = lax.broadcasted_iota(jnp.int32, (8, 128), 0)
    first_half = lane < 64
    upper = sub < 4
    low = sub % 4
    reach = jnp.maximum(jnp.maximum((lane % 64) // 8, lane % 8), sub)
    n_own, n_all = table[15, 0], table[15, 1]

    load = pltpu.make_async_copy(p_hbm, p_ref, load_sem)
    load.start()

    def place(group):
        per_row = 128 // GROUP
        return group // per_row, GROUP * lax.rem(group, per_row)

    def prepare(group, _):
        row, at = place(group)
        fours = []
        for q in range(GROUP):
            slot = GROUP * group + q
            ident = jnp.maximum(table[row, at + q] - 1, 0)
            keep = reach < table[48 + row, at + q]
            g = [coupling[k, ident] for k in range(4)]
            lines = []
            for p in range(2):
                value = jnp.where(keep, p_ref[ident, pl.ds(8 * p, 8), :], 0.0)
                pm[slot, pl.ds(16 * p, 8), :] = value
                pm[slot, pl.ds(16 * p + 8, 8), :] = pltpu.roll(value, 64, 1)
                lines += [jnp.where(first_half, g[2 * p], g[2 * p + 1]), jnp.where(first_half, g[2 * p + 1], g[2 * p])]
            even, odd = jnp.where(low < 2, lines[0], lines[2]), jnp.where(low < 2, lines[1], lines[3])
            fours.append(jnp.where(low % 2 == 0, even, odd))
        for t in range(GROUP // 2):
            gains[pl.ds(pl.multiple_of(4 * GROUP * group, 64) + 8 * t, 8), :] = jnp.where(
                upper, fours[2 * t], fours[2 * t + 1]
            )
        return 0

    def unpack(d, _):
        for r in range(0, 96, 8):
            pair = vp_ref[d, pl.ds(r, 8), :]
            swapped = pltpu.roll(pair, 64, 1)
            v_ref[d, pl.ds(8 + 2 * r, 8, stride=2), :] = jnp.where(first_half, pair, swapped) + DIAG
            v_ref[d, pl.ds(9 + 2 * r, 8, stride=2), :] = jnp.where(first_half, swapped, pair) + DIAG
        return 0

    lax.fori_loop(0, G, unpack, 0)

    def apply(now, old, new, offset, base, rows, alpha, beta, count):
        def split(d, _):
            for r in range(0, rows, 16):
                v = now[d, pl.ds(base + r, 16), :]
                top = v.astype(BF16)
                hi[d, pl.ds(r, 16), :] = top
                lo[d, pl.ds(r, 16), :] = (v - top.astype(F32)).astype(BF16)
            return 0

        lax.fori_loop(0, G, split, 0)

        def multiply(it):
            px, py = it // 2, it % 2

            def dom(kx, ky):
                return 4 * lax.rem(px + kx, 4) + lax.rem(py + ky, 4)

            def pair(part, a, b):
                return jnp.concatenate([part[a, pl.ds(0, rows), :], part[b, pl.ds(0, rows), :]], axis=1)

            def stack(cases):
                return jnp.concatenate(
                    [jnp.concatenate([pair(part, *c) for part in (hi, lo) for c in case], axis=1) for case in cases],
                    axis=0,
                )

            lhs_x = stack([((dom(0, k), dom(2, k)), (dom(1, k), dom(3, k))) for k in (0, 2)])
            lhs_y = stack([((dom(k, 1), dom(k, 3)),) for k in (0, 2)])
            acc_x[pl.ds(0, 2 * rows), :] = jnp.dot(lhs_x, w_ref[pl.ds(0, 1024), :], preferred_element_type=F32)
            acc_y[pl.ds(0, 2 * rows), :] = jnp.dot(lhs_y, w_ref[pl.ds(1024, 512), :], preferred_element_type=F32)

        def finish(it):
            px, py = it // 2, it % 2
            for kx in range(2):
                for ky in range(2):
                    d = 4 * (px + 2 * kx) + py + 2 * ky
                    for r in range(0, rows, 8):
                        s = base + r
                        mid = now[d, pl.ds(s, 8), :]
                        val = acc_x[pl.ds(rows * ky + r, 8), pl.ds(128 * kx, 128)]
                        val = val + acc_y[pl.ds(rows * kx + r, 8), pl.ds(128 * ky, 128)]
                        val = val * (alpha * KIN / WSCALE)
                        val = val + (alpha * v_ref[d, pl.ds(s, 8), :]) * mid
                        for m in range(1, 7):
                            val = val + (alpha * KIN * STENCIL[m]) * (
                                now[d, pl.ds(s + m, 8), :] + now[d, pl.ds(s - m, 8), :]
                            )
                        if beta:
                            val = val - beta * old[d, pl.ds(s, 8), :]
                        new[d, pl.ds(s - offset, 8), :] = val

        def both_parts(it, _):
            finish(it)
            multiply(it + 1)
            return 0

        multiply(0)
        lax.fori_loop(0, 3, both_parts, 0)
        finish(3)

        if old is None:
            load.wait()
            lax.fori_loop(0, n_all // GROUP, prepare, 0)

        def project(group):
            row, at = place(group)
            for q in range(GROUP):
                box = now[table[16 + row, at + q], pl.ds(table[32 + row, at + q], 8), :]
                for i in range(4):
                    prods[pl.ds(32 * q + 8 * i, 8), :] = pm[GROUP * group + q, pl.ds(8 * i, 8), :] * box
            out = []
            for t in range(GROUP // 2):
                v = [prods[pl.ds(64 * t + i, 8, stride=8), :] for i in range(8)]
                while len(v) > 1:
                    v = [v[i] + v[i + 1] for i in range(0, len(v), 2)]
                out.append(v[0])
            return tuple(out)

        def weigh(group, sums):
            out = []
            for t in range(GROUP // 2):
                v = sums[t]
                one = jnp.sum(jnp.where(first_half, v, 0.0), axis=1, keepdims=True)
                two = jnp.sum(jnp.where(first_half, 0.0, v), axis=1, keepdims=True)
                gain = gains[pl.ds(pl.multiple_of(4 * GROUP * group, 64) + 8 * t, 8), :]
                out.append(alpha * gain * jnp.where(first_half, one, two))
            return tuple(out)

        def spread(group, coef):
            row, at = place(group)
            adds = []
            for q in range(GROUP):
                terms = []
                for i in range(4):
                    k = 4 * (q % 2) + i
                    piece = jnp.broadcast_to(coef[q // 2][k : k + 1, :], (8, 128))
                    terms.append(pm[GROUP * group + q, pl.ds(8 * i, 8), :] * piece)
                adds.append((terms[0] + terms[1]) + (terms[2] + terms[3]))
            for q in range(GROUP):
                d, r = table[16 + row, at + q], table[32 + row, at + q] - offset
                new[d, pl.ds(r, 8), :] = new[d, pl.ds(r, 8), :] + adds[q]

        groups = count // GROUP

        def stages(group, carry):
            sums, coef = carry
            nxt = project(group)
            spread(jnp.maximum(group - 2, 0), coef)
            return nxt, weigh(group - 1, sums)

        @pl.when(groups > 0)
        def _():
            none = tuple(jnp.zeros((8, 128), F32) for _ in range(GROUP // 2))
            sums, coef = lax.fori_loop(1, groups, stages, (project(0), none))
            spread(jnp.maximum(groups - 2, 0), coef)
            spread(groups - 1, weigh(groups - 1, sums))

    plan = steps()
    chain = ((x_ref, None, bufb, 0, n_all), (bufb, x_ref, bufa, 0, n_all),
             (bufa, bufb, bufb, 0, n_all), (bufb, bufa, o_ref, PAD, n_own))
    for (now, old, new, offset, count), (base, rows), (alpha, beta) in zip(chain, RANGES, plan):
        apply(now, old, new, offset, base, rows, alpha, beta, count)


def run_filter(table, coupling, x, v, p, w):
    smem = pl.BlockSpec(memory_space=pltpu.SMEM)
    vmem = pl.BlockSpec(memory_space=pltpu.VMEM)
    return pl.pallas_call(
        filter_kernel,
        out_shape=jax.ShapeDtypeStruct((G, 128, 128), F32),
        in_specs=[smem] * 2 + [vmem] * 2 + [pl.BlockSpec(memory_space=pltpu.HBM), vmem],
        out_specs=vmem,
        scratch_shapes=[
            pltpu.VMEM((1024, 16, 128), F32),
            pltpu.VMEM((G, ROWS, 128), F32),
            pltpu.VMEM((G, ROWS, 128), F32),
            pltpu.VMEM((G, ROWS, 128), F32),
            pltpu.VMEM((G, RANGES[0][1], 128), BF16),
            pltpu.VMEM((G, RANGES[0][1], 128), BF16),
            pltpu.VMEM((2 * RANGES[0][1], 256), F32),
            pltpu.VMEM((2 * RANGES[0][1], 256), F32),
            pltpu.VMEM((SLOTS, 32, 128), F32),
            pltpu.VMEM((4 * SLOTS, 128), F32),
            pltpu.VMEM((32 * GROUP, 128), F32),
            pltpu.SemaphoreType.DMA,
        ],
        compiler_params=pltpu.CompilerParams(vmem_limit_bytes=56 * 2**20),
        name="chebyshev",
    )(table, coupling, x, v, p, w)


MESH = pl.DeviceIdType.MESH
PARTS = ((0, 24, 16, (0, 1, 2)), (24, 24, 16, (1, 0, 2)), (48, 40, 24, (1, 2, 0)), (88, 40, 24, (0, 2, 1)))
FAR_FIRST = (10, 6, 9, 11, 14, 5, 7, 13, 15, 2, 8, 1, 3, 4, 12)
A2A_CUTS = (12, 16)
V_PARTS = ((0, 32, 16, (0, 1)), (32, 32, 16, (1, 0)))


def position():
    return lax.axis_index("gx"), lax.axis_index("gy"), lax.axis_index("gz")


def plane_peer(offset):
    gx, gy, gz = position()
    return (lax.rem(gx + offset // 4, 4), lax.rem(gy + offset % 4, 4), gz)


def plane_source(offset):
    gx, gy, _ = position()
    return 4 * lax.rem(gx + 4 - offset // 4, 4) + lax.rem(gy + 4 - offset % 4, 4)


def line_peer(offset):
    gx, gy, gz = position()
    return (gx, gy, lax.rem(gz + offset, 8))


def greet():
    sem = pltpu.get_barrier_semaphore()

    def plane(o, _):
        pl.semaphore_signal(sem, inc=1, device_id=plane_peer(o), device_id_type=MESH)
        return 0

    def line(o, _):
        pl.semaphore_signal(sem, inc=1, device_id=line_peer(o), device_id_type=MESH)
        return 0

    lax.fori_loop(1, 16, plane, 0)
    lax.fori_loop(1, 8, line, 0)


def remote(src, dst, send, recv, target):
    return pltpu.make_async_remote_copy(
        src_ref=src, dst_ref=dst, send_sem=send, recv_sem=recv, device_id=target, device_id_type=MESH
    )


def pack(orb, pot, proj, perm, sent, vown, pown, cells, pair):
    first_half = lax.broadcasted_iota(jnp.int32, (16, 128), 1) < 64
    for q in range(G):
        sent[q] = orb[pl.ds(128 * q, 128), :].T
    pair[...] = pot[...].T
    vown[...] = jnp.concatenate([pair[pl.ds(0, 64, stride=2), :], pair[pl.ds(1, 64, stride=2), :]], axis=1)
    x = jnp.concatenate([proj[a] for a in range(8)], axis=0)
    top = x.astype(BF16)
    rest = x - top.astype(F32)
    mid = rest.astype(BF16)
    low = (rest - mid.astype(F32)).astype(BF16)
    parts = jnp.dot(jnp.concatenate([top, mid, low], axis=0), perm[...], preferred_element_type=F32)
    moved = (parts[:32] + parts[32:64]) + parts[64:]
    for t in range(4):
        cells[t] = moved[:, 128 * t : 128 * t + 128]
    for t in range(4):
        even, odd = cells[t, pl.ds(0, 16, stride=2), :], cells[t, pl.ds(1, 16, stride=2), :]
        pown[pl.ds(2 * t, 16, stride=8), :] = jnp.where(first_half, even, pltpu.roll(odd, 64, 1))
        pown[pl.ds(2 * t + 1, 16, stride=8), :] = jnp.where(first_half, pltpu.roll(even, 64, 1), odd)


def list_atoms(owner, anchor, extent, gz):
    rank = owner[...]
    z = jnp.concatenate([anchor[2:3, 128 * r : 128 * r + 128] for r in range(8)], axis=0)
    slab = rank % 8
    own = slab == gz
    near = ((slab == (gz + 7) % 8) & (z + MARGIN >= 128)) | ((slab == (gz + 1) % 8) & (z + B <= MARGIN))
    row = lax.broadcasted_iota(jnp.int32, (128, 128), 0)
    col = lax.broadcasted_iota(jnp.int32, (128, 128), 1)
    sub = lax.broadcasted_iota(jnp.int32, (8, 128), 0)
    before = (row < col).astype(F32)

    def ranks(mask):
        m = mask.astype(F32)
        inside = jnp.dot(m.astype(BF16), before.astype(BF16), preferred_element_type=F32)
        counts = jnp.sum(m, axis=1, keepdims=True)
        base = jnp.zeros((1, 1), F32)
        bases = []
        for r in range(8):
            bases.append(base)
            base = base + counts[r : r + 1]
        return inside + jnp.concatenate(bases, axis=0), base

    at_own, n_own = ranks(own)
    at_near, n_near = ranks(near)
    first = jnp.floor((n_own + (GROUP - 1.0)) * (1.0 / GROUP)) * GROUP
    last = first + jnp.floor((n_near + (GROUP - 1.0)) * (1.0 / GROUP)) * GROUP
    at = jnp.where(own, at_own, jnp.where(near, at_near + first, -1.0)).astype(jnp.int32)
    high = jnp.where(at >= 0, at // 128, -1)
    low = (at % 128).astype(F32).T
    ident = 128 * sub + lax.broadcasted_iota(jnp.int32, (8, 128), 1) + 1
    slot_row = lax.broadcasted_iota(jnp.int32, (16, 128), 0)
    shift = jnp.where(near, jnp.where(slab == (gz + 1) % 8, 128, -128), 0)
    fields = [ident // 32, ident % 32, rank // 8, z + shift + PAD, extent[...]]
    found = jnp.zeros((80, 128), F32)
    for r in range(8):
        hit = slot_row == high[r : r + 1]
        right = (low[:, r : r + 1] == col.astype(F32)).astype(BF16)
        left = [jnp.where(hit, f[r : r + 1].astype(F32), 0.0).astype(BF16) for f in fields]
        found = found + jnp.dot(jnp.concatenate(left, axis=0), right, preferred_element_type=F32)
    table = found[:16] * 32.0 + found[16:32]
    lane = lax.broadcasted_iota(jnp.int32, (16, 128), 1)
    start = jnp.where(table > 0.0, found[48:64], float(PAD))
    table = jnp.where(slot_row == 15, jnp.where(lane == 0, first, jnp.where(lane == 1, last, 0.0)), table)
    return jnp.concatenate([table, found[32:48], start, found[64:80]], axis=0).astype(jnp.int32)


def gather_kernel(
    orb, pot, proj, perm, owner, anchor, extent, x_out, v_out, p_out, table,
    sent, vown, pown, cells, pair,
    a2a_send, a2a_recv, p_send, p_recv, v_send, v_recv, twin_send, twin_recv, halo_send, halo_recv, here,
):
    gx, gy, gz = position()
    y, core = gz // 2, gz % 2
    mine = 4 * gx + gy
    greet()
    pack(orb, pot, proj, perm, sent, vown, pown, cells, pair)
    pl.semaphore_wait(pltpu.get_barrier_semaphore(), 22)
    local = [
        pltpu.make_async_copy(pown, p_out.at[gx, gy, y, core], here.at[0]),
        pltpu.make_async_copy(vown, v_out.at[gx, gy, pl.ds(16, 64)], here.at[1]),
        pltpu.make_async_copy(sent.at[mine], x_out.at[mine, pl.ds(PAD, 128)], here.at[2]),
    ]
    for copy in local:
        copy.start()
    where = (gx, gy, y)

    def near(dim, step):
        return lax.rem(where[dim] + step + 4, 4)

    def neighbour(dim, step):
        at = list(where)
        at[dim] = near(dim, step)
        return (at[0], at[1], 2 * at[2] + core)

    def p_view(part, at2, at3, rows, at1=None):
        start, _, _, (d1, d2, d3) = PARTS[part]
        idx = [None, None, None]
        idx[d1] = pl.ds(0, 4) if at1 is None else at1
        idx[d2] = at2
        idx[d3] = at3
        return p_out.at[idx[0], idx[1], idx[2], core, pl.ds(start + rows[0], rows[1])]

    def v_view(held, dim, at, start, rows):
        idx = [pl.ds(0, 4) if k in held else where[k] for k in range(2)]
        idx[dim] = at
        return v_out.at[idx[0], idx[1], pl.ds(16 + start, rows)]

    used = [0] * len(PARTS)

    def p_copy(part, src, dim, step, dst=None):
        k = used[part]
        used[part] += 1
        return remote(src, src if dst is None else dst, p_send.at[part, k], p_recv.at[part, k], neighbour(dim, step))

    partner = (gx, gy, gz + 1 - 2 * core)
    twins = []

    def twin(part, at2, at3):
        k = sum(1 for t in twins if t[0] == part)
        src = p_view(part, at2, at3, (0, PARTS[part][1]))
        copy = remote(src, src, twin_send.at[part, k], twin_recv.at[part, k], partner)
        copy.start()
        twins.append((part, copy))

    def start(copies):
        for copy in copies:
            copy.start()
        return copies

    def wait(copies):
        for copy in copies:
            copy.wait()

    def a2a(o):
        peer = plane_peer(o)
        return remote(
            sent.at[4 * peer[0] + peer[1]], x_out.at[mine, pl.ds(PAD, 128)], a2a_send.at[o], a2a_recv.at[o], peer
        )

    def send_a2a(lo_o, hi_o):
        def step(o, _):
            a2a(o).start()
            return 0

        lax.fori_loop(lo_o, hi_o, step, 0)

    def v_copies(phase):
        out = []
        for i, (at, rows, half, order) in enumerate(V_PARTS):
            dim, held = order[phase], order[:phase]
            dst = v_view(held, dim, where[dim], at, rows)
            src = dst if phase else vown.at[pl.ds(at, rows)]
            for k in range(3):
                sems = (v_send.at[i, 3 * phase + k], v_recv.at[i, 3 * phase + k])
                out.append(remote(src, dst, *sems, neighbour(dim, k + 1)))
        return out

    def along3(part, at2):
        d3 = PARTS[part][3][2]
        src = p_view(part, at2, where[d3], (0, PARTS[part][1]))
        return [p_copy(part, src, d3, 1), p_copy(part, src, d3, -1)]

    def forward3(part, at2):
        rows, half, d3 = PARTS[part][1], PARTS[part][2], PARTS[part][3][2]
        return [
            p_copy(part, p_view(part, at2, near(d3, -1), (0, half)), d3, 1),
            p_copy(part, p_view(part, at2, near(d3, 1), (half, rows - half)), d3, -1),
        ]

    every = range(len(PARTS))
    dims = [part[3] for part in PARTS]
    right, left = line_peer(1), line_peer(7)
    whole = pl.ds(0, 4)
    first = []
    for i in every:
        d1, d2, d3 = dims[i]
        own = p_view(i, where[d2], where[d3], (0, PARTS[i][1]), where[d1])
        src = pown.at[pl.ds(PARTS[i][0], PARTS[i][1])]
        first += [p_copy(i, src, d1, k, own) for k in (1, 3, 2)]
    start(first)
    v = start(v_copies(0))
    send_a2a(1, A2A_CUTS[0])
    table[...] = list_atoms(owner, anchor, extent, gz)
    wait(local)
    wait(first)
    second, a5 = [], []
    for k in (1, 3, 2):
        for i in every:
            d1, d2, d3 = dims[i]
            second.append(p_copy(i, p_view(i, where[d2], where[d3], (0, PARTS[i][1])), d2, k))
    start(second)
    for i in every:
        a5 += start(along3(i, where[dims[i][1]]))
    wait(v)
    v = start(v_copies(1))
    send_a2a(A2A_CUTS[0], A2A_CUTS[1])
    b5 = []
    at = 0
    for k in (1, 3, 2):
        for i in every:
            wait(second[at : at + 1])
            at += 1
            b5 += start(along3(i, near(dims[i][1], -k)))
    for i in every:
        twin(i, whole, where[dims[i][2]])
    wait(v)
    halos = start([
        remote(v_out.at[whole, whole, pl.ds(64, 16)], v_out.at[whole, whole, pl.ds(0, 16)],
               halo_send.at[2], halo_recv.at[2], right),
        remote(v_out.at[whole, whole, pl.ds(16, 16)], v_out.at[whole, whole, pl.ds(80, 16)],
               halo_send.at[3], halo_recv.at[3], left),
    ])
    wait(a5)
    last = []
    for i in every:
        last += start(forward3(i, where[dims[i][1]]))

    def finish_a2a(o, _):
        a2a(o).wait()
        return 0

    at = 0
    for k in (1, 3, 2):
        for i in every:
            wait(b5[at : at + 2])
            at += 2
            last += start(forward3(i, near(dims[i][1], -k)))
    lax.fori_loop(1, 16, finish_a2a, 0)
    halos += start([
        remote(x_out.at[pl.ds(0, G), pl.ds(PAD + 128 - HALO, HALO)], x_out.at[pl.ds(0, G), pl.ds(PAD - HALO, HALO)],
               halo_send.at[0], halo_recv.at[0], right),
        remote(x_out.at[pl.ds(0, G), pl.ds(PAD, HALO)], x_out.at[pl.ds(0, G), pl.ds(PAD + 128, HALO)],
               halo_send.at[1], halo_recv.at[1], left),
    ])
    for i in every:
        for k in (1, -1):
            twin(i, whole, near(dims[i][2], k))
    wait(last)
    for i in every:
        twin(i, whole, near(dims[i][2], 2))
    wait(halos)
    wait([copy for _, copy in twins])


def permutation():
    at = np.arange(512)
    perm = np.zeros((512, 512), np.float32)
    perm[at, (at % 8) * 64 + at // 8] = 1.0
    return perm


def run_gather(orb, pot, proj, perm, owner, anchor, extent):
    vmem = pl.BlockSpec(memory_space=pltpu.VMEM)
    hbm = pl.BlockSpec(memory_space=pltpu.HBM)
    dma = pltpu.SemaphoreType.DMA
    return pl.pallas_call(
        gather_kernel,
        out_shape=(
            jax.ShapeDtypeStruct((G, ROWS, 128), F32),
            jax.ShapeDtypeStruct((4, 4, 96, 128), F32),
            jax.ShapeDtypeStruct((4, 4, 4, 2, 128, 128), F32),
            jax.ShapeDtypeStruct((64, 128), jnp.int32),
        ),
        in_specs=[vmem] * 7,
        out_specs=(hbm, hbm, hbm, vmem),
        scratch_shapes=[
            pltpu.VMEM((G, 128, 128), F32),
            pltpu.VMEM((64, 128), F32),
            pltpu.VMEM((128, 128), F32),
            pltpu.VMEM((4, 32, 128), F32),
            pltpu.VMEM((128, 64), F32),
            dma((16,)), dma((16,)), dma((4, 22)), dma((4, 22)), dma((2, 6)), dma((2, 6)),
            dma((4, 4)), dma((4, 4)), dma((4,)), dma((4,)), dma((3,)),
        ],
        compiler_params=pltpu.CompilerParams(collective_id=1, has_side_effects=True),
        name="gather",
    )(orb, pot, proj, perm, owner, anchor, extent)


def return_kernel(
    y, out, total, recv, gram_a, gram_b, a2a_send, a2a_recv, a_send, a_recv, b_send, b_recv, here,
):
    gx, gy, gz = position()
    mine = 4 * gx + gy
    own = pltpu.make_async_copy(y.at[mine], recv.at[mine], here.at[0])
    own.start()
    greet()
    pl.semaphore_wait(pltpu.get_barrier_semaphore(), 22)

    def a2a(o):
        peer = plane_peer(o)
        return remote(
            y.at[4 * peer[0] + peer[1]], recv.at[mine], a2a_send.at[o], a2a_recv.at[o], peer
        )

    for o in FAR_FIRST:
        a2a(o).start()

    def place(source):
        out[pl.ds(pl.multiple_of(128 * source, 128), 128), :] = recv[source].T

    own.wait()
    place(mine)

    def receive(o, _):
        a2a(o).wait()
        place(plane_source(o))
        return 0

    lax.fori_loop(1, 16, receive, 0)

    def gram(c, acc):
        cells = jnp.concatenate([out[pl.ds(8 * c + i, 32, stride=64), :] for i in range(8)], axis=1)
        top = cells.astype(BF16)
        rest = (cells - top.astype(F32)).astype(BF16)
        both = jnp.concatenate([top, rest], axis=0)
        return acc + lax.dot_general(both, both, (((1,), (1,)), ((), ())), preferred_element_type=F32)

    acc = lax.fori_loop(0, 8, gram, jnp.zeros((64, 64), F32))
    g = acc[:32, :32] + (acc[:32, 32:] + acc[32:, :32])
    gram_a[mine] = jnp.concatenate([g[8 * b : 8 * b + 8] for b in range(4)], axis=1)

    def plane(o):
        return remote(gram_a.at[mine], gram_a.at[mine], a_send.at[o], a_recv.at[o], plane_peer(o))

    def line(o):
        return remote(gram_b.at[gz], gram_b.at[gz], b_send.at[o], b_recv.at[o], line_peer(o))

    def wait_plane(o, _):
        plane(o).wait()
        return 0

    def wait_line(o, _):
        line(o).wait()
        return 0

    for o in FAR_FIRST:
        plane(o).start()
    lax.fori_loop(1, 16, wait_plane, 0)
    acc = gram_a[0]
    for i in range(1, 16):
        acc = acc + gram_a[i]
    gram_b[gz] = acc
    for o in (4, 3, 5, 2, 6, 1, 7):
        line(o).start()
    lax.fori_loop(1, 8, wait_line, 0)
    acc = gram_b[0]
    for i in range(1, 8):
        acc = acc + gram_b[i]
    acc = acc * (1.0 / (32 * 32 * 1024))
    for b in range(4):
        total[pl.ds(8 * b, 8), :] = acc[:, 32 * b : 32 * b + 32]


def run_return(y):
    vmem = pl.BlockSpec(memory_space=pltpu.VMEM)
    dma = pltpu.SemaphoreType.DMA
    return pl.pallas_call(
        return_kernel,
        out_shape=(jax.ShapeDtypeStruct((2048, 128), F32), jax.ShapeDtypeStruct((32, 32), F32)),
        in_specs=[pl.BlockSpec(memory_space=pltpu.HBM)],
        out_specs=(vmem, vmem),
        scratch_shapes=[
            pltpu.VMEM((G, 128, 128), F32),
            pltpu.VMEM((G, 8, 128), F32),
            pltpu.VMEM((8, 8, 128), F32),
            dma((16,)), dma((16,)), dma((16,)), dma((16,)), dma((8,)), dma((8,)), dma((1,)),
        ],
        compiler_params=pltpu.CompilerParams(collective_id=2, has_side_effects=True),
        name="giveback",
    )(y)


def body(orbitals, potential, projectors, owner_rank, box_anchor, box_extent, coupling):
    perm = jnp.asarray(permutation()).astype(BF16)
    x, v, p, table = run_gather(
        orbitals.reshape(2048, 128), potential.reshape(64, 128), projectors, perm,
        owner_rank.reshape(8, 128), box_anchor, box_extent.reshape(8, 128),
    )
    w = jnp.asarray(weights()).astype(BF16)
    y = run_filter(
        table, coupling.T,
        x, v.reshape(G, 96, 128), p.reshape(1024, 16, 128), w,
    )
    filtered, total = run_return(y)
    return filtered.reshape(orbitals.shape), total


def solution(mesh):
    return jax.shard_map(
        body,
        mesh=mesh,
        in_specs=(
            P(None, "gx", "gy", "gz"),
            P("gx", "gy", "gz"),
            P(("gx", "gy", "gz"), None, None),
            P(),
            P(),
            P(),
            P(),
        ),
        out_specs=(P(None, "gx", "gy", "gz"), P()),
        check_vma=False,
    )
```

```python
import functools

import jax
import jax.numpy as jnp
import numpy as np
from jax import lax
from jax.experimental import pallas as pl
from jax.experimental.pallas import tpu as pltpu
from jax.sharding import PartitionSpec as P

B = 8
DEGREE = 4
STENCIL = (
    -5369.0 / 1800.0,
    12.0 / 7.0,
    -15.0 / 56.0,
    10.0 / 189.0,
    -1.0 / 112.0,
    2.0 / 1925.0,
    -1.0 / 16632.0,
)
SPACING = 0.5
LOW_EDGE = -2.5
CUTOFF = 4.0
UPPER = 60.0
HALF = (UPPER - CUTOFF) / 2.0
MIDDLE = (UPPER + CUTOFF) / 2.0

G = 16
PAD = 40
ROWS = 208
HALO = 32
MARGIN = 27
RANGES = ((16, 176), (24, 160), (32, 144), (40, 128))
WSCALE = 35.0 / 32.0
KIN = -0.5 / (SPACING * SPACING)
DIAG = KIN * 3.0 * STENCIL[0] - MIDDLE
GROUP = 16
SLOTS = 1024 + 2 * GROUP
F32 = jnp.float32
BF16 = jnp.bfloat16


def steps():
    sigma_one = HALF / (LOW_EDGE - MIDDLE)
    sigma = sigma_one
    out = [(sigma_one / HALF, 0.0)]
    for _ in range(1, DEGREE):
        nxt = 1.0 / (2.0 / sigma_one - sigma)
        out.append((2.0 * nxt / HALF, sigma * nxt))
        sigma = nxt
    return out


def weights():
    c = np.asarray(STENCIL, np.float64) * WSCALE

    def coef(m):
        m = abs(m)
        return c[m] if 1 <= m <= 6 else 0.0

    eye = np.eye(8)
    band = {s: np.array([[coef(8 * s + a - b) for b in range(8)] for a in range(8)]) for s in (-1, 0, 1)}
    two = np.eye(2)
    centre = np.kron(two, np.kron(band[0], eye) + np.kron(eye, band[0]))
    ym, yp = (np.kron(two, np.kron(eye, band[s])) for s in (-1, 1))
    xm, xp = (np.kron(two, np.kron(band[s], eye)) for s in (-1, 1))
    zero = np.zeros_like(centre)
    own = np.block([[centre, zero], [zero, centre]])
    across_x = np.block([[xp, xm], [xm, xp]])
    across_y = np.block([[yp, ym], [ym, yp]])
    both = [np.concatenate([own, across_x]), across_y]
    return np.concatenate([both[0], both[0], both[1], both[1]], axis=0).astype(np.float32)


def filter_kernel(
    table, coupling,
    x_ref, vp_ref, p_hbm, w_ref, o_ref,
    p_ref, v_ref, bufa, bufb, hi, lo, acc_x, acc_y, pm, gains, prods, load_sem,
):
    lane = lax.broadcasted_iota(jnp.int32, (8, 128), 1)
    sub = lax.broadcasted_iota(jnp.int32, (8, 128), 0)
    first_half = lane < 64
    upper = sub < 4
    low = sub % 4
    reach = jnp.maximum(jnp.maximum((lane % 64) // 8, lane % 8), sub)
    n_own, n_all = table[15, 0], table[15, 1]

    load = pltpu.make_async_copy(p_hbm, p_ref, load_sem)
    load.start()

    def place(group):
        per_row = 128 // GROUP
        return group // per_row, GROUP * lax.rem(group, per_row)

    def prepare(group, _):
        row, at = place(group)
        fours = []
        for q in range(GROUP):
            slot = GROUP * group + q
            ident = jnp.maximum(table[row, at + q] - 1, 0)
            keep = reach < table[48 + row, at + q]
            g = [coupling[k, ident] for k in range(4)]
            lines = []
            for p in range(2):
                value = jnp.where(keep, p_ref[ident, pl.ds(8 * p, 8), :], 0.0)
                pm[slot, pl.ds(16 * p, 8), :] = value
                pm[slot, pl.ds(16 * p + 8, 8), :] = pltpu.roll(value, 64, 1)
                lines += [jnp.where(first_half, g[2 * p], g[2 * p + 1]), jnp.where(first_half, g[2 * p + 1], g[2 * p])]
            even, odd = jnp.where(low < 2, lines[0], lines[2]), jnp.where(low < 2, lines[1], lines[3])
            fours.append(jnp.where(low % 2 == 0, even, odd))
        for t in range(GROUP // 2):
            gains[pl.ds(pl.multiple_of(4 * GROUP * group, 64) + 8 * t, 8), :] = jnp.where(
                upper, fours[2 * t], fours[2 * t + 1]
            )
        return 0

    def unpack(d, _):
        for r in range(0, 96, 8):
            pair = vp_ref[d, pl.ds(r, 8), :]
            swapped = pltpu.roll(pair, 64, 1)
            v_ref[d, pl.ds(8 + 2 * r, 8, stride=2), :] = jnp.where(first_half, pair, swapped) + DIAG
            v_ref[d, pl.ds(9 + 2 * r, 8, stride=2), :] = jnp.where(first_half, swapped, pair) + DIAG
        return 0

    lax.fori_loop(0, G, unpack, 0)

    def apply(now, old, new, offset, base, rows, alpha, beta, count):
        def split(d, _):
            for r in range(0, rows, 16):
                v = now[d, pl.ds(base + r, 16), :]
                top = v.astype(BF16)
                hi[d, pl.ds(r, 16), :] = top
                lo[d, pl.ds(r, 16), :] = (v - top.astype(F32)).astype(BF16)
            return 0

        lax.fori_loop(0, G, split, 0)

        def multiply(it):
            px, py = it // 2, it % 2

            def dom(kx, ky):
                return 4 * lax.rem(px + kx, 4) + lax.rem(py + ky, 4)

            def pair(part, a, b):
                return jnp.concatenate([part[a, pl.ds(0, rows), :], part[b, pl.ds(0, rows), :]], axis=1)

            def stack(cases):
                return jnp.concatenate(
                    [jnp.concatenate([pair(part, *c) for part in (hi, lo) for c in case], axis=1) for case in cases],
                    axis=0,
                )

            lhs_x = stack([((dom(0, k), dom(2, k)), (dom(1, k), dom(3, k))) for k in (0, 2)])
            lhs_y = stack([((dom(k, 1), dom(k, 3)),) for k in (0, 2)])
            acc_x[pl.ds(0, 2 * rows), :] = jnp.dot(lhs_x, w_ref[pl.ds(0, 1024), :], preferred_element_type=F32)
            acc_y[pl.ds(0, 2 * rows), :] = jnp.dot(lhs_y, w_ref[pl.ds(1024, 512), :], preferred_element_type=F32)

        def finish(it):
            px, py = it // 2, it % 2
            for kx in range(2):
                for ky in range(2):
                    d = 4 * (px + 2 * kx) + py + 2 * ky
                    for r in range(0, rows, 8):
                        s = base + r
                        mid = now[d, pl.ds(s, 8), :]
                        val = acc_x[pl.ds(rows * ky + r, 8), pl.ds(128 * kx, 128)]
                        val = val + acc_y[pl.ds(rows * kx + r, 8), pl.ds(128 * ky, 128)]
                        val = val * (alpha * KIN / WSCALE)
                        val = val + (alpha * v_ref[d, pl.ds(s, 8), :]) * mid
                        for m in range(1, 7):
                            val = val + (alpha * KIN * STENCIL[m]) * (
                                now[d, pl.ds(s + m, 8), :] + now[d, pl.ds(s - m, 8), :]
                            )
                        if beta:
                            val = val - beta * old[d, pl.ds(s, 8), :]
                        new[d, pl.ds(s - offset, 8), :] = val

        def both_parts(it, _):
            finish(it)
            multiply(it + 1)
            return 0

        multiply(0)
        lax.fori_loop(0, 3, both_parts, 0)
        finish(3)

        if old is None:
            load.wait()
            lax.fori_loop(0, n_all // GROUP, prepare, 0)

        def project(group):
            row, at = place(group)
            for q in range(GROUP):
                box = now[table[16 + row, at + q], pl.ds(table[32 + row, at + q], 8), :]
                for i in range(4):
                    prods[pl.ds(32 * q + 8 * i, 8), :] = pm[GROUP * group + q, pl.ds(8 * i, 8), :] * box
            out = []
            for t in range(GROUP // 2):
                v = [prods[pl.ds(64 * t + i, 8, stride=8), :] for i in range(8)]
                while len(v) > 1:
                    v = [v[i] + v[i + 1] for i in range(0, len(v), 2)]
                out.append(v[0])
            return tuple(out)

        def weigh(group, sums):
            out = []
            for t in range(GROUP // 2):
                v = sums[t]
                one = jnp.sum(jnp.where(first_half, v, 0.0), axis=1, keepdims=True)
                two = jnp.sum(jnp.where(first_half, 0.0, v), axis=1, keepdims=True)
                gain = gains[pl.ds(pl.multiple_of(4 * GROUP * group, 64) + 8 * t, 8), :]
                out.append(alpha * gain * jnp.where(first_half, one, two))
            return tuple(out)

        def spread(group, coef):
            row, at = place(group)
            adds = []
            for q in range(GROUP):
                terms = []
                for i in range(4):
                    k = 4 * (q % 2) + i
                    piece = jnp.broadcast_to(coef[q // 2][k : k + 1, :], (8, 128))
                    terms.append(pm[GROUP * group + q, pl.ds(8 * i, 8), :] * piece)
                adds.append((terms[0] + terms[1]) + (terms[2] + terms[3]))
            for q in range(GROUP):
                d, r = table[16 + row, at + q], table[32 + row, at + q] - offset
                new[d, pl.ds(r, 8), :] = new[d, pl.ds(r, 8), :] + adds[q]

        groups = count // GROUP

        def stages(group, carry):
            sums, coef = carry
            nxt = project(group)
            spread(jnp.maximum(group - 2, 0), coef)
            return nxt, weigh(group - 1, sums)

        @pl.when(groups > 0)
        def _():
            none = tuple(jnp.zeros((8, 128), F32) for _ in range(GROUP // 2))
            sums, coef = lax.fori_loop(1, groups, stages, (project(0), none))
            spread(jnp.maximum(groups - 2, 0), coef)
            spread(groups - 1, weigh(groups - 1, sums))

    plan = steps()
    chain = ((x_ref, None, bufb, 0, n_all), (bufb, x_ref, bufa, 0, n_all),
             (bufa, bufb, bufb, 0, n_all), (bufb, bufa, o_ref, PAD, n_own))
    for (now, old, new, offset, count), (base, rows), (alpha, beta) in zip(chain, RANGES, plan):
        apply(now, old, new, offset, base, rows, alpha, beta, count)


def run_filter(table, coupling, x, v, p, w):
    smem = pl.BlockSpec(memory_space=pltpu.SMEM)
    vmem = pl.BlockSpec(memory_space=pltpu.VMEM)
    return pl.pallas_call(
        filter_kernel,
        out_shape=jax.ShapeDtypeStruct((G, 128, 128), F32),
        in_specs=[smem] * 2 + [vmem] * 2 + [pl.BlockSpec(memory_space=pltpu.HBM), vmem],
        out_specs=vmem,
        scratch_shapes=[
            pltpu.VMEM((1024, 16, 128), F32),
            pltpu.VMEM((G, ROWS, 128), F32),
            pltpu.VMEM((G, ROWS, 128), F32),
            pltpu.VMEM((G, ROWS, 128), F32),
            pltpu.VMEM((G, RANGES[0][1], 128), BF16),
            pltpu.VMEM((G, RANGES[0][1], 128), BF16),
            pltpu.VMEM((2 * RANGES[0][1], 256), F32),
            pltpu.VMEM((2 * RANGES[0][1], 256), F32),
            pltpu.VMEM((SLOTS, 32, 128), F32),
            pltpu.VMEM((4 * SLOTS, 128), F32),
            pltpu.VMEM((32 * GROUP, 128), F32),
            pltpu.SemaphoreType.DMA,
        ],
        compiler_params=pltpu.CompilerParams(vmem_limit_bytes=56 * 2**20),
        name="chebyshev",
    )(table, coupling, x, v, p, w)


MESH = pl.DeviceIdType.MESH
PARTS = ((0, 24, 16, (0, 1, 2)), (24, 24, 16, (1, 0, 2)), (48, 40, 24, (1, 2, 0)), (88, 40, 24, (0, 2, 1)))
FAR_FIRST = (10, 6, 9, 11, 14, 5, 7, 13, 15, 2, 8, 1, 3, 4, 12)
A2A_CUTS = (12, 16)
V_PARTS = ((0, 32, 16, (0, 1)), (32, 32, 16, (1, 0)))


def position():
    return lax.axis_index("gx"), lax.axis_index("gy"), lax.axis_index("gz")


def plane_peer(offset):
    gx, gy, gz = position()
    return (lax.rem(gx + offset // 4, 4), lax.rem(gy + offset % 4, 4), gz)


def plane_source(offset):
    gx, gy, _ = position()
    return 4 * lax.rem(gx + 4 - offset // 4, 4) + lax.rem(gy + 4 - offset % 4, 4)


def line_peer(offset):
    gx, gy, gz = position()
    return (gx, gy, lax.rem(gz + offset, 8))


def greet():
    sem = pltpu.get_barrier_semaphore()

    def plane(o, _):
        pl.semaphore_signal(sem, inc=1, device_id=plane_peer(o), device_id_type=MESH)
        return 0

    def line(o, _):
        pl.semaphore_signal(sem, inc=1, device_id=line_peer(o), device_id_type=MESH)
        return 0

    lax.fori_loop(1, 16, plane, 0)
    lax.fori_loop(1, 8, line, 0)


def remote(src, dst, send, recv, target):
    return pltpu.make_async_remote_copy(
        src_ref=src, dst_ref=dst, send_sem=send, recv_sem=recv, device_id=target, device_id_type=MESH
    )


def pack(orb, pot, proj, perm, sent, vown, pown, cells, pair):
    first_half = lax.broadcasted_iota(jnp.int32, (16, 128), 1) < 64
    for q in range(G):
        sent[q] = orb[pl.ds(128 * q, 128), :].T
    pair[...] = pot[...].T
    vown[...] = jnp.concatenate([pair[pl.ds(0, 64, stride=2), :], pair[pl.ds(1, 64, stride=2), :]], axis=1)
    x = jnp.concatenate([proj[a] for a in range(8)], axis=0)
    top = x.astype(BF16)
    rest = x - top.astype(F32)
    mid = rest.astype(BF16)
    low = (rest - mid.astype(F32)).astype(BF16)
    parts = jnp.dot(jnp.concatenate([top, mid, low], axis=0), perm[...], preferred_element_type=F32)
    moved = (parts[:32] + parts[32:64]) + parts[64:]
    for t in range(4):
        cells[t] = moved[:, 128 * t : 128 * t + 128]
    for t in range(4):
        even, odd = cells[t, pl.ds(0, 16, stride=2), :], cells[t, pl.ds(1, 16, stride=2), :]
        pown[pl.ds(2 * t, 16, stride=8), :] = jnp.where(first_half, even, pltpu.roll(odd, 64, 1))
        pown[pl.ds(2 * t + 1, 16, stride=8), :] = jnp.where(first_half, pltpu.roll(even, 64, 1), odd)


def list_atoms(owner, anchor, extent, gz):
    rank = owner[...]
    z = jnp.concatenate([anchor[2:3, 128 * r : 128 * r + 128] for r in range(8)], axis=0)
    slab = rank % 8
    own = slab == gz
    near = ((slab == (gz + 7) % 8) & (z + MARGIN >= 128)) | ((slab == (gz + 1) % 8) & (z + B <= MARGIN))
    row = lax.broadcasted_iota(jnp.int32, (128, 128), 0)
    col = lax.broadcasted_iota(jnp.int32, (128, 128), 1)
    sub = lax.broadcasted_iota(jnp.int32, (8, 128), 0)
    before = (row < col).astype(F32)

    def ranks(mask):
        m = mask.astype(F32)
        inside = jnp.dot(m.astype(BF16), before.astype(BF16), preferred_element_type=F32)
        counts = jnp.sum(m, axis=1, keepdims=True)
        base = jnp.zeros((1, 1), F32)
        bases = []
        for r in range(8):
            bases.append(base)
            base = base + counts[r : r + 1]
        return inside + jnp.concatenate(bases, axis=0), base

    at_own, n_own = ranks(own)
    at_near, n_near = ranks(near)
    first = jnp.floor((n_own + (GROUP - 1.0)) * (1.0 / GROUP)) * GROUP
    last = first + jnp.floor((n_near + (GROUP - 1.0)) * (1.0 / GROUP)) * GROUP
    at = jnp.where(own, at_own, jnp.where(near, at_near + first, -1.0)).astype(jnp.int32)
    high = jnp.where(at >= 0, at // 128, -1)
    low = (at % 128).astype(F32).T
    ident = 128 * sub + lax.broadcasted_iota(jnp.int32, (8, 128), 1) + 1
    slot_row = lax.broadcasted_iota(jnp.int32, (16, 128), 0)
    shift = jnp.where(near, jnp.where(slab == (gz + 1) % 8, 128, -128), 0)
    fields = [ident // 32, ident % 32, rank // 8, z + shift + PAD, extent[...]]
    found = jnp.zeros((80, 128), F32)
    for r in range(8):
        hit = slot_row == high[r : r + 1]
        right = (low[:, r : r + 1] == col.astype(F32)).astype(BF16)
        left = [jnp.where(hit, f[r : r + 1].astype(F32), 0.0).astype(BF16) for f in fields]
        found = found + jnp.dot(jnp.concatenate(left, axis=0), right, preferred_element_type=F32)
    table = found[:16] * 32.0 + found[16:32]
    lane = lax.broadcasted_iota(jnp.int32, (16, 128), 1)
    start = jnp.where(table > 0.0, found[48:64], float(PAD))
    table = jnp.where(slot_row == 15, jnp.where(lane == 0, first, jnp.where(lane == 1, last, 0.0)), table)
    return jnp.concatenate([table, found[32:48], start, found[64:80]], axis=0).astype(jnp.int32)


def gather_kernel(
    orb, pot, proj, perm, owner, anchor, extent, x_out, v_out, p_out, table,
    sent, vown, pown, cells, pair,
    a2a_send, a2a_recv, p_send, p_recv, v_send, v_recv, twin_send, twin_recv, halo_send, halo_recv, here,
):
    gx, gy, gz = position()
    y, core = gz // 2, gz % 2
    mine = 4 * gx + gy
    greet()
    pack(orb, pot, proj, perm, sent, vown, pown, cells, pair)
    pl.semaphore_wait(pltpu.get_barrier_semaphore(), 22)
    local = [
        pltpu.make_async_copy(pown, p_out.at[gx, gy, y, core], here.at[0]),
        pltpu.make_async_copy(vown, v_out.at[gx, gy, pl.ds(16, 64)], here.at[1]),
        pltpu.make_async_copy(sent.at[mine], x_out.at[mine, pl.ds(PAD, 128)], here.at[2]),
    ]
    for copy in local:
        copy.start()
    where = (gx, gy, y)

    def near(dim, step):
        return lax.rem(where[dim] + step + 4, 4)

    def neighbour(dim, step):
        at = list(where)
        at[dim] = near(dim, step)
        return (at[0], at[1], 2 * at[2] + core)

    def p_view(part, at2, at3, rows, at1=None):
        start, _, _, (d1, d2, d3) = PARTS[part]
        idx = [None, None, None]
        idx[d1] = pl.ds(0, 4) if at1 is None else at1
        idx[d2] = at2
        idx[d3] = at3
        return p_out.at[idx[0], idx[1], idx[2], core, pl.ds(start + rows[0], rows[1])]

    def v_view(held, dim, at, start, rows):
        idx = [pl.ds(0, 4) if k in held else where[k] for k in range(2)]
        idx[dim] = at
        return v_out.at[idx[0], idx[1], pl.ds(16 + start, rows)]

    used = [0] * len(PARTS)

    def p_copy(part, src, dim, step, dst=None):
        k = used[part]
        used[part] += 1
        return remote(src, src if dst is None else dst, p_send.at[part, k], p_recv.at[part, k], neighbour(dim, step))

    partner = (gx, gy, gz + 1 - 2 * core)
    twins = []

    def twin(part, at2, at3):
        k = sum(1 for t in twins if t[0] == part)
        src = p_view(part, at2, at3, (0, PARTS[part][1]))
        copy = remote(src, src, twin_send.at[part, k], twin_recv.at[part, k], partner)
        copy.start()
        twins.append((part, copy))

    def start(copies):
        for copy in copies:
            copy.start()
        return copies

    def wait(copies):
        for copy in copies:
            copy.wait()

    def a2a(o):
        peer = plane_peer(o)
        return remote(
            sent.at[4 * peer[0] + peer[1]], x_out.at[mine, pl.ds(PAD, 128)], a2a_send.at[o], a2a_recv.at[o], peer
        )

    def send_a2a(lo_o, hi_o):
        def step(o, _):
            a2a(o).start()
            return 0

        lax.fori_loop(lo_o, hi_o, step, 0)

    def v_copies(phase):
        out = []
        for i, (at, rows, half, order) in enumerate(V_PARTS):
            dim, held = order[phase], order[:phase]
            dst = v_view(held, dim, where[dim], at, rows)
            src = dst if phase else vown.at[pl.ds(at, rows)]
            for k in range(3):
                sems = (v_send.at[i, 3 * phase + k], v_recv.at[i, 3 * phase + k])
                out.append(remote(src, dst, *sems, neighbour(dim, k + 1)))
        return out

    def along3(part, at2):
        d3 = PARTS[part][3][2]
        src = p_view(part, at2, where[d3], (0, PARTS[part][1]))
        return [p_copy(part, src, d3, 1), p_copy(part, src, d3, -1)]

    def forward3(part, at2):
        rows, half, d3 = PARTS[part][1], PARTS[part][2], PARTS[part][3][2]
        return [
            p_copy(part, p_view(part, at2, near(d3, -1), (0, half)), d3, 1),
            p_copy(part, p_view(part, at2, near(d3, 1), (half, rows - half)), d3, -1),
        ]

    every = range(len(PARTS))
    dims = [part[3] for part in PARTS]
    right, left = line_peer(1), line_peer(7)
    whole = pl.ds(0, 4)
    first = []
    for i in every:
        d1, d2, d3 = dims[i]
        own = p_view(i, where[d2], where[d3], (0, PARTS[i][1]), where[d1])
        src = pown.at[pl.ds(PARTS[i][0], PARTS[i][1])]
        first += [p_copy(i, src, d1, k, own) for k in (1, 3, 2)]
    start(first)
    v = start(v_copies(0))
    send_a2a(1, A2A_CUTS[0])
    table[...] = list_atoms(owner, anchor, extent, gz)
    wait(local)
    wait(first)
    second, a5 = [], []
    for k in (1, 3, 2):
        for i in every:
            d1, d2, d3 = dims[i]
            second.append(p_copy(i, p_view(i, where[d2], where[d3], (0, PARTS[i][1])), d2, k))
    start(second)
    for i in every:
        a5 += start(along3(i, where[dims[i][1]]))
    wait(v)
    v = start(v_copies(1))
    send_a2a(A2A_CUTS[0], A2A_CUTS[1])
    b5 = []
    at = 0
    for k in (1, 3, 2):
        for i in every:
            wait(second[at : at + 1])
            at += 1
            b5 += start(along3(i, near(dims[i][1], -k)))
    for i in every:
        twin(i, whole, where[dims[i][2]])
    wait(v)
    halos = start([
        remote(v_out.at[whole, whole, pl.ds(64, 16)], v_out.at[whole, whole, pl.ds(0, 16)],
               halo_send.at[2], halo_recv.at[2], right),
        remote(v_out.at[whole, whole, pl.ds(16, 16)], v_out.at[whole, whole, pl.ds(80, 16)],
               halo_send.at[3], halo_recv.at[3], left),
    ])
    wait(a5)
    last = []
    for i in every:
        last += start(forward3(i, where[dims[i][1]]))

    def finish_a2a(o, _):
        a2a(o).wait()
        return 0

    at = 0
    for k in (1, 3, 2):
        for i in every:
            wait(b5[at : at + 2])
            at += 2
            last += start(forward3(i, near(dims[i][1], -k)))
    lax.fori_loop(1, 16, finish_a2a, 0)
    halos += start([
        remote(x_out.at[pl.ds(0, G), pl.ds(PAD + 128 - HALO, HALO)], x_out.at[pl.ds(0, G), pl.ds(PAD - HALO, HALO)],
               halo_send.at[0], halo_recv.at[0], right),
        remote(x_out.at[pl.ds(0, G), pl.ds(PAD, HALO)], x_out.at[pl.ds(0, G), pl.ds(PAD + 128, HALO)],
               halo_send.at[1], halo_recv.at[1], left),
    ])
    for i in every:
        for k in (1, -1):
            twin(i, whole, near(dims[i][2], k))
    wait(last)
    for i in every:
        twin(i, whole, near(dims[i][2], 2))
    wait(halos)
    wait([copy for _, copy in twins])


def permutation():
    at = np.arange(512)
    perm = np.zeros((512, 512), np.float32)
    perm[at, (at % 8) * 64 + at // 8] = 1.0
    return perm


def run_gather(orb, pot, proj, perm, owner, anchor, extent):
    vmem = pl.BlockSpec(memory_space=pltpu.VMEM)
    hbm = pl.BlockSpec(memory_space=pltpu.HBM)
    dma = pltpu.SemaphoreType.DMA
    return pl.pallas_call(
        gather_kernel,
        out_shape=(
            jax.ShapeDtypeStruct((G, ROWS, 128), F32),
            jax.ShapeDtypeStruct((4, 4, 96, 128), F32),
            jax.ShapeDtypeStruct((4, 4, 4, 2, 128, 128), F32),
            jax.ShapeDtypeStruct((64, 128), jnp.int32),
        ),
        in_specs=[vmem] * 7,
        out_specs=(hbm, hbm, hbm, vmem),
        scratch_shapes=[
            pltpu.VMEM((G, 128, 128), F32),
            pltpu.VMEM((64, 128), F32),
            pltpu.VMEM((128, 128), F32),
            pltpu.VMEM((4, 32, 128), F32),
            pltpu.VMEM((128, 64), F32),
            dma((16,)), dma((16,)), dma((4, 22)), dma((4, 22)), dma((2, 6)), dma((2, 6)),
            dma((4, 4)), dma((4, 4)), dma((4,)), dma((4,)), dma((3,)),
        ],
        compiler_params=pltpu.CompilerParams(collective_id=1, has_side_effects=True),
        name="gather",
    )(orb, pot, proj, perm, owner, anchor, extent)


def return_kernel(
    y, out, total, recv, gram_a, gram_b, a2a_send, a2a_recv, a_send, a_recv, b_send, b_recv, here,
):
    gx, gy, gz = position()
    mine = 4 * gx + gy
    own = pltpu.make_async_copy(y.at[mine], recv.at[mine], here.at[0])
    own.start()
    greet()
    pl.semaphore_wait(pltpu.get_barrier_semaphore(), 22)

    def a2a(o):
        peer = plane_peer(o)
        return remote(
            y.at[4 * peer[0] + peer[1]], recv.at[mine], a2a_send.at[o], a2a_recv.at[o], peer
        )

    for o in FAR_FIRST:
        a2a(o).start()

    def place(source):
        out[pl.ds(pl.multiple_of(128 * source, 128), 128), :] = recv[source].T

    own.wait()
    place(mine)

    def receive(o, _):
        a2a(o).wait()
        place(plane_source(o))
        return 0

    lax.fori_loop(1, 16, receive, 0)

    def gram(c, acc):
        cells = jnp.concatenate([out[pl.ds(8 * c + i, 32, stride=64), :] for i in range(8)], axis=1)
        top = cells.astype(BF16)
        rest = (cells - top.astype(F32)).astype(BF16)
        both = jnp.concatenate([top, rest], axis=0)
        return acc + lax.dot_general(both, both, (((1,), (1,)), ((), ())), preferred_element_type=F32)

    acc = lax.fori_loop(0, 8, gram, jnp.zeros((64, 64), F32))
    g = acc[:32, :32] + (acc[:32, 32:] + acc[32:, :32])
    gram_a[mine] = jnp.concatenate([g[8 * b : 8 * b + 8] for b in range(4)], axis=1)

    def plane(o):
        return remote(gram_a.at[mine], gram_a.at[mine], a_send.at[o], a_recv.at[o], plane_peer(o))

    def line(o):
        return remote(gram_b.at[gz], gram_b.at[gz], b_send.at[o], b_recv.at[o], line_peer(o))

    def wait_plane(o, _):
        plane(o).wait()
        return 0

    def wait_line(o, _):
        line(o).wait()
        return 0

    for o in FAR_FIRST:
        plane(o).start()
    lax.fori_loop(1, 16, wait_plane, 0)
    acc = gram_a[0]
    for i in range(1, 16):
        acc = acc + gram_a[i]
    gram_b[gz] = acc
    for o in (4, 3, 5, 2, 6, 1, 7):
        line(o).start()
    lax.fori_loop(1, 8, wait_line, 0)
    acc = gram_b[0]
    for i in range(1, 8):
        acc = acc + gram_b[i]
    for b in range(4):
        total[pl.ds(8 * b, 8), :] = acc[:, 32 * b : 32 * b + 32]


def run_return(y):
    vmem = pl.BlockSpec(memory_space=pltpu.VMEM)
    dma = pltpu.SemaphoreType.DMA
    return pl.pallas_call(
        return_kernel,
        out_shape=(jax.ShapeDtypeStruct((2048, 128), F32), jax.ShapeDtypeStruct((32, 32), F32)),
        in_specs=[pl.BlockSpec(memory_space=pltpu.HBM)],
        out_specs=(vmem, vmem),
        scratch_shapes=[
            pltpu.VMEM((G, 128, 128), F32),
            pltpu.VMEM((G, 8, 128), F32),
            pltpu.VMEM((8, 8, 128), F32),
            dma((16,)), dma((16,)), dma((16,)), dma((16,)), dma((8,)), dma((8,)), dma((1,)),
        ],
        compiler_params=pltpu.CompilerParams(collective_id=2, has_side_effects=True),
        name="giveback",
    )(y)


def body(orbitals, potential, projectors, owner_rank, box_anchor, box_extent, coupling):
    perm = jnp.asarray(permutation()).astype(BF16)
    x, v, p, table = run_gather(
        orbitals.reshape(2048, 128), potential.reshape(64, 128), projectors, perm,
        owner_rank.reshape(8, 128), box_anchor, box_extent.reshape(8, 128),
    )
    w = jnp.asarray(weights()).astype(BF16)
    y = run_filter(
        table, coupling.T,
        x, v.reshape(G, 96, 128), p.reshape(1024, 16, 128), w,
    )
    filtered, total = run_return(y)
    return filtered.reshape(orbitals.shape), total * (1.0 / (32 * 32 * 1024))


def solution(mesh):
    return jax.shard_map(
        body,
        mesh=mesh,
        in_specs=(
            P(None, "gx", "gy", "gz"),
            P("gx", "gy", "gz"),
            P(("gx", "gy", "gz"), None, None),
            P(),
            P(),
            P(),
            P(),
        ),
        out_specs=(P(None, "gx", "gy", "gz"), P()),
        check_vma=False,
    )
```
